512 devices in a mesh: blk: 64 (over y, z_lo, core), col: 8 (over x, z_hi).
Axes of the slice: x: 4, y: 4, z: 16 (z_hi: 2, z_lo: 8; z = z_hi * 8 + z_lo), core: 2. Of those that a mesh axis runs over, the one named last changes fastest.
Arguments:
- node_feats: bfloat16 [256, 131072], P('col', 'blk'), may hold values from -6 to 6
- tile_dst: int32 [3584], P('blk'), may hold values from 0 to 15
- tile_src: int32 [3584], P('blk'), may hold values from 0 to 47, as said below
- tile_cnt: int32 [3584, 128, 128], P('blk'), may hold values from 0 to 3, as said below
- send_blk: int32 [64, 8, 4], P('blk'), may hold values from 0 to 15
- self_weight: bfloat16 [256, 256], replicated, may hold values from -0.375 to 0.375
- neigh_weight: bfloat16 [256, 256], replicated, may hold values from -0.75 to 0.75
- bias: float32 [256], replicated, may hold values from -4 to 4
- cotangent: bfloat16 [256, 131072], P('col', 'blk'), may hold values from -6 to 6
Outputs:
- grad_feats: bfloat16 [256, 131072], P('col', 'blk')
- grad_self: float32 [256, 256], P('col')
- grad_neigh: float32 [256, 256], P('col')
- grad_bias: float32 [256], P('col')
The draws below stay inside these ranges and needn't reach their ends.
Inputs may be any that keep to these rules, and one draw needn't show every extreme that they name: `tile_src`: of each device's 56 entries, the first 32 are 16 + a permutation of 0 to 32 - 1 (every received slot is read by one tile); the others are own blocks below 16. `tile_cnt`: edge counts; some rows of a tile are empty.
All inputs are finite; a program needn't handle non-finite values.
Results may differ from the reference program's by a relative error of at most 0.006.
Values may be sent and summed in bfloat16 or wider, within the bound.
No kernel may reach another device: no remote copies, remote signals or barrier semaphores. Data moves between devices by JAX's collectives and lax.ppermute only.
A program may use at most 64 MiB of HBM per device.

```python
import jax
import jax.numpy as jnp
from jax import lax

D = 256
BLK = 128
HOPS = 4
NB_DEV = 16
SCAP = 4
LOCAL_TILES = 24
SLOTS = 32
TILES = 56
NODES = 131072
N_BLK = 64


def draw_tile_dst(key, part):
    table = jax.random.randint(key, (N_BLK, TILES), 0, NB_DEV, dtype=jnp.int32)
    table = table.at[:, 0].set(NB_DEV - 1)
    table = table.at[:, 1].set(0)
    return table.reshape(N_BLK * TILES)


def draw_tile_src(key, part):
    perm_key, local_key = jax.random.split(jax.random.fold_in(key, 11))
    keys = jax.random.split(perm_key, N_BLK)
    orders = jax.vmap(lambda single: jax.random.permutation(single, SLOTS))(keys).astype(jnp.int32)
    local_part = jax.random.randint(local_key, (N_BLK, LOCAL_TILES), 0, NB_DEV, dtype=jnp.int32)
    local_part = local_part.at[:, 0].set(0)
    table = jnp.concatenate([orders + NB_DEV, local_part], axis=1)
    return table.reshape(N_BLK * TILES)


def draw_tile_cnt(key, part):
    row_key, entry_key, value_key = jax.random.split(jax.random.fold_in(key, 23), 3)
    total = N_BLK * TILES
    active = jax.random.randint(row_key, (total, BLK, 1), 0, 2, dtype=jnp.int32)
    present = (jax.random.randint(entry_key, (total, BLK, BLK), 0, 16, dtype=jnp.int32) == 0).astype(jnp.int32)
    values = jax.random.randint(value_key, (total, BLK, BLK), 1, 4, dtype=jnp.int32)
    counts = active * present * values
    return counts.at[0, 0, 0].set(3)


def place_ends(values, stream_key, low, high):
    longest = values.shape.index(max(values.shape))
    spots = []
    for shift in (0, 1):
        where = [jax.random.randint(jax.random.fold_in(stream_key, axis), (), 0, length) for axis, length in enumerate(values.shape)]
        where[longest] = (where[longest] + shift) % values.shape[longest]
        spots.append(tuple(where))
    return values.at[spots[0]].set(low).at[spots[1]].set(high)


def steps_of(stream_key, dims, cuts, smallest, high):
    level, own = 1.0, jax.random.fold_in(stream_key, 6)
    for axis_at, parts in cuts:
        draws = jnp.exp(jax.random.uniform(jax.random.fold_in(own, axis_at), (parts,), jnp.float32, smallest / len(cuts), high / len(cuts)))
        level = level * jnp.repeat(draws, dims[axis_at] // parts).reshape([-1 if axis == axis_at else 1 for axis in range(len(dims))])
    return level


def scatter_about(key, shape, spread, bound, shards=(), kind=jnp.bfloat16):
    result = jax.random.normal(key, shape, jnp.float32) * spread
    if len(shards) > 0:
        result = steps_of(key, shape, shards, -0.22, 0.18) * result
    return jnp.clip(result, min=-bound, max=bound).astype(kind)


def setup_inputs(seed: int = 0) -> dict:
    arg_keys = jax.random.split(jax.random.key(seed), 10)
    return {
        "node_feats": scatter_about(arg_keys[0], (D, NODES), 1.0, 6.0, ((0, 8), (1, 64))),
        "tile_dst": draw_tile_dst(jax.random.fold_in(arg_keys[9], 71), 0),
        "tile_src": draw_tile_src(jax.random.fold_in(arg_keys[9], 71), 0),
        "tile_cnt": draw_tile_cnt(jax.random.fold_in(arg_keys[9], 71), 0),
        "send_blk": place_ends(jax.random.randint(arg_keys[4], (N_BLK, 2 * HOPS, SCAP), 0, NB_DEV), jax.random.fold_in(arg_keys[4], 1), 0, NB_DEV - 1).astype(jnp.int32),
        "self_weight": scatter_about(arg_keys[5], (D, D), D ** -0.5, 0.375),
        "neigh_weight": scatter_about(arg_keys[6], (D, D), (D // 4) ** -0.5, 0.75),
        "bias": scatter_about(arg_keys[7], (D,), 0.7, 4.0, (), jnp.float32),
        "cotangent": scatter_about(arg_keys[8], (D, NODES), 1.0, 6.0, ((0, 8), (1, 64))),
    }


def gelu_slope(pre_act):
    inner = 0.7978845608 * (pre_act + 0.044715 * pre_act * pre_act * pre_act)
    tanh_value = jnp.tanh(inner)
    return 0.5 * (1.0 + tanh_value) + 0.5 * pre_act * (1.0 - tanh_value * tanh_value) * 0.7978845608 * (1.0 + 3.0 * 0.044715 * pre_act * pre_act)


def reference(node_feats, tile_dst, tile_src, tile_cnt, send_blk, self_weight, neigh_weight, bias, cotangent):
    width = node_feats.shape[0]
    all_blocks = N_BLK * NB_DEV
    highest = lax.Precision.HIGHEST
    feat_blocks = node_feats.astype(jnp.float32).reshape(width, all_blocks, BLK)
    dest_table = tile_dst.reshape(N_BLK, TILES)
    source_table = tile_src.reshape(N_BLK, TILES)
    counts = tile_cnt.reshape(N_BLK, TILES, BLK, BLK)
    device_ids = jnp.arange(N_BLK, dtype=jnp.int32)[:, None]
    is_local = source_table < NB_DEV
    remote_index = jnp.maximum(source_table - NB_DEV, 0)
    offset_index = remote_index // SCAP
    slot_index = remote_index % SCAP
    distance = (offset_index // 2 + 1) * (1 - 2 * (offset_index % 2))
    sender = (device_ids - distance) % N_BLK
    sent_block = send_blk[sender, offset_index, slot_index]
    global_src = jnp.where(is_local, device_ids * NB_DEV + source_table, sender * NB_DEV + sent_block).astype(jnp.int32)
    dest_onehot = (dest_table[:, :, None] == jnp.arange(NB_DEV, dtype=jnp.int32)[None, None, :]).astype(jnp.float32)

    def forward_one(inputs):
        sources, tile_counts, onehot = inputs
        picked = feat_blocks[:, sources]
        count_float = tile_counts.astype(jnp.float32)
        products = jnp.einsum("ctj,tij->cti", picked, count_float, precision=highest)
        summed = jnp.einsum("cti,tb->cbi", products, onehot, precision=highest)
        degree_part = jnp.einsum("ti,tb->bi", jnp.sum(tile_counts, axis=2).astype(jnp.float32), onehot, precision=highest)
        return summed, degree_part

    agg_raw, degree = lax.map(forward_one, (global_src, counts, dest_onehot))
    agg_raw = agg_raw.transpose(1, 0, 2, 3).reshape(width, NODES)
    floor_degree = jnp.maximum(degree.reshape(NODES), 1.0)
    aggregate = (agg_raw / floor_degree[None, :]).astype(jnp.bfloat16)
    pre_act = (jnp.dot(self_weight.T, node_feats, preferred_element_type=jnp.float32)
               + jnp.dot(neigh_weight.T, aggregate, preferred_element_type=jnp.float32)
               + bias[:, None])
    grad_pre = (cotangent.astype(jnp.float32) * gelu_slope(pre_act)).astype(jnp.bfloat16)
    grad_self = jnp.dot(node_feats, grad_pre.T, preferred_element_type=jnp.float32)
    grad_neigh = jnp.dot(aggregate, grad_pre.T, preferred_element_type=jnp.float32)
    grad_bias = jnp.sum(grad_pre.astype(jnp.float32), axis=1)
    scaled = (jnp.dot(neigh_weight, grad_pre, preferred_element_type=jnp.float32) / floor_degree[None, :]).astype(jnp.bfloat16)
    scaled_blocks = scaled.astype(jnp.float32).reshape(width, N_BLK, NB_DEV, BLK).transpose(1, 0, 2, 3)

    def backward_one(total, inputs):
        sources, tile_counts, onehot, part = inputs
        picked = jnp.einsum("cbi,tb->cti", part, onehot, precision=highest)
        contrib = jnp.einsum("cti,tij->ctj", picked, tile_counts.astype(jnp.float32), precision=highest)
        return total.at[:, sources].add(contrib), None

    back_sum, leftover = lax.scan(backward_one, jnp.zeros((width, all_blocks, BLK), jnp.float32),
                                  (global_src, counts, dest_onehot, scaled_blocks))
    grad_feats = (jnp.dot(self_weight, grad_pre, preferred_element_type=jnp.float32)
                  + back_sum.reshape(width, NODES)).astype(jnp.bfloat16)
    return grad_feats, grad_self, grad_neigh, grad_bias
```

```python
import jax
import jax.numpy as jnp
from jax import lax
from jax.sharding import PartitionSpec as P

GROUP = 8


def gelu_slope(pre_act):
    inner = 0.7978845608 * (pre_act + 0.044715 * pre_act * pre_act * pre_act)
    tanh_value = jnp.tanh(inner)
    return 0.5 * (1.0 + tanh_value) + 0.5 * pre_act * (
        1.0 - tanh_value * tanh_value
    ) * 0.7978845608 * (1.0 + 3.0 * 0.044715 * pre_act * pre_act)


def halo_groups(devices, shift):
    return [
        [(first + shift + i) % devices for i in range(GROUP)]
        for first in range(0, devices, GROUP)
    ]


def offset_to_index(distance):
    k = 2 * (jnp.abs(distance) - 1) + (distance < 0).astype(jnp.int32)
    return jnp.clip(k, 0, 7)


def swap(rows, shift):
    devices = lax.axis_size("blk")
    return lax.all_to_all(
        rows, "blk", 0, 0, axis_index_groups=halo_groups(devices, shift), tiled=False
    )


def per_device(
    node_feats, tile_dst, tile_src, tile_cnt, send_blk, self_weight, neigh_weight, bias, cotangent
):
    highest = lax.Precision.HIGHEST
    dim, nodes = node_feats.shape
    width = tile_cnt.shape[1]
    blocks = nodes // width
    slot_cap = send_blk.shape[2]
    slots = send_blk.shape[1] * slot_cap
    cols = lax.axis_size("col")
    per_col = blocks // cols
    full = cols * dim
    bf16 = jnp.bfloat16

    def by_block(value):
        return value.reshape(dim, blocks, width).transpose(1, 0, 2)

    def to_full(value):
        return value.transpose(0, 2, 1, 3).reshape(full, per_col * width)

    def from_full(value):
        return value.reshape(cols, dim, per_col, width).transpose(0, 2, 1, 3)

    col = lax.axis_index("col")
    blk = lax.axis_index("blk")
    peers = jnp.arange(GROUP, dtype=jnp.int32)
    place_a = blk % GROUP
    place_b = (blk + GROUP // 2) % GROUP
    out_a = offset_to_index(peers - place_a)
    out_b = offset_to_index(peers - place_b)
    back_a = offset_to_index(place_a - peers)
    back_b = offset_to_index(place_b - peers)
    kinds = jnp.arange(2 * (GROUP // 2), dtype=jnp.int32)
    distance = (kinds // 2 + 1) * (1 - 2 * (kinds % 2))
    from_a = place_a - distance
    in_a = (from_a >= 0) & (from_a < GROUP)
    came_row = jnp.where(in_a, from_a, GROUP + jnp.clip(place_b - distance, 0, GROUP - 1))
    ahead_a = place_a + distance
    ahead_in_a = (ahead_a >= 0) & (ahead_a < GROUP)
    ret_row = jnp.where(ahead_in_a, ahead_a, GROUP + jnp.clip(place_b + distance, 0, GROUP - 1))

    table = send_blk[0]
    feats = by_block(node_feats)
    send_a = jnp.take(feats, table[out_a].reshape(-1), axis=0)
    send_b = jnp.take(feats, table[out_b].reshape(-1), axis=0)
    shape = (GROUP, slot_cap, dim, width)
    got_b = swap(send_b.reshape(shape), GROUP // 2)
    got_a = swap(send_a.reshape(shape), 0)
    sources = jnp.concatenate(
        [
            feats,
            got_a.reshape(GROUP * slot_cap, dim, width),
            got_b.reshape(GROUP * slot_cap, dim, width),
        ],
        axis=0,
    )
    slot = jnp.maximum(tile_src - blocks, 0)
    remote = blocks + came_row[slot // slot_cap] * slot_cap + slot % slot_cap
    source = jnp.where(tile_src < blocks, tile_src, remote)
    counts = tile_cnt.astype(bf16)
    picked = jnp.take(sources, source, axis=0)
    products = jnp.einsum("tcj,tij->tci", picked, counts, preferred_element_type=jnp.float32)
    dest = (tile_dst[:, None] == jnp.arange(blocks, dtype=jnp.int32)[None, :]).astype(jnp.float32)
    agg_raw = jnp.einsum("tci,tb->bci", products, dest, precision=highest)
    degree = jnp.einsum(
        "ti,tb->bi", jnp.sum(tile_cnt, axis=2).astype(jnp.float32), dest, precision=highest
    )
    floor_degree = jnp.maximum(degree, 1.0)
    aggregate = (agg_raw / floor_degree[:, None, :]).astype(bf16)

    def split(value):
        return value.reshape(cols, 1, per_col, dim, width)

    mixed = jnp.concatenate([split(feats), split(aggregate), split(by_block(cotangent))], axis=1)
    mixed = lax.all_to_all(mixed, "col", 0, 0, tiled=False)
    x_full = to_full(mixed[:, 0])
    agg_full = to_full(mixed[:, 1])
    cot_full = to_full(mixed[:, 2])
    first = (((0,), (0,)), ((), ()))
    last = (((1,), (1,)), ((), ()))
    pre_act = (
        lax.dot_general(self_weight, x_full, first, preferred_element_type=jnp.float32)
        + lax.dot_general(neigh_weight, agg_full, first, preferred_element_type=jnp.float32)
        + bias[:, None]
    )
    dz = (cot_full.astype(jnp.float32) * gelu_slope(pre_act)).astype(bf16)
    my_degree = lax.dynamic_slice_in_dim(floor_degree, col * per_col, per_col, 0).reshape(1, -1)
    scaled = (jnp.dot(neigh_weight, dz, preferred_element_type=jnp.float32) / my_degree).astype(bf16)
    own = jnp.dot(self_weight, dz, preferred_element_type=jnp.float32).astype(bf16)
    home = jnp.concatenate([from_full(scaled)[:, None], from_full(own)[:, None]], axis=1)
    home = lax.all_to_all(home, "col", 0, 0, tiled=False)

    weight_part = jnp.concatenate(
        [
            lax.dot_general(x_full, dz, last, preferred_element_type=jnp.float32).reshape(cols, dim, full),
            lax.dot_general(agg_full, dz, last, preferred_element_type=jnp.float32).reshape(cols, dim, full),
            jnp.broadcast_to(
                jnp.sum(dz.astype(jnp.float32), axis=1)[None, None, :], (cols, 16, full)
            ),
        ],
        axis=1,
    ).astype(bf16)
    weight = jnp.sum(
        lax.all_to_all(weight_part, "col", 0, 0, tiled=False).astype(jnp.float32), axis=0
    )

    def total(value, groups):
        count = len(groups[0])
        copies = jnp.broadcast_to(value.astype(bf16)[None], (count,) + value.shape)
        return jnp.sum(
            lax.all_to_all(
                copies, "blk", 0, 0, axis_index_groups=groups, tiled=False
            ).astype(jnp.float32),
            axis=0,
        )

    devices = lax.axis_size("blk")
    spread = [[16 * y + 2 * z + c for y in range(devices // 16) for c in range(2)] for z in range(8)]
    along = [[16 * y + 2 * z + c for z in range(8)] for y in range(devices // 16) for c in range(2)]
    weight = total(total(weight, spread), along)
    grad_self = weight[:dim]
    grad_neigh = weight[dim : 2 * dim]
    grad_bias = lax.dynamic_slice_in_dim(weight[2 * dim], col * dim, dim, 0)

    scaled_blocks = home[:, 0].reshape(blocks, dim, width)
    own_blocks = home[:, 1].reshape(blocks, dim, width)
    scaled_tiles = jnp.take(scaled_blocks, tile_dst, axis=0)
    contrib = jnp.einsum("tci,tij->tcj", scaled_tiles, counts, preferred_element_type=jnp.float32)
    tile_of_slot = jnp.argmax(
        tile_src[None, :slots] == blocks + jnp.arange(slots, dtype=jnp.int32)[:, None], axis=1
    ).astype(jnp.int32).reshape(-1, slot_cap)
    away = contrib[:slots].astype(bf16)
    ret_b = swap(jnp.take(away, tile_of_slot[back_b].reshape(-1), axis=0).reshape(shape), GROUP // 2)
    ret_a = swap(jnp.take(away, tile_of_slot[back_a].reshape(-1), axis=0).reshape(shape), 0)
    returned = jnp.concatenate([ret_a, ret_b], axis=0)[ret_row].reshape(slots, dim, width)
    local = (
        tile_src[slots:, None] == jnp.arange(blocks, dtype=jnp.int32)[None, :]
    ).astype(jnp.float32)
    back_local = jnp.einsum("tcj,ts->scj", contrib[slots:], local, precision=highest)
    sent = (
        table.reshape(-1)[:, None] == jnp.arange(blocks, dtype=jnp.int32)[None, :]
    ).astype(bf16)
    back_remote = jnp.einsum("tcj,ts->scj", returned, sent, preferred_element_type=jnp.float32)
    grad_feats = (own_blocks.astype(jnp.float32) + back_local + back_remote).astype(bf16)
    grad_feats = grad_feats.transpose(1, 0, 2).reshape(dim, nodes)
    return grad_feats, grad_self, grad_neigh, grad_bias


def solution(mesh):
    placed = (
        P("col", "blk"),
        P("blk"),
        P("blk"),
        P("blk", None, None),
        P("blk", None, None),
        P(),
        P(),
        P(),
        P("col", "blk"),
    )
    return jax.shard_map(
        per_device,
        mesh=mesh,
        in_specs=placed,
        out_specs=(P("col", "blk"), P("col", None), P("col", None), P("col")),
        check_vma=False,
    )
```

```python
import functools

import jax
import jax.numpy as jnp
from jax import lax
from jax.experimental import pallas as pl
from jax.experimental.pallas import tpu as pltpu
from jax.sharding import PartitionSpec as P

GROUP = 8
Y, Z_LO, CORE, X, Z_HI = 4, 8, 2, 4, 2
BF16 = jnp.bfloat16
F32 = jnp.float32
FIRST = (((0,), (0,)), ((), ()))
LAST = (((1,), (1,)), ((), ()))
VMEM = pl.BlockSpec(memory_space=pltpu.VMEM)
SMEM = pl.BlockSpec(memory_space=pltpu.SMEM)


def gelu_slope(pre_act):
    inner = 0.7978845608 * (pre_act + 0.044715 * pre_act * pre_act * pre_act)
    tanh_value = jnp.tanh(inner)
    return 0.5 * (1.0 + tanh_value) + 0.5 * pre_act * (
        1.0 - tanh_value * tanh_value
    ) * 0.7978845608 * (1.0 + 3.0 * 0.044715 * pre_act * pre_act)


def dot(left, right, dims=(((1,), (0,)), ((), ()))):
    return lax.dot_general(left, right, dims, preferred_element_type=F32)


def call(body, out_shape, in_specs, scratch=(), cost=(1e7, 1e6)):
    outs = jax.tree.map(lambda _: VMEM, out_shape)
    return pl.pallas_call(
        body,
        out_shape=out_shape,
        in_specs=in_specs,
        out_specs=outs,
        scratch_shapes=scratch,
        compiler_params=pltpu.CompilerParams(vmem_limit_bytes=32 * 2**20),
        cost_estimate=pl.CostEstimate(
            flops=int(cost[0]), bytes_accessed=int(cost[1]), transcendentals=0
        ),
    )


def places():
    blk = lax.axis_index("blk")
    return lax.rem(blk, GROUP), lax.rem(blk + GROUP // 2, GROUP)


def kind_of(distance):
    k = 2 * (jnp.abs(distance) - 1) + jnp.where(distance < 0, 1, 0)
    return jnp.clip(k, 0, 7)


def offset_of(kind):
    return (kind // 2 + 1) * (1 - 2 * lax.rem(kind, 2))


def inside(place):
    return jnp.logical_and(place >= 0, place < GROUP)


def bounded(place):
    return jnp.clip(place, 0, GROUP - 1)


def pack_kernel(width, x_ref, cot_ref, send_ref, a_ref, b_ref, xc_ref):
    place_a, place_b = places()
    cap = send_ref.shape[1]
    for ref, place in ((b_ref, place_b), (a_ref, place_a)):
        for peer in range(GROUP):
            kind = kind_of(peer - place)
            for m in range(cap):
                start = pl.multiple_of(send_ref[kind, m] * width, width)
                ref[peer, m] = x_ref[:, pl.ds(start, width)]
    for block in range(x_ref.shape[1] // width):
        cols = slice(block * width, (block + 1) * width)
        xc_ref[block // 2, 0, block % 2] = x_ref[:, cols]
        xc_ref[block // 2, 1, block % 2] = cot_ref[:, cols]


def local_kernel(slots, chunk, x_ref, dst_ref, src_ref, cnt_ref, half_ref, acc_ref):
    step = pl.program_id(0)
    width = cnt_ref.shape[1]
    dim = x_ref.shape[0]
    half_ref[...] = cnt_ref[...].astype(F32).astype(BF16)

    @pl.when(step == 0)
    def _():
        acc_ref[...] = jnp.zeros_like(acc_ref)

    @pl.when(step * chunk >= slots)
    def _():
        ones = jnp.ones((16, width), BF16)
        for i in range(chunk):
            tile = step * chunk + i
            start = pl.multiple_of(src_ref[tile] * width, width)
            rows = jnp.concatenate([x_ref[:, pl.ds(start, width)], ones], axis=0)
            dst = dst_ref[tile]
            acc_ref[dst] += dot(rows, half_ref[i], LAST)[: dim + 8]


def aggregate_kernel(slots, a_ref, b_ref, dst_ref, src_ref, half_ref, acc_in, agg_ref, deg_ref, acc_ref):
    place_a, place_b = places()
    cap, dim, width = a_ref.shape[1:]
    blocks = acc_in.shape[0]
    ones = jnp.ones((16, width), BF16)
    acc_ref[...] = acc_in[...]
    for tile in range(slots):
        slot = src_ref[tile] - blocks
        kind = slot // cap
        m = lax.rem(slot, cap)
        row_a = place_a - offset_of(kind)
        row_b = place_b - offset_of(kind)
        got = jnp.where(inside(row_a), a_ref[bounded(row_a), m], b_ref[bounded(row_b), m])
        rows = jnp.concatenate([got, ones], axis=0)
        dst = dst_ref[tile]
        acc_ref[dst] += dot(rows, half_ref[tile], LAST)[: dim + 8]
    for block in range(blocks):
        degree = jnp.maximum(acc_ref[block, dim : dim + 8], 1.0)
        deg_ref[block] = degree
        agg_ref[block // 2, block % 2] = (acc_ref[block, :dim] / degree[:1]).astype(BF16)


def node_kernel(
    xc_ref, agg_ref, deg_ref, wt_ref, neigh_ref, own_w_ref, bias_ref, home_ref, dz_ref, xa_ref
):
    cols, _, per_col, dim, width = xc_ref.shape
    full = cols * dim
    col = lax.axis_index("col")
    for p in range(per_col):
        lanes = slice(p * width, (p + 1) * width)
        x = xc_ref[:, 0, p].reshape(full, width)
        cot = xc_ref[:, 1, p].reshape(full, width)
        xa = jnp.concatenate([x, agg_ref[:, p].reshape(full, width)], axis=0)
        xa_ref[:, lanes] = xa
        pre = dot(wt_ref[...], xa) + bias_ref[...]
        dz = (cot.astype(F32) * gelu_slope(pre)).astype(BF16)
        dz_ref[:, lanes] = dz
        degree = deg_ref[col * per_col + p][:1]
        scaled = (dot(neigh_ref[...], dz) / degree).astype(BF16)
        home_ref[:, 0, p] = scaled.reshape(cols, dim, width)
        own = dot(own_w_ref[...], dz).astype(BF16)
        home_ref[:, 1, p] = own.reshape(cols, dim, width)


def weight_kernel(dim, xa_ref, dz_ref, part_ref):
    full = dz_ref.shape[0]
    grads = dot(xa_ref[...], dz_ref[...], LAST)
    total = dot(jnp.ones((16, dz_ref.shape[1]), BF16), dz_ref[...], LAST)
    tail = jnp.concatenate([total[:8, :128], total[8:, 128:]], axis=0).astype(BF16)
    for which in range(2):
        for quarter in range(4):
            for x in range(X):
                rows = [
                    grads[start : start + 8]
                    for z in range(Z_HI)
                    for start in [which * full + (x * Z_HI + z) * dim + quarter * 8]
                ]
                piece = (which * 4 + quarter) * X + x
                part_ref[piece, :, :full] = jnp.concatenate(rows, axis=0).astype(BF16)
                part_ref[piece, :, full:] = tail


def contribution_kernel(slots, home_ref, dst_ref, src_ref, half_ref, a_ref, b_ref, hold_ref):
    place_a, place_b = places()
    blocks = home_ref.shape[0] * home_ref.shape[2]
    cap = a_ref.shape[1]
    for tile in range(slots):
        dst = dst_ref[tile]
        value = dot(home_ref[dst // 2, 0, lax.rem(dst, 2)], half_ref[tile])
        hold_ref[src_ref[tile] - blocks] = value.astype(BF16)
    for ref, place in ((b_ref, place_b), (a_ref, place_a)):
        for peer in range(GROUP):
            kind = kind_of(place - peer)
            for m in range(cap):
                ref[peer, m] = hold_ref[kind * cap + m]


def local_back_kernel(slots, home_ref, dst_ref, src_ref, half_ref, acc_ref):
    per = home_ref.shape[2]
    for block in range(acc_ref.shape[0]):
        acc_ref[block] = home_ref[block // per, 1, block % per].astype(F32)
    for tile in range(slots, half_ref.shape[0]):
        dst = dst_ref[tile]
        src = src_ref[tile]
        acc_ref[src] += dot(home_ref[dst // 2, 0, lax.rem(dst, 2)], half_ref[tile])


def finish_kernel(acc_in, a_ref, b_ref, send_ref, out_ref, acc_ref):
    place_a, place_b = places()
    kinds, cap = send_ref.shape
    width = acc_in.shape[2]
    acc_ref[...] = acc_in[...]
    for kind in range(kinds):
        offset = (kind // 2 + 1) * (1 - 2 * (kind % 2))
        row_a = place_a + offset
        row_b = place_b + offset
        for m in range(cap):
            got = jnp.where(inside(row_a), a_ref[bounded(row_a), m], b_ref[bounded(row_b), m])
            acc_ref[send_ref[kind, m]] += got.astype(F32)
    for block in range(acc_ref.shape[0]):
        out_ref[:, block * width : (block + 1) * width] = acc_ref[block].astype(BF16)


def rank(y, z_lo, core, x, z_hi):
    return ((y * Z_LO + z_lo) * CORE + core) * X * Z_HI + x * Z_HI + z_hi


def swap(rows, shift):
    devices = lax.axis_size("blk")
    groups = [
        [(first + shift + i) % devices for i in range(GROUP)] for first in range(0, devices, GROUP)
    ]
    return lax.all_to_all(rows, "blk", 0, 0, axis_index_groups=groups, tiled=False)


def over_col(rows):
    return lax.all_to_all(rows, "col", 0, 0, tiled=False)


def per_device(
    node_feats, tile_dst, tile_src, tile_cnt, send_blk, self_weight, neigh_weight, bias, cotangent
):
    dim, nodes = node_feats.shape
    tiles, width = tile_cnt.shape[:2]
    blocks = nodes // width
    table = send_blk[0]
    kinds, cap = table.shape
    slots = kinds * cap
    cols = X * Z_HI
    per_col = blocks // cols
    full = cols * dim
    chunk = 8
    halo = jax.ShapeDtypeStruct((GROUP, cap, dim, width), BF16)
    pairs = jax.ShapeDtypeStruct((cols, 2, per_col, dim, width), BF16)
    ranged = jax.ShapeDtypeStruct((cols, per_col, dim, width), BF16)

    send_a, send_b, xc = call(
        functools.partial(pack_kernel, width),
        (halo, halo, pairs),
        [VMEM, VMEM, SMEM],
    )(node_feats, cotangent, table)
    got_b = swap(send_b, GROUP // 2)
    got_a = swap(send_a, 0)
    xc, got_a = lax.optimization_barrier((xc, got_a))
    xc = over_col(xc)
    whole = lambda shape: pl.BlockSpec(shape, lambda i: (0,) * len(shape))
    half, acc = pl.pallas_call(
        functools.partial(local_kernel, slots, chunk),
        grid=(tiles // chunk,),
        out_shape=(
            jax.ShapeDtypeStruct(tile_cnt.shape, BF16),
            jax.ShapeDtypeStruct((blocks, dim + 8, width), F32),
        ),
        in_specs=[
            whole((dim, nodes)),
            SMEM,
            SMEM,
            pl.BlockSpec((chunk, width, width), lambda i: (i, 0, 0)),
        ],
        out_specs=(
            pl.BlockSpec((chunk, width, width), lambda i: (i, 0, 0)),
            whole((blocks, dim + 8, width)),
        ),
        compiler_params=pltpu.CompilerParams(vmem_limit_bytes=32 * 2**20),
        cost_estimate=pl.CostEstimate(
            flops=60000000, bytes_accessed=6000000, transcendentals=0
        ),
    )(node_feats, tile_dst, tile_src, tile_cnt)
    weight_t = jnp.concatenate([self_weight.T, neigh_weight.T], axis=1)
    bias_col = bias[:, None]
    agg, degree = call(
        functools.partial(aggregate_kernel, slots),
        (ranged, jax.ShapeDtypeStruct((blocks, 8, width), F32)),
        [VMEM, VMEM, SMEM, SMEM, VMEM, VMEM],
        [pltpu.VMEM((blocks, dim + 8, width), F32)],
    )(got_a, got_b, tile_dst, tile_src, half, acc)
    agg, xc = lax.optimization_barrier((agg, xc))
    agg = over_col(agg)
    home, dz, xa = call(
        node_kernel,
        (
            pairs,
            jax.ShapeDtypeStruct((full, per_col * width), BF16),
            jax.ShapeDtypeStruct((2 * full, per_col * width), BF16),
        ),
        [VMEM] * 7,
    )(xc, agg, degree, weight_t, neigh_weight, self_weight, bias_col)
    home = over_col(home)
    part = call(
        functools.partial(weight_kernel, dim),
        jax.ShapeDtypeStruct((Y * CORE * X, 16, full + 128), BF16),
        [VMEM] * 2,
    )(xa, dz)
    part, home = lax.optimization_barrier((part, home))

    both = ("blk", "col")
    flat = [
        [rank(y, l, c, x, h) for y in range(Y) for c in range(CORE) for x in range(X)]
        for l in range(Z_LO)
        for h in range(Z_HI)
    ]
    line = [
        [rank(y, l, c, x, h) for h in range(Z_HI) for l in range(Z_LO)]
        for y in range(Y)
        for c in range(CORE)
        for x in range(X)
    ]
    plane = [[(y * Z_LO + l) * CORE + c for y in range(Y) for c in range(CORE)] for l in range(Z_LO)]
    part = lax.all_to_all(part, both, 0, 0, axis_index_groups=flat, tiled=False)
    away_a, away_b = call(
        functools.partial(contribution_kernel, slots),
        (halo, halo),
        [VMEM, SMEM, SMEM, VMEM],
        [pltpu.VMEM((slots, dim, width), BF16)],
    )(home, tile_dst, tile_src, half)
    away_b, part = lax.optimization_barrier((away_b, part))
    back_b = swap(away_b, GROUP // 2)
    away_a, back_b = lax.optimization_barrier((away_a, back_b))
    back_a = swap(away_a, 0)
    part = jnp.sum(part.astype(F32), axis=0)
    tail = jnp.concatenate([part[0:4, full:], part[8:12, full:]], axis=0)
    ends = [jnp.concatenate([part[8 * h : 8 * h + 8, :full], tail], axis=1) for h in range(Z_HI)]
    part = jnp.broadcast_to(jnp.stack(ends)[:, None], (Z_HI, Z_LO, 8, full + 128))
    part = part.reshape(Z_HI * Z_LO, 8, full + 128)
    part, back_a = lax.optimization_barrier((part, back_a))
    part = jnp.sum(lax.all_to_all(part, both, 0, 0, axis_index_groups=line, tiled=False), axis=0)
    grad_bias = jnp.concatenate([part[0, full:], part[4, full:]])
    grad_bias = lax.dynamic_slice_in_dim(grad_bias, lax.axis_index("col") * dim, dim, 0)
    part = jnp.broadcast_to(part[None, :, :full], (Y * CORE, 8, full))
    part = lax.all_to_all(part, "blk", 0, 0, axis_index_groups=plane, tiled=False)
    part = part.reshape(2, dim, full)
    grad_self, grad_neigh = part[0], part[1]

    acc = call(
        functools.partial(local_back_kernel, slots),
        jax.ShapeDtypeStruct((blocks, dim, width), F32),
        [VMEM, SMEM, SMEM, VMEM],
    )(home, tile_dst, tile_src, half)
    grad_feats = call(
        finish_kernel,
        jax.ShapeDtypeStruct((dim, nodes), BF16),
        [VMEM, VMEM, VMEM, SMEM],
        [pltpu.VMEM((blocks, dim, width), F32)],
    )(acc, back_a, back_b, table)
    return grad_feats, grad_self, grad_neigh, grad_bias


def solution(mesh):
    placed = (
        P("col", "blk"),
        P("blk"),
        P("blk"),
        P("blk", None, None),
        P("blk", None, None),
        P(),
        P(),
        P(),
        P("col", "blk"),
    )
    return jax.shard_map(
        per_device,
        mesh=mesh,
        in_specs=placed,
        out_specs=(P("col", "blk"), P("col", None), P("col", None), P("col")),
        check_vma=False,
    )
```

```python
import functools

import jax
import jax.numpy as jnp
from jax import lax
from jax.experimental import pallas as pl
from jax.experimental.pallas import tpu as pltpu
from jax.sharding import PartitionSpec as P

GROUP = 8
Y, Z_LO, CORE, X, Z_HI = 4, 8, 2, 4, 2
BF16 = jnp.bfloat16
F32 = jnp.float32
FIRST = (((0,), (0,)), ((), ()))
LAST = (((1,), (1,)), ((), ()))
VMEM = pl.BlockSpec(memory_space=pltpu.VMEM)
SMEM = pl.BlockSpec(memory_space=pltpu.SMEM)


def gelu_slope(pre_act):
    inner = 0.7978845608 * (pre_act + 0.044715 * pre_act * pre_act * pre_act)
    tanh_value = jnp.tanh(inner)
    return 0.5 * (1.0 + tanh_value) + 0.5 * pre_act * (
        1.0 - tanh_value * tanh_value
    ) * 0.7978845608 * (1.0 + 3.0 * 0.044715 * pre_act * pre_act)


def dot(left, right, dims=(((1,), (0,)), ((), ()))):
    return lax.dot_general(left, right, dims, preferred_element_type=F32)


def call(body, out_shape, in_specs, scratch=(), cost=(1e7, 1e6)):
    outs = jax.tree.map(lambda _: VMEM, out_shape)
    return pl.pallas_call(
        body,
        out_shape=out_shape,
        in_specs=in_specs,
        out_specs=outs,
        scratch_shapes=scratch,
        compiler_params=pltpu.CompilerParams(vmem_limit_bytes=32 * 2**20),
        cost_estimate=pl.CostEstimate(
            flops=int(cost[0]), bytes_accessed=int(cost[1]), transcendentals=0
        ),
    )


def places():
    blk = lax.axis_index("blk")
    return lax.rem(blk, GROUP), lax.rem(blk + GROUP // 2, GROUP)


def kind_of(distance):
    k = 2 * (jnp.abs(distance) - 1) + jnp.where(distance < 0, 1, 0)
    return jnp.clip(k, 0, 7)


def offset_of(kind):
    return (kind // 2 + 1) * (1 - 2 * lax.rem(kind, 2))


def inside(place):
    return jnp.logical_and(place >= 0, place < GROUP)


def bounded(place):
    return jnp.clip(place, 0, GROUP - 1)


def pack_kernel(width, x_ref, send_ref, a_ref, b_ref):
    place_a, place_b = places()
    cap = send_ref.shape[1]
    for ref, place in ((b_ref, place_b), (a_ref, place_a)):
        for peer in range(GROUP):
            kind = kind_of(peer - place)
            for m in range(cap):
                start = pl.multiple_of(send_ref[kind, m] * width, width)
                ref[peer, m] = x_ref[:, pl.ds(start, width)]


def column():
    col = lax.axis_index("col")
    return col // Z_HI, lax.rem(col, Z_HI)


def split_kernel(width, x_ref, cot_ref, keep_ref, away_ref):
    z_hi = column()[1]
    per = keep_ref.shape[2]
    for x in range(X):
        for out, z in ((keep_ref, z_hi), (away_ref, 1 - z_hi)):
            for p in range(per):
                start = pl.multiple_of(((x * Z_HI + z) * per + p) * width, width)
                out[x, 0, p] = x_ref[:, pl.ds(start, width)]
                out[x, 1, p] = cot_ref[:, pl.ds(start, width)]


def relay_kernel(keep_ref, got_ref, *outs):
    x = column()[0]
    for step, out in enumerate(outs, start=1):
        to = lax.rem(x + step, X)
        out[0] = keep_ref[to]
        out[1] = got_ref[to]


def local_kernel(slots, chunk, x_ref, dst_ref, src_ref, cnt_ref, half_ref, acc_ref):
    step = pl.program_id(0)
    width = cnt_ref.shape[1]
    dim = x_ref.shape[0]
    half_ref[...] = cnt_ref[...].astype(F32).astype(BF16)

    @pl.when(step == 0)
    def _():
        acc_ref[...] = jnp.zeros_like(acc_ref)

    @pl.when(step * chunk >= slots)
    def _():
        ones = jnp.ones((16, width), BF16)
        for i in range(chunk):
            tile = step * chunk + i
            start = pl.multiple_of(src_ref[tile] * width, width)
            rows = jnp.concatenate([x_ref[:, pl.ds(start, width)], ones], axis=0)
            dst = dst_ref[tile]
            acc_ref[dst] += dot(rows, half_ref[i], LAST)[: dim + 8]


def aggregate_kernel(slots, a_ref, b_ref, dst_ref, src_ref, half_ref, acc_in, agg_ref, deg_ref, acc_ref):
    place_a, place_b = places()
    cap, dim, width = a_ref.shape[1:]
    blocks = acc_in.shape[0]
    ones = jnp.ones((16, width), BF16)
    acc_ref[...] = acc_in[...]
    for tile in range(slots):
        slot = src_ref[tile] - blocks
        kind = slot // cap
        m = lax.rem(slot, cap)
        row_a = place_a - offset_of(kind)
        row_b = place_b - offset_of(kind)
        got = jnp.where(inside(row_a), a_ref[bounded(row_a), m], b_ref[bounded(row_b), m])
        rows = jnp.concatenate([got, ones], axis=0)
        dst = dst_ref[tile]
        acc_ref[dst] += dot(rows, half_ref[tile], LAST)[: dim + 8]
    for block in range(blocks):
        degree = jnp.maximum(acc_ref[block, dim : dim + 8], 1.0)
        deg_ref[block] = degree
        agg_ref[block // 2, block % 2] = (acc_ref[block, :dim] / degree[:1]).astype(BF16)


def node_kernel(
    keep_ref,
    got_ref,
    one_ref,
    two_ref,
    three_ref,
    agg_ref,
    deg_ref,
    wt_ref,
    neigh_ref,
    own_w_ref,
    bias_ref,
    scaled_ref,
    keep_own_ref,
    away_own_ref,
    dz_ref,
    xa_ref,
    cot_ref,
    own_ref,
):
    _, per_col, dim, width = scaled_ref.shape
    cols = X * Z_HI
    full = cols * dim
    x, z_hi = column()
    arrived = [(keep_ref[x], got_ref[x])]
    arrived += [(ref[0], ref[1]) for ref in (one_ref, two_ref, three_ref)]
    for step, pair in enumerate(arrived):
        source = lax.rem(x + X - step, X)
        for z, piece in ((z_hi, pair[0]), (1 - z_hi, pair[1])):
            rows = pl.ds(pl.multiple_of((source * Z_HI + z) * dim, dim), dim)
            for p in range(per_col):
                lanes = slice(p * width, (p + 1) * width)
                xa_ref[rows, lanes] = piece[0, p]
                cot_ref[rows, lanes] = piece[1, p]
    for p in range(per_col):
        lanes = slice(p * width, (p + 1) * width)
        xa_ref[full:, lanes] = agg_ref[:, p].reshape(full, width)
        pre = dot(wt_ref[...], xa_ref[:, lanes]) + bias_ref[...]
        dz = (cot_ref[:, lanes].astype(F32) * gelu_slope(pre)).astype(BF16)
        dz_ref[:, lanes] = dz
        degree = deg_ref[(x * Z_HI + z_hi) * per_col + p][:1]
        scaled = (dot(neigh_ref[...], dz) / degree).astype(BF16)
        scaled_ref[:, p] = scaled.reshape(cols, dim, width)
        own_ref[:, lanes] = dot(own_w_ref[...], dz).astype(BF16)
    for to in range(X):
        for out, z in ((keep_own_ref, z_hi), (away_own_ref, 1 - z_hi)):
            rows = pl.ds(pl.multiple_of((to * Z_HI + z) * dim, dim), dim)
            for p in range(per_col):
                out[to, p] = own_ref[rows, p * width : (p + 1) * width]


def weight_kernel(dim, xa_ref, dz_ref, part_ref):
    full = dz_ref.shape[0]
    grads = dot(xa_ref[...], dz_ref[...], LAST)
    total = dot(jnp.ones((16, dz_ref.shape[1]), BF16), dz_ref[...], LAST)
    tail = jnp.concatenate([total[:8, :128], total[8:, 128:]], axis=0).astype(BF16)
    for which in range(2):
        for quarter in range(4):
            for x in range(X):
                rows = [
                    grads[start : start + 8]
                    for z in range(Z_HI)
                    for start in [which * full + (x * Z_HI + z) * dim + quarter * 8]
                ]
                piece = (which * 4 + quarter) * X + x
                part_ref[piece, :, :full] = jnp.concatenate(rows, axis=0).astype(BF16)
                part_ref[piece, :, full:] = tail


def fold_kernel(part_ref, mine_ref, other_ref):
    full = part_ref.shape[2] - 128
    z_hi = column()[1]
    total = part_ref[0].astype(F32)
    for i in range(1, part_ref.shape[0]):
        total += part_ref[i].astype(F32)
    tail = jnp.concatenate([total[0:4, full:], total[8:12, full:]], axis=0)
    low, high = total[:8, :full], total[8:, :full]
    mine_ref[:, :full] = jnp.where(z_hi == 0, low, high)
    other_ref[:, :full] = jnp.where(z_hi == 0, high, low)
    mine_ref[:, full:] = tail
    other_ref[:, full:] = tail


def order_kernel(near_ref, far_ref, self_ref, neigh_ref):
    blk = lax.axis_index("blk")
    mine = blk // (Z_LO * CORE) * CORE + lax.rem(blk, CORE)
    for piece in range(Y * CORE):
        offset = jnp.bitwise_xor(mine, piece)
        rows = jnp.where(lax.rem(offset, 2) == 0, near_ref[offset // 2], far_ref[offset // 2])
        out = self_ref if piece < 4 else neigh_ref
        out[piece % 4 * 8 : piece % 4 * 8 + 8] = rows


def contribution_kernel(slots, home_ref, dst_ref, src_ref, half_ref, a_ref, b_ref, hold_ref):
    place_a, place_b = places()
    blocks = home_ref.shape[0] * home_ref.shape[1]
    cap = a_ref.shape[1]
    for tile in range(slots):
        dst = dst_ref[tile]
        value = dot(home_ref[dst // 2, lax.rem(dst, 2)], half_ref[tile])
        hold_ref[src_ref[tile] - blocks] = value.astype(BF16)
    for ref, place in ((b_ref, place_b), (a_ref, place_a)):
        for peer in range(GROUP):
            kind = kind_of(place - peer)
            for m in range(cap):
                ref[peer, m] = hold_ref[kind * cap + m]


def local_back_kernel(slots, home_ref, dst_ref, src_ref, half_ref, acc_ref):
    acc_ref[...] = jnp.zeros_like(acc_ref)
    for tile in range(slots, half_ref.shape[0]):
        dst = dst_ref[tile]
        src = src_ref[tile]
        acc_ref[src] += dot(home_ref[dst // 2, lax.rem(dst, 2)], half_ref[tile])


def finish_kernel(
    acc_in, a_ref, b_ref, keep_ref, got_ref, one_ref, two_ref, three_ref, send_ref, out_ref, acc_ref
):
    place_a, place_b = places()
    x, z_hi = column()
    kinds, cap = send_ref.shape
    width = acc_in.shape[2]
    per = keep_ref.shape[1]
    arrived = [(keep_ref[x], got_ref[x])]
    arrived += [(ref[0], ref[1]) for ref in (one_ref, two_ref, three_ref)]
    for step, pair in enumerate(arrived):
        source = lax.rem(x + X - step, X)
        for z, piece in ((z_hi, pair[0]), (1 - z_hi, pair[1])):
            for p in range(per):
                block = (source * Z_HI + z) * per + p
                acc_ref[block] = acc_in[block] + piece[p].astype(F32)
    for kind in range(kinds):
        offset = (kind // 2 + 1) * (1 - 2 * (kind % 2))
        row_a = place_a + offset
        row_b = place_b + offset
        for m in range(cap):
            got = jnp.where(inside(row_a), a_ref[bounded(row_a), m], b_ref[bounded(row_b), m])
            acc_ref[send_ref[kind, m]] += got.astype(F32)
    for block in range(acc_ref.shape[0]):
        out_ref[:, block * width : (block + 1) * width] = acc_ref[block].astype(BF16)


def rank(y, z_lo, core, x, z_hi):
    return ((y * Z_LO + z_lo) * CORE + core) * X * Z_HI + x * Z_HI + z_hi


def swap(rows, shift):
    devices = lax.axis_size("blk")
    groups = [
        [(first + shift + i) % devices for i in range(GROUP)] for first in range(0, devices, GROUP)
    ]
    return lax.all_to_all(rows, "blk", 0, 0, axis_index_groups=groups, tiled=False)


def over_col(rows):
    return lax.all_to_all(rows, "col", 0, 0, tiled=False)


def flip_z(rows):
    return lax.ppermute(rows, "col", [(c, c ^ 1) for c in range(X * Z_HI)])


def turn_x(keep, got):
    shape = jax.ShapeDtypeStruct((2,) + keep.shape[1:], BF16)
    sent = call(relay_kernel, (shape,) * (X - 1), [VMEM] * 2)(keep, got)
    cols = X * Z_HI
    return [
        lax.ppermute(piece, "col", [(c, (c + Z_HI * step) % cols) for c in range(cols)])
        for step, piece in enumerate(sent, start=1)
    ]


def across(rows, bit):
    return lax.ppermute(rows, "blk", [(e, e ^ bit) for e in range(Y * Z_LO * CORE)])


def per_device(
    node_feats, tile_dst, tile_src, tile_cnt, send_blk, self_weight, neigh_weight, bias, cotangent
):
    dim, nodes = node_feats.shape
    tiles, width = tile_cnt.shape[:2]
    blocks = nodes // width
    table = send_blk[0]
    kinds, cap = table.shape
    slots = kinds * cap
    cols = X * Z_HI
    per_col = blocks // cols
    full = cols * dim
    chunk = 8
    halo = jax.ShapeDtypeStruct((GROUP, cap, dim, width), BF16)
    ranged = jax.ShapeDtypeStruct((cols, per_col, dim, width), BF16)
    half_x = jax.ShapeDtypeStruct((X, 2, per_col, dim, width), BF16)
    half_own = jax.ShapeDtypeStruct((X, per_col, dim, width), BF16)

    send_a, send_b = call(
        functools.partial(pack_kernel, width), (halo, halo), [VMEM, SMEM]
    )(node_feats, table)
    got_b = swap(send_b, GROUP // 2)
    keep, away = call(
        functools.partial(split_kernel, width), (half_x, half_x), [VMEM] * 2
    )(node_feats, cotangent)
    got = flip_z(away)
    send_a, got_b = lax.optimization_barrier((send_a, got_b))
    got_a = swap(send_a, 0)
    whole = lambda shape: pl.BlockSpec(shape, lambda i: (0,) * len(shape))
    half, acc = pl.pallas_call(
        functools.partial(local_kernel, slots, chunk),
        grid=(tiles // chunk,),
        out_shape=(
            jax.ShapeDtypeStruct(tile_cnt.shape, BF16),
            jax.ShapeDtypeStruct((blocks, dim + 8, width), F32),
        ),
        in_specs=[
            whole((dim, nodes)),
            SMEM,
            SMEM,
            pl.BlockSpec((chunk, width, width), lambda i: (i, 0, 0)),
        ],
        out_specs=(
            pl.BlockSpec((chunk, width, width), lambda i: (i, 0, 0)),
            whole((blocks, dim + 8, width)),
        ),
        compiler_params=pltpu.CompilerParams(vmem_limit_bytes=32 * 2**20),
        cost_estimate=pl.CostEstimate(
            flops=60000000, bytes_accessed=6000000, transcendentals=0
        ),
    )(node_feats, tile_dst, tile_src, tile_cnt)
    weight_t = jnp.concatenate([self_weight.T, neigh_weight.T], axis=1)
    bias_col = bias[:, None]
    agg, degree = call(
        functools.partial(aggregate_kernel, slots),
        (ranged, jax.ShapeDtypeStruct((blocks, 8, width), F32)),
        [VMEM, VMEM, SMEM, SMEM, VMEM, VMEM],
        [pltpu.VMEM((blocks, dim + 8, width), F32)],
    )(got_a, got_b, tile_dst, tile_src, half, acc)
    got, agg = lax.optimization_barrier((got, agg))
    agg = over_col(agg)
    turned = turn_x(keep, got)
    scaled, keep_own, away_own, dz, xa = call(
        node_kernel,
        (
            ranged,
            half_own,
            half_own,
            jax.ShapeDtypeStruct((full, per_col * width), BF16),
            jax.ShapeDtypeStruct((2 * full, per_col * width), BF16),
        ),
        [VMEM] * 11,
        [pltpu.VMEM((full, per_col * width), BF16)] * 2,
    )(keep, got, *turned, agg, degree, weight_t, neigh_weight, self_weight, bias_col)
    scaled = over_col(scaled)
    part = call(
        functools.partial(weight_kernel, dim),
        jax.ShapeDtypeStruct((Y * CORE * X, 16, full + 128), BF16),
        [VMEM] * 2,
    )(xa, dz)
    part, scaled, away_own = lax.optimization_barrier((part, scaled, away_own))

    flat = [
        [rank(y, l, c, x, h) for y in range(Y) for c in range(CORE) for x in range(X)]
        for l in range(Z_LO)
        for h in range(Z_HI)
    ]
    part = lax.all_to_all(part, ("blk", "col"), 0, 0, axis_index_groups=flat, tiled=False)
    got_own = flip_z(away_own)
    away_a, away_b = call(
        functools.partial(contribution_kernel, slots),
        (halo, halo),
        [VMEM, SMEM, SMEM, VMEM],
        [pltpu.VMEM((slots, dim, width), BF16)],
    )(scaled, tile_dst, tile_src, half)
    away_b, part = lax.optimization_barrier((away_b, part))
    back_b = swap(away_b, GROUP // 2)
    away_a, back_b = lax.optimization_barrier((away_a, back_b))
    back_a = swap(away_a, 0)
    piece = jax.ShapeDtypeStruct((8, full + 128), F32)
    mine, other = call(fold_kernel, (piece, piece), [VMEM])(part)
    mine += flip_z(other)
    for bit in (CORE, 2 * CORE, 4 * CORE):
        mine += across(mine, bit)
    grad_bias = jnp.concatenate([mine[0, full:], mine[4, full:]])
    grad_bias = lax.dynamic_slice_in_dim(grad_bias, lax.axis_index("col") * dim, dim, 0)
    rows = mine[None, :, :full]
    for bit in (CORE * Z_LO, 2 * CORE * Z_LO):
        rows = jnp.concatenate([rows, across(rows, bit)], axis=0)
    grad = jax.ShapeDtypeStruct((dim, full), F32)
    grad_self, grad_neigh = call(order_kernel, (grad, grad), [VMEM] * 2)(rows, across(rows, 1))
    acc = call(
        functools.partial(local_back_kernel, slots),
        jax.ShapeDtypeStruct((blocks, dim, width), F32),
        [VMEM, SMEM, SMEM, VMEM],
    )(scaled, tile_dst, tile_src, half)
    turned = turn_x(keep_own, got_own)
    grad_feats = call(
        finish_kernel,
        jax.ShapeDtypeStruct((dim, nodes), BF16),
        [VMEM] * 8 + [SMEM],
        [pltpu.VMEM((blocks, dim, width), F32)],
    )(acc, back_a, back_b, keep_own, got_own, *turned, table)
    return grad_feats, grad_self, grad_neigh, grad_bias


def solution(mesh):
    placed = (
        P("col", "blk"),
        P("blk"),
        P("blk"),
        P("blk", None, None),
        P("blk", None, None),
        P(),
        P(),
        P(),
        P("col", "blk"),
    )
    return jax.shard_map(
        per_device,
        mesh=mesh,
        in_specs=placed,
        out_specs=(P("col", "blk"), P("col", None), P("col", None), P("col")),
        check_vma=False,
    )
```

```python
import functools

import jax
import jax.numpy as jnp
from jax import lax
from jax.experimental import pallas as pl
from jax.experimental.pallas import tpu as pltpu
from jax.sharding import PartitionSpec as P

GROUP = 8
Y, Z_LO, CORE, X, Z_HI = 4, 8, 2, 4, 2
BF16 = jnp.bfloat16
F32 = jnp.float32
FIRST = (((0,), (0,)), ((), ()))
LAST = (((1,), (1,)), ((), ()))
VMEM = pl.BlockSpec(memory_space=pltpu.VMEM)
SMEM = pl.BlockSpec(memory_space=pltpu.SMEM)


def gelu_slope(pre_act):
    inner = 0.7978845608 * (pre_act + 0.044715 * pre_act * pre_act * pre_act)
    tanh_value = jnp.tanh(inner)
    return 0.5 * (1.0 + tanh_value) + 0.5 * pre_act * (
        1.0 - tanh_value * tanh_value
    ) * 0.7978845608 * (1.0 + 3.0 * 0.044715 * pre_act * pre_act)


def dot(left, right, dims=(((1,), (0,)), ((), ()))):
    return lax.dot_general(left, right, dims, preferred_element_type=F32)


def call(body, out_shape, in_specs, scratch=(), cost=(1e7, 1e6)):
    outs = jax.tree.map(lambda _: VMEM, out_shape)
    return pl.pallas_call(
        body,
        out_shape=out_shape,
        in_specs=in_specs,
        out_specs=outs,
        scratch_shapes=scratch,
        compiler_params=pltpu.CompilerParams(vmem_limit_bytes=32 * 2**20),
        cost_estimate=pl.CostEstimate(
            flops=int(cost[0]), bytes_accessed=int(cost[1]), transcendentals=0
        ),
    )


def places():
    blk = lax.axis_index("blk")
    return lax.rem(blk, GROUP), lax.rem(blk + GROUP // 2, GROUP)


def kind_of(distance):
    k = 2 * (jnp.abs(distance) - 1) + jnp.where(distance < 0, 1, 0)
    return jnp.clip(k, 0, 7)


def offset_of(kind):
    return (kind // 2 + 1) * (1 - 2 * lax.rem(kind, 2))


def inside(place):
    return jnp.logical_and(place >= 0, place < GROUP)


def bounded(place):
    return jnp.clip(place, 0, GROUP - 1)


def pack_kernel(width, x_ref, send_ref, a_ref, b_ref):
    place_a, place_b = places()
    cap = send_ref.shape[1]
    for ref, place in ((b_ref, place_b), (a_ref, place_a)):
        for peer in range(GROUP):
            kind = kind_of(peer - place)
            for m in range(cap):
                start = pl.multiple_of(send_ref[kind, m] * width, width)
                ref[peer, m] = x_ref[:, pl.ds(start, width)]


def column():
    col = lax.axis_index("col")
    return col // Z_HI, lax.rem(col, Z_HI)


def range_half():
    z = column()[1] * Z_LO + lax.rem(lax.axis_index("blk") // CORE, Z_LO)
    middle = jnp.logical_and(z >= Z_LO // 2, z < Z_LO // 2 * 3)
    return jnp.where(middle, 0, 1)


def split_kernel(width, x_ref, cot_ref, plus_ref, minus_ref):
    z_hi = column()[1]
    per = plus_ref.shape[2]
    for x in range(X):
        for out, h in ((plus_ref, z_hi), (minus_ref, 1 - z_hi)):
            for p in range(per):
                start = pl.multiple_of(((x * Z_HI + h) * per + p) * width, width)
                out[x, 0, p] = x_ref[:, pl.ds(start, width)]
                out[x, 1, p] = cot_ref[:, pl.ds(start, width)]


def join_kernel(xc_plus_ref, xc_minus_ref, agg_plus_ref, agg_minus_ref, out_ref):
    for side, (xc, agg) in enumerate(((xc_plus_ref, agg_plus_ref), (xc_minus_ref, agg_minus_ref))):
        for which in range(2):
            out_ref[:, which, side] = xc[:, which]
        out_ref[:, 2, side] = agg[...]


def join_back_kernel(plus_ref, minus_ref, out_ref):
    out_ref[:, 0] = plus_ref[...]
    out_ref[:, 1] = minus_ref[...]


def local_kernel(slots, chunk, x_ref, dst_ref, src_ref, cnt_ref, half_ref, acc_ref):
    step = pl.program_id(0)
    width = cnt_ref.shape[1]
    dim = x_ref.shape[0]
    half_ref[...] = cnt_ref[...].astype(F32).astype(BF16)

    @pl.when(step == 0)
    def _():
        acc_ref[...] = jnp.zeros_like(acc_ref)

    @pl.when(step * chunk >= slots)
    def _():
        ones = jnp.ones((16, width), BF16)
        for i in range(chunk):
            tile = step * chunk + i
            start = pl.multiple_of(src_ref[tile] * width, width)
            rows = jnp.concatenate([x_ref[:, pl.ds(start, width)], ones], axis=0)
            dst = dst_ref[tile]
            acc_ref[dst] += dot(rows, half_ref[i], LAST)[: dim + 8]


def aggregate_kernel(
    slots, a_ref, b_ref, dst_ref, src_ref, half_ref, acc_in, plus_ref, minus_ref, deg_ref, acc_ref
):
    place_a, place_b = places()
    z_hi = column()[1]
    cap, dim, width = a_ref.shape[1:]
    blocks = acc_in.shape[0]
    per = plus_ref.shape[1]
    ones = jnp.ones((16, width), BF16)
    acc_ref[...] = acc_in[...]
    for tile in range(slots):
        slot = src_ref[tile] - blocks
        kind = slot // cap
        m = lax.rem(slot, cap)
        row_a = place_a - offset_of(kind)
        row_b = place_b - offset_of(kind)
        got = jnp.where(inside(row_a), a_ref[bounded(row_a), m], b_ref[bounded(row_b), m])
        rows = jnp.concatenate([got, ones], axis=0)
        dst = dst_ref[tile]
        acc_ref[dst] += dot(rows, half_ref[tile], LAST)[: dim + 8]
    for block in range(blocks):
        deg_ref[block] = jnp.maximum(acc_ref[block, dim : dim + 8], 1.0)
    for x in range(X):
        for out, h in ((plus_ref, z_hi), (minus_ref, 1 - z_hi)):
            for p in range(per):
                block = (x * Z_HI + h) * per + p
                out[x, p] = (acc_ref[block, :dim] / deg_ref[block, :1]).astype(BF16)


def node_kernel(
    in_ref, wt_ref, neigh_ref, own_w_ref, bias_ref, plus_ref, minus_ref, dz_ref, xa_ref, cot_ref, home_ref
):
    _, _, sides, per_col, dim, width = in_ref.shape
    full = X * Z_HI * dim
    half = range_half()
    for x in range(X):
        for side, z in ((0, half), (1, 1 - half)):
            start = (x * Z_HI + z) * dim
            rows = pl.ds(pl.multiple_of(start, dim), dim)
            agg_rows = pl.ds(pl.multiple_of(full + start, dim), dim)
            for p in range(per_col):
                lanes = slice(p * width, (p + 1) * width)
                xa_ref[rows, lanes] = in_ref[x, 0, side, p]
                cot_ref[rows, lanes] = in_ref[x, 1, side, p]
                xa_ref[agg_rows, lanes] = in_ref[x, 2, side, p]
    for p in range(per_col):
        lanes = slice(p * width, (p + 1) * width)
        pre = dot(wt_ref[...], xa_ref[:, lanes]) + bias_ref[...]
        dz = (cot_ref[:, lanes].astype(F32) * gelu_slope(pre)).astype(BF16)
        dz_ref[:, lanes] = dz
        home_ref[0, :, lanes] = dot(neigh_ref[...], dz).astype(BF16)
        home_ref[1, :, lanes] = dot(own_w_ref[...], dz).astype(BF16)
    for x in range(X):
        for out, z in ((minus_ref, half), (plus_ref, 1 - half)):
            rows = pl.ds(pl.multiple_of((x * Z_HI + z) * dim, dim), dim)
            for which in range(2):
                for p in range(per_col):
                    out[x, which, p] = home_ref[which, rows, p * width : (p + 1) * width]


def weight_kernel(dim, xa_ref, dz_ref, part_ref):
    full = dz_ref.shape[0]
    grads = dot(xa_ref[...], dz_ref[...], LAST)
    total = dot(jnp.ones((16, dz_ref.shape[1]), BF16), dz_ref[...], LAST)
    tail = jnp.concatenate([total[:8, :128], total[8:, 128:]], axis=0).astype(BF16)
    for which in range(2):
        for quarter in range(4):
            for x in range(X):
                rows = [
                    grads[start : start + 8]
                    for z in range(Z_HI)
                    for start in [which * full + (x * Z_HI + z) * dim + quarter * 8]
                ]
                piece = (which * 4 + quarter) * X + x
                part_ref[piece, :, :full] = jnp.concatenate(rows, axis=0).astype(BF16)
                part_ref[piece, :, full:] = tail


def contribution_kernel(
    slots, home_ref, deg_ref, dst_ref, src_ref, half_ref, a_ref, b_ref, scaled_ref, hold_ref
):
    place_a, place_b = places()
    z_hi = column()[1]
    blocks = scaled_ref.shape[0]
    cap = a_ref.shape[1]
    per = home_ref.shape[3]
    for x in range(X):
        for side, h in ((0, 1 - z_hi), (1, z_hi)):
            for p in range(per):
                block = (x * Z_HI + h) * per + p
                value = home_ref[x, side, 0, p].astype(F32) / deg_ref[block, :1]
                scaled_ref[block] = value.astype(BF16)
    for tile in range(slots):
        value = dot(scaled_ref[dst_ref[tile]], half_ref[tile])
        hold_ref[src_ref[tile] - blocks] = value.astype(BF16)
    for ref, place in ((b_ref, place_b), (a_ref, place_a)):
        for peer in range(GROUP):
            kind = kind_of(place - peer)
            for m in range(cap):
                ref[peer, m] = hold_ref[kind * cap + m]


def local_back_kernel(slots, scaled_ref, home_ref, dst_ref, src_ref, half_ref, acc_ref):
    z_hi = column()[1]
    per = home_ref.shape[3]
    for x in range(X):
        for side, h in ((0, 1 - z_hi), (1, z_hi)):
            for p in range(per):
                acc_ref[(x * Z_HI + h) * per + p] = home_ref[x, side, 1, p].astype(F32)
    for tile in range(slots, half_ref.shape[0]):
        acc_ref[src_ref[tile]] += dot(scaled_ref[dst_ref[tile]], half_ref[tile])


def finish_kernel(acc_in, a_ref, b_ref, send_ref, out_ref, acc_ref):
    place_a, place_b = places()
    kinds, cap = send_ref.shape
    width = acc_in.shape[2]
    acc_ref[...] = acc_in[...]
    for kind in range(kinds):
        offset = (kind // 2 + 1) * (1 - 2 * (kind % 2))
        row_a = place_a + offset
        row_b = place_b + offset
        for m in range(cap):
            got = jnp.where(inside(row_a), a_ref[bounded(row_a), m], b_ref[bounded(row_b), m])
            acc_ref[send_ref[kind, m]] += got.astype(F32)
    for block in range(acc_ref.shape[0]):
        out_ref[:, block * width : (block + 1) * width] = acc_ref[block].astype(BF16)


def rank(y, z_lo, core, x, z_hi):
    return ((y * Z_LO + z_lo) * CORE + core) * X * Z_HI + x * Z_HI + z_hi


def swap(rows, shift):
    devices = lax.axis_size("blk")
    groups = [
        [(first + shift + i) % devices for i in range(GROUP)] for first in range(0, devices, GROUP)
    ]
    return lax.all_to_all(rows, "blk", 0, 0, axis_index_groups=groups, tiled=False)


def over_x(rows):
    groups = [[x * Z_HI + h for x in range(X)] for h in range(Z_HI)]
    return lax.all_to_all(rows, "col", 0, 0, axis_index_groups=groups, tiled=False)


def along_z(rows, step):
    chips = Z_LO * Z_HI
    route = []
    for y in range(Y):
        for core in range(CORE):
            for x in range(X):
                for z in range(chips):
                    to = (z + step) % chips
                    route.append(
                        (
                            rank(y, z % Z_LO, core, x, z // Z_LO),
                            rank(y, to % Z_LO, core, x, to // Z_LO),
                        )
                    )
    return lax.ppermute(rows, ("blk", "col"), sorted(route))


def per_device(
    node_feats, tile_dst, tile_src, tile_cnt, send_blk, self_weight, neigh_weight, bias, cotangent
):
    dim, nodes = node_feats.shape
    tiles, width = tile_cnt.shape[:2]
    blocks = nodes // width
    table = send_blk[0]
    kinds, cap = table.shape
    slots = kinds * cap
    cols = X * Z_HI
    per_col = blocks // cols
    full = cols * dim
    chunk = 8
    shape = lambda *dims: jax.ShapeDtypeStruct(dims + (dim, width), BF16)
    halo = shape(GROUP, cap)
    step = Z_LO // 2

    send_a, send_b = call(
        functools.partial(pack_kernel, width), (halo, halo), [VMEM, SMEM]
    )(node_feats, table)
    got_b = swap(send_b, GROUP // 2)
    xc_plus, xc_minus = call(
        functools.partial(split_kernel, width), (shape(X, 2, per_col),) * 2, [VMEM] * 2
    )(node_feats, cotangent)
    send_a, got_b, xc_plus, xc_minus = lax.optimization_barrier((send_a, got_b, xc_plus, xc_minus))
    xc_plus = along_z(xc_plus, step)
    xc_minus = along_z(xc_minus, -step)
    got_a = swap(send_a, 0)
    whole = lambda shape: pl.BlockSpec(shape, lambda i: (0,) * len(shape))
    half, acc = pl.pallas_call(
        functools.partial(local_kernel, slots, chunk),
        grid=(tiles // chunk,),
        out_shape=(
            jax.ShapeDtypeStruct(tile_cnt.shape, BF16),
            jax.ShapeDtypeStruct((blocks, dim + 8, width), F32),
        ),
        in_specs=[
            whole((dim, nodes)),
            SMEM,
            SMEM,
            pl.BlockSpec((chunk, width, width), lambda i: (i, 0, 0)),
        ],
        out_specs=(
            pl.BlockSpec((chunk, width, width), lambda i: (i, 0, 0)),
            whole((blocks, dim + 8, width)),
        ),
        compiler_params=pltpu.CompilerParams(vmem_limit_bytes=32 * 2**20),
        cost_estimate=pl.CostEstimate(
            flops=60000000, bytes_accessed=6000000, transcendentals=0
        ),
    )(node_feats, tile_dst, tile_src, tile_cnt)
    weight_t = jnp.concatenate([self_weight.T, neigh_weight.T], axis=1)
    bias_col = bias[:, None]
    agg_plus, agg_minus, degree = call(
        functools.partial(aggregate_kernel, slots),
        (shape(X, per_col), shape(X, per_col), jax.ShapeDtypeStruct((blocks, 8, width), F32)),
        [VMEM, VMEM, SMEM, SMEM, VMEM, VMEM],
        [pltpu.VMEM((blocks, dim + 8, width), F32)],
    )(got_a, got_b, tile_dst, tile_src, half, acc)
    agg_plus = along_z(agg_plus, step)
    agg_minus = along_z(agg_minus, -step)
    ranged = call(join_kernel, shape(X, 3, 2, per_col), [VMEM] * 4)(
        xc_plus, xc_minus, agg_plus, agg_minus
    )
    ranged = over_x(ranged)
    plus, minus, dz, xa = call(
        node_kernel,
        (
            shape(X, 2, per_col),
            shape(X, 2, per_col),
            jax.ShapeDtypeStruct((full, per_col * width), BF16),
            jax.ShapeDtypeStruct((2 * full, per_col * width), BF16),
        ),
        [VMEM] * 5,
        [
            pltpu.VMEM((full, per_col * width), BF16),
            pltpu.VMEM((2, full, per_col * width), BF16),
        ],
    )(ranged, weight_t, neigh_weight, self_weight, bias_col)
    plus = along_z(plus, step)
    minus = along_z(minus, -step)
    part = call(
        functools.partial(weight_kernel, dim),
        jax.ShapeDtypeStruct((Y * CORE * X, 16, full + 128), BF16),
        [VMEM] * 2,
    )(xa, dz)

    both = ("blk", "col")
    flat = [
        [rank(y, l, c, x, h) for y in range(Y) for c in range(CORE) for x in range(X)]
        for l in range(Z_LO)
        for h in range(Z_HI)
    ]
    line = [
        [rank(y, l, c, x, h) for h in range(Z_HI) for l in range(Z_LO)]
        for y in range(Y)
        for c in range(CORE)
        for x in range(X)
    ]
    plane = [[(y * Z_LO + l) * CORE + c for y in range(Y) for c in range(CORE)] for l in range(Z_LO)]
    part = lax.all_to_all(part, both, 0, 0, axis_index_groups=flat, tiled=False)
    home = call(join_back_kernel, shape(X, 2, 2, per_col), [VMEM] * 2)(plus, minus)
    home, part = lax.optimization_barrier((home, part))
    home = over_x(home)
    away_a, away_b, scaled = call(
        functools.partial(contribution_kernel, slots),
        (halo, halo, shape(blocks)),
        [VMEM, VMEM, SMEM, SMEM, VMEM],
        [pltpu.VMEM((slots, dim, width), BF16)],
    )(home, degree, tile_dst, tile_src, half)
    back_b = swap(away_b, GROUP // 2)
    away_a, back_b = lax.optimization_barrier((away_a, back_b))
    back_a = swap(away_a, 0)
    part = jnp.sum(part.astype(F32), axis=0)
    tail = jnp.concatenate([part[0:4, full:], part[8:12, full:]], axis=0)
    ends = [jnp.concatenate([part[8 * h : 8 * h + 8, :full], tail], axis=1) for h in range(Z_HI)]
    part = jnp.broadcast_to(jnp.stack(ends)[:, None], (Z_HI, Z_LO, 8, full + 128))
    part = part.reshape(Z_HI * Z_LO, 8, full + 128)
    part, back_a = lax.optimization_barrier((part, back_a))
    part = jnp.sum(lax.all_to_all(part, both, 0, 0, axis_index_groups=line, tiled=False), axis=0)
    grad_bias = jnp.concatenate([part[0, full:], part[4, full:]])
    grad_bias = lax.dynamic_slice_in_dim(grad_bias, lax.axis_index("col") * dim, dim, 0)
    part = jnp.broadcast_to(part[None, :, :full], (Y * CORE, 8, full))
    part = lax.all_to_all(part, "blk", 0, 0, axis_index_groups=plane, tiled=False)
    part = part.reshape(2, dim, full)
    grad_self, grad_neigh = part[0], part[1]
    acc = call(
        functools.partial(local_back_kernel, slots),
        jax.ShapeDtypeStruct((blocks, dim, width), F32),
        [VMEM, VMEM, SMEM, SMEM, VMEM],
    )(scaled, home, tile_dst, tile_src, half)
    grad_feats = call(
        finish_kernel,
        jax.ShapeDtypeStruct((dim, nodes), BF16),
        [VMEM, VMEM, VMEM, SMEM],
        [pltpu.VMEM((blocks, dim, width), F32)],
    )(acc, back_a, back_b, table)
    return grad_feats, grad_self, grad_neigh, grad_bias


def solution(mesh):
    placed = (
        P("col", "blk"),
        P("blk"),
        P("blk"),
        P("blk", None, None),
        P("blk", None, None),
        P(),
        P(),
        P(),
        P("col", "blk"),
    )
    return jax.shard_map(
        per_device,
        mesh=mesh,
        in_specs=placed,
        out_specs=(P("col", "blk"), P("col", None), P("col", None), P("col")),
        check_vma=False,
    )
```

```python
import functools

import jax
import jax.numpy as jnp
from jax import lax
from jax.experimental import pallas as pl
from jax.experimental.pallas import tpu as pltpu
from jax.sharding import PartitionSpec as P

GROUP = 8
Y, Z_LO, CORE, X, Z_HI = 4, 8, 2, 4, 2
BF16 = jnp.bfloat16
F32 = jnp.float32
FIRST = (((0,), (0,)), ((), ()))
LAST = (((1,), (1,)), ((), ()))
VMEM = pl.BlockSpec(memory_space=pltpu.VMEM)
SMEM = pl.BlockSpec(memory_space=pltpu.SMEM)


def gelu_slope(pre_act):
    inner = 0.7978845608 * (pre_act + 0.044715 * pre_act * pre_act * pre_act)
    tanh_value = jnp.tanh(inner)
    return 0.5 * (1.0 + tanh_value) + 0.5 * pre_act * (
        1.0 - tanh_value * tanh_value
    ) * 0.7978845608 * (1.0 + 3.0 * 0.044715 * pre_act * pre_act)


def dot(left, right, dims=(((1,), (0,)), ((), ()))):
    return lax.dot_general(left, right, dims, preferred_element_type=F32)


def call(body, out_shape, in_specs, scratch=(), cost=(1e7, 1e6)):
    outs = jax.tree.map(lambda _: VMEM, out_shape)
    return pl.pallas_call(
        body,
        out_shape=out_shape,
        in_specs=in_specs,
        out_specs=outs,
        scratch_shapes=scratch,
        compiler_params=pltpu.CompilerParams(vmem_limit_bytes=32 * 2**20),
        cost_estimate=pl.CostEstimate(
            flops=int(cost[0]), bytes_accessed=int(cost[1]), transcendentals=0
        ),
    )


def places():
    blk = lax.axis_index("blk")
    return lax.rem(blk, GROUP), lax.rem(blk + GROUP // 2, GROUP)


def kind_of(distance):
    k = 2 * (jnp.abs(distance) - 1) + jnp.where(distance < 0, 1, 0)
    return jnp.clip(k, 0, 7)


def offset_of(kind):
    return (kind // 2 + 1) * (1 - 2 * lax.rem(kind, 2))


def inside(place):
    return jnp.logical_and(place >= 0, place < GROUP)


def bounded(place):
    return jnp.clip(place, 0, GROUP - 1)


def pack_kernel(width, x_ref, send_ref, a_ref, b_ref):
    place_a, place_b = places()
    cap = send_ref.shape[1]
    for ref, place in ((b_ref, place_b), (a_ref, place_a)):
        for peer in range(GROUP):
            kind = kind_of(peer - place)
            for m in range(cap):
                start = pl.multiple_of(send_ref[kind, m] * width, width)
                ref[peer, m] = x_ref[:, pl.ds(start, width)]


def column():
    col = lax.axis_index("col")
    return col // Z_HI, lax.rem(col, Z_HI)


def range_half():
    z = column()[1] * Z_LO + lax.rem(lax.axis_index("blk") // CORE, Z_LO)
    middle = jnp.logical_and(z >= Z_LO // 2, z < Z_LO // 2 * 3)
    return jnp.where(middle, 0, 1)


def split_kernel(width, x_ref, cot_ref, plus_ref, minus_ref):
    z_hi = column()[1]
    per = plus_ref.shape[2]
    for x in range(X):
        for out, h in ((plus_ref, z_hi), (minus_ref, 1 - z_hi)):
            for p in range(per):
                start = pl.multiple_of(((x * Z_HI + h) * per + p) * width, width)
                out[x, 0, p] = x_ref[:, pl.ds(start, width)]
                out[x, 1, p] = cot_ref[:, pl.ds(start, width)]


def join_kernel(xc_plus_ref, xc_minus_ref, agg_plus_ref, agg_minus_ref, out_ref):
    for side, (xc, agg) in enumerate(((xc_plus_ref, agg_plus_ref), (xc_minus_ref, agg_minus_ref))):
        for which in range(2):
            out_ref[:, which, side] = xc[:, which]
        out_ref[:, 2, side] = agg[...]


def join_back_kernel(plus_ref, minus_ref, out_ref):
    out_ref[:, 0] = plus_ref[...]
    out_ref[:, 1] = minus_ref[...]


def local_kernel(slots, chunk, x_ref, dst_ref, src_ref, cnt_ref, half_ref, acc_ref):
    step = pl.program_id(0)
    width = cnt_ref.shape[1]
    dim = x_ref.shape[0]
    half_ref[...] = cnt_ref[...].astype(F32).astype(BF16)

    @pl.when(step == 0)
    def _():
        acc_ref[...] = jnp.zeros_like(acc_ref)

    @pl.when(step * chunk >= slots)
    def _():
        ones = jnp.ones((16, width), BF16)
        for i in range(chunk):
            tile = step * chunk + i
            start = pl.multiple_of(src_ref[tile] * width, width)
            rows = jnp.concatenate([x_ref[:, pl.ds(start, width)], ones], axis=0)
            dst = dst_ref[tile]
            acc_ref[dst] += dot(rows, half_ref[i], LAST)[: dim + 8]


def aggregate_kernel(
    slots, a_ref, b_ref, dst_ref, src_ref, half_ref, acc_in, plus_ref, minus_ref, deg_ref, acc_ref
):
    place_a, place_b = places()
    z_hi = column()[1]
    cap, dim, width = a_ref.shape[1:]
    blocks = acc_in.shape[0]
    per = plus_ref.shape[1]
    ones = jnp.ones((16, width), BF16)
    acc_ref[...] = acc_in[...]
    for tile in range(slots):
        slot = src_ref[tile] - blocks
        kind = slot // cap
        m = lax.rem(slot, cap)
        row_a = place_a - offset_of(kind)
        row_b = place_b - offset_of(kind)
        got = jnp.where(inside(row_a), a_ref[bounded(row_a), m], b_ref[bounded(row_b), m])
        rows = jnp.concatenate([got, ones], axis=0)
        dst = dst_ref[tile]
        acc_ref[dst] += dot(rows, half_ref[tile], LAST)[: dim + 8]
    for block in range(blocks):
        deg_ref[block] = jnp.maximum(acc_ref[block, dim : dim + 8], 1.0)
    for x in range(X):
        for out, h in ((plus_ref, z_hi), (minus_ref, 1 - z_hi)):
            for p in range(per):
                block = (x * Z_HI + h) * per + p
                out[x, p] = (acc_ref[block, :dim] / deg_ref[block, :1]).astype(BF16)


def node_kernel(
    in_ref, wt_ref, neigh_ref, own_w_ref, bias_ref, plus_ref, minus_ref, dz_ref, xa_ref, cot_ref, home_ref
):
    _, _, sides, per_col, dim, width = in_ref.shape
    full = X * Z_HI * dim
    half = range_half()
    for x in range(X):
        for side, z in ((0, half), (1, 1 - half)):
            start = (x * Z_HI + z) * dim
            rows = pl.ds(pl.multiple_of(start, dim), dim)
            agg_rows = pl.ds(pl.multiple_of(full + start, dim), dim)
            for p in range(per_col):
                lanes = slice(p * width, (p + 1) * width)
                xa_ref[rows, lanes] = in_ref[x, 0, side, p]
                cot_ref[rows, lanes] = in_ref[x, 1, side, p]
                xa_ref[agg_rows, lanes] = in_ref[x, 2, side, p]
    for p in range(per_col):
        lanes = slice(p * width, (p + 1) * width)
        pre = dot(wt_ref[...], xa_ref[:, lanes]) + bias_ref[...]
        dz = (cot_ref[:, lanes].astype(F32) * gelu_slope(pre)).astype(BF16)
        dz_ref[:, lanes] = dz
        home_ref[0, :, lanes] = dot(neigh_ref[...], dz).astype(BF16)
        home_ref[1, :, lanes] = dot(own_w_ref[...], dz).astype(BF16)
    for x in range(X):
        for out, z in ((minus_ref, half), (plus_ref, 1 - half)):
            rows = pl.ds(pl.multiple_of((x * Z_HI + z) * dim, dim), dim)
            for which in range(2):
                for p in range(per_col):
                    out[x, which, p] = home_ref[which, rows, p * width : (p + 1) * width]


def weight_kernel(dim, xa_ref, dz_ref, part_ref):
    full = dz_ref.shape[0]
    grads = dot(xa_ref[...], dz_ref[...], LAST)
    total = dot(jnp.ones((16, dz_ref.shape[1]), BF16), dz_ref[...], LAST)
    tail = jnp.concatenate([total[:8, :128], total[8:, 128:]], axis=0).astype(BF16)
    for which in range(2):
        for quarter in range(4):
            for x in range(X):
                rows = [
                    grads[start : start + 8]
                    for z in range(Z_HI)
                    for start in [which * full + (x * Z_HI + z) * dim + quarter * 8]
                ]
                piece = (which * 4 + quarter) * X + x
                part_ref[piece, :, :full] = jnp.concatenate(rows, axis=0).astype(BF16)
                part_ref[piece, :, full:] = tail


def contribution_kernel(
    slots, home_ref, deg_ref, dst_ref, src_ref, half_ref, a_ref, b_ref, scaled_ref, hold_ref
):
    place_a, place_b = places()
    z_hi = column()[1]
    blocks = scaled_ref.shape[0]
    cap = a_ref.shape[1]
    per = home_ref.shape[3]
    for x in range(X):
        for side, h in ((0, 1 - z_hi), (1, z_hi)):
            for p in range(per):
                block = (x * Z_HI + h) * per + p
                value = home_ref[x, side, 0, p].astype(F32) / deg_ref[block, :1]
                scaled_ref[block] = value.astype(BF16)
    for tile in range(slots):
        value = dot(scaled_ref[dst_ref[tile]], half_ref[tile])
        hold_ref[src_ref[tile] - blocks] = value.astype(BF16)
    for ref, place in ((b_ref, place_b), (a_ref, place_a)):
        for peer in range(GROUP):
            kind = kind_of(place - peer)
            for m in range(cap):
                ref[peer, m] = hold_ref[kind * cap + m]


def local_back_kernel(slots, scaled_ref, home_ref, dst_ref, src_ref, half_ref, acc_ref):
    z_hi = column()[1]
    per = home_ref.shape[3]
    for x in range(X):
        for side, h in ((0, 1 - z_hi), (1, z_hi)):
            for p in range(per):
                acc_ref[(x * Z_HI + h) * per + p] = home_ref[x, side, 1, p].astype(F32)
    for tile in range(slots, half_ref.shape[0]):
        acc_ref[src_ref[tile]] += dot(scaled_ref[dst_ref[tile]], half_ref[tile])


def finish_kernel(acc_in, a_ref, b_ref, send_ref, out_ref, acc_ref):
    place_a, place_b = places()
    kinds, cap = send_ref.shape
    width = acc_in.shape[2]
    acc_ref[...] = acc_in[...]
    for kind in range(kinds):
        offset = (kind // 2 + 1) * (1 - 2 * (kind % 2))
        row_a = place_a + offset
        row_b = place_b + offset
        for m in range(cap):
            got = jnp.where(inside(row_a), a_ref[bounded(row_a), m], b_ref[bounded(row_b), m])
            acc_ref[send_ref[kind, m]] += got.astype(F32)
    for block in range(acc_ref.shape[0]):
        out_ref[:, block * width : (block + 1) * width] = acc_ref[block].astype(BF16)


def rank(y, z_lo, core, x, z_hi):
    return ((y * Z_LO + z_lo) * CORE + core) * X * Z_HI + x * Z_HI + z_hi


def swap(rows, shift):
    devices = lax.axis_size("blk")
    groups = [
        [(first + shift + i) % devices for i in range(GROUP)] for first in range(0, devices, GROUP)
    ]
    return lax.all_to_all(rows, "blk", 0, 0, axis_index_groups=groups, tiled=False)


def over_x(rows):
    groups = [[x * Z_HI + h for x in range(X)] for h in range(Z_HI)]
    return lax.all_to_all(rows, "col", 0, 0, axis_index_groups=groups, tiled=False)


def along_z(rows, step):
    chips = Z_LO * Z_HI
    route = []
    for y in range(Y):
        for core in range(CORE):
            for x in range(X):
                for z in range(chips):
                    to = (z + step) % chips
                    route.append(
                        (
                            rank(y, z % Z_LO, core, x, z // Z_LO),
                            rank(y, to % Z_LO, core, x, to // Z_LO),
                        )
                    )
    return lax.ppermute(rows, ("blk", "col"), sorted(route))


def per_device(
    node_feats, tile_dst, tile_src, tile_cnt, send_blk, self_weight, neigh_weight, bias, cotangent
):
    dim, nodes = node_feats.shape
    tiles, width = tile_cnt.shape[:2]
    blocks = nodes // width
    table = send_blk[0]
    kinds, cap = table.shape
    slots = kinds * cap
    cols = X * Z_HI
    per_col = blocks // cols
    full = cols * dim
    chunk = 8
    shape = lambda *dims: jax.ShapeDtypeStruct(dims + (dim, width), BF16)
    halo = shape(GROUP, cap)
    step = Z_LO // 2

    send_a, send_b = call(
        functools.partial(pack_kernel, width), (halo, halo), [VMEM, SMEM]
    )(node_feats, table)
    got_b = swap(send_b, GROUP // 2)
    xc_plus, xc_minus = call(
        functools.partial(split_kernel, width), (shape(X, 2, per_col),) * 2, [VMEM] * 2
    )(node_feats, cotangent)
    whole = lambda shape: pl.BlockSpec(shape, lambda i: (0,) * len(shape))
    half, acc = pl.pallas_call(
        functools.partial(local_kernel, slots, chunk),
        grid=(tiles // chunk,),
        out_shape=(
            jax.ShapeDtypeStruct(tile_cnt.shape, BF16),
            jax.ShapeDtypeStruct((blocks, dim + 8, width), F32),
        ),
        in_specs=[
            whole((dim, nodes)),
            SMEM,
            SMEM,
            pl.BlockSpec((chunk, width, width), lambda i: (i, 0, 0)),
        ],
        out_specs=(
            pl.BlockSpec((chunk, width, width), lambda i: (i, 0, 0)),
            whole((blocks, dim + 8, width)),
        ),
        compiler_params=pltpu.CompilerParams(vmem_limit_bytes=32 * 2**20),
        cost_estimate=pl.CostEstimate(
            flops=60000000, bytes_accessed=6000000, transcendentals=0
        ),
    )(node_feats, tile_dst, tile_src, tile_cnt)
    send_a, got_b, xc_plus, xc_minus, half, acc = lax.optimization_barrier(
        (send_a, got_b, xc_plus, xc_minus, half, acc)
    )
    xc_plus = along_z(xc_plus, step)
    xc_minus = along_z(xc_minus, -step)
    got_a = swap(send_a, 0)
    weight_t = jnp.concatenate([self_weight.T, neigh_weight.T], axis=1)
    bias_col = bias[:, None]
    agg_plus, agg_minus, degree = call(
        functools.partial(aggregate_kernel, slots),
        (shape(X, per_col), shape(X, per_col), jax.ShapeDtypeStruct((blocks, 8, width), F32)),
        [VMEM, VMEM, SMEM, SMEM, VMEM, VMEM],
        [pltpu.VMEM((blocks, dim + 8, width), F32)],
    )(got_a, got_b, tile_dst, tile_src, half, acc)
    agg_plus = along_z(agg_plus, step)
    agg_minus = along_z(agg_minus, -step)
    ranged = call(join_kernel, shape(X, 3, 2, per_col), [VMEM] * 4)(
        xc_plus, xc_minus, agg_plus, agg_minus
    )
    ranged = over_x(ranged)
    plus, minus, dz, xa = call(
        node_kernel,
        (
            shape(X, 2, per_col),
            shape(X, 2, per_col),
            jax.ShapeDtypeStruct((full, per_col * width), BF16),
            jax.ShapeDtypeStruct((2 * full, per_col * width), BF16),
        ),
        [VMEM] * 5,
        [
            pltpu.VMEM((full, per_col * width), BF16),
            pltpu.VMEM((2, full, per_col * width), BF16),
        ],
    )(ranged, weight_t, neigh_weight, self_weight, bias_col)
    plus = along_z(plus, step)
    minus = along_z(minus, -step)
    part = call(
        functools.partial(weight_kernel, dim),
        jax.ShapeDtypeStruct((Y * CORE * X, 16, full + 128), BF16),
        [VMEM] * 2,
    )(xa, dz)

    both = ("blk", "col")
    flat = [
        [rank(y, l, c, x, h) for y in range(Y) for c in range(CORE) for x in range(X)]
        for l in range(Z_LO)
        for h in range(Z_HI)
    ]
    line = [
        [rank(y, l, c, x, h) for h in range(Z_HI) for l in range(Z_LO)]
        for y in range(Y)
        for c in range(CORE)
        for x in range(X)
    ]
    plane = [[(y * Z_LO + l) * CORE + c for y in range(Y) for c in range(CORE)] for l in range(Z_LO)]
    part = lax.all_to_all(part, both, 0, 0, axis_index_groups=flat, tiled=False)
    home = call(join_back_kernel, shape(X, 2, 2, per_col), [VMEM] * 2)(plus, minus)
    home, part = lax.optimization_barrier((home, part))
    home = over_x(home)
    away_a, away_b, scaled = call(
        functools.partial(contribution_kernel, slots),
        (halo, halo, shape(blocks)),
        [VMEM, VMEM, SMEM, SMEM, VMEM],
        [pltpu.VMEM((slots, dim, width), BF16)],
    )(home, degree, tile_dst, tile_src, half)
    back_b = swap(away_b, GROUP // 2)
    away_a, back_b = lax.optimization_barrier((away_a, back_b))
    back_a = swap(away_a, 0)
    part = jnp.sum(part.astype(F32), axis=0)
    tail = jnp.concatenate([part[0:4, full:], part[8:12, full:]], axis=0)
    ends = [jnp.concatenate([part[8 * h : 8 * h + 8, :full], tail], axis=1) for h in range(Z_HI)]
    part = jnp.broadcast_to(jnp.stack(ends)[:, None], (Z_HI, Z_LO, 8, full + 128))
    part = part.reshape(Z_HI * Z_LO, 8, full + 128).astype(BF16)
    part, back_a = lax.optimization_barrier((part, back_a))
    part = lax.all_to_all(part, both, 0, 0, axis_index_groups=line, tiled=False)
    part = jnp.sum(part.astype(F32), axis=0)
    grad_bias = jnp.concatenate([part[0, full:], part[4, full:]])
    grad_bias = lax.dynamic_slice_in_dim(grad_bias, lax.axis_index("col") * dim, dim, 0)
    part = jnp.broadcast_to(part[None, :, :full].astype(BF16), (Y * CORE, 8, full))
    part = lax.all_to_all(part, "blk", 0, 0, axis_index_groups=plane, tiled=False)
    part = part.astype(F32).reshape(2, dim, full)
    grad_self, grad_neigh = part[0], part[1]
    acc = call(
        functools.partial(local_back_kernel, slots),
        jax.ShapeDtypeStruct((blocks, dim, width), F32),
        [VMEM, VMEM, SMEM, SMEM, VMEM],
    )(scaled, home, tile_dst, tile_src, half)
    grad_feats = call(
        finish_kernel,
        jax.ShapeDtypeStruct((dim, nodes), BF16),
        [VMEM, VMEM, VMEM, SMEM],
        [pltpu.VMEM((blocks, dim, width), F32)],
    )(acc, back_a, back_b, table)
    return grad_feats, grad_self, grad_neigh, grad_bias


def solution(mesh):
    placed = (
        P("col", "blk"),
        P("blk"),
        P("blk"),
        P("blk", None, None),
        P("blk", None, None),
        P(),
        P(),
        P(),
        P("col", "blk"),
    )
    return jax.shard_map(
        per_device,
        mesh=mesh,
        in_specs=placed,
        out_specs=(P("col", "blk"), P("col", None), P("col", None), P("col")),
        check_vma=False,
    )
```

```python
import functools

import jax
import jax.numpy as jnp
from jax import lax
from jax.experimental import pallas as pl
from jax.experimental.pallas import tpu as pltpu
from jax.sharding import PartitionSpec as P

GROUP = 8
Y, Z_LO, CORE, X, Z_HI = 4, 8, 2, 4, 2
BF16 = jnp.bfloat16
F32 = jnp.float32
FIRST = (((0,), (0,)), ((), ()))
LAST = (((1,), (1,)), ((), ()))
VMEM = pl.BlockSpec(memory_space=pltpu.VMEM)
SMEM = pl.BlockSpec(memory_space=pltpu.SMEM)


def gelu_slope(pre_act):
    inner = 0.7978845608 * (pre_act + 0.044715 * pre_act * pre_act * pre_act)
    tanh_value = jnp.tanh(inner)
    return 0.5 * (1.0 + tanh_value) + 0.5 * pre_act * (
        1.0 - tanh_value * tanh_value
    ) * 0.7978845608 * (1.0 + 3.0 * 0.044715 * pre_act * pre_act)


def dot(left, right, dims=(((1,), (0,)), ((), ()))):
    return lax.dot_general(left, right, dims, preferred_element_type=F32)


def call(body, out_shape, in_specs, scratch=(), cost=(1e7, 1e6)):
    outs = jax.tree.map(lambda _: VMEM, out_shape)
    return pl.pallas_call(
        body,
        out_shape=out_shape,
        in_specs=in_specs,
        out_specs=outs,
        scratch_shapes=scratch,
        compiler_params=pltpu.CompilerParams(vmem_limit_bytes=32 * 2**20),
        cost_estimate=pl.CostEstimate(
            flops=int(cost[0]), bytes_accessed=int(cost[1]), transcendentals=0
        ),
    )


def places():
    blk = lax.axis_index("blk")
    return lax.rem(blk, GROUP), lax.rem(blk + GROUP // 2, GROUP)


def kind_of(distance):
    k = 2 * (jnp.abs(distance) - 1) + jnp.where(distance < 0, 1, 0)
    return jnp.clip(k, 0, 7)


def offset_of(kind):
    return (kind // 2 + 1) * (1 - 2 * lax.rem(kind, 2))


def inside(place):
    return jnp.logical_and(place >= 0, place < GROUP)


def bounded(place):
    return jnp.clip(place, 0, GROUP - 1)


def pack_kernel(width, x_ref, send_ref, a_ref, b_ref):
    place_a, place_b = places()
    cap = send_ref.shape[1]
    for ref, place in ((b_ref, place_b), (a_ref, place_a)):
        for peer in range(GROUP):
            kind = kind_of(peer - place)
            for m in range(cap):
                start = pl.multiple_of(send_ref[kind, m] * width, width)
                ref[peer, m] = x_ref[:, pl.ds(start, width)]


def column():
    col = lax.axis_index("col")
    return col // Z_HI, lax.rem(col, Z_HI)


def range_half():
    z = column()[1] * Z_LO + lax.rem(lax.axis_index("blk") // CORE, Z_LO)
    middle = jnp.logical_and(z >= Z_LO // 2, z < Z_LO // 2 * 3)
    return jnp.where(middle, 0, 1)


def split_kernel(width, x_ref, cot_ref, plus_ref, minus_ref):
    z_hi = column()[1]
    per = plus_ref.shape[2]
    for x in range(X):
        for out, h in ((plus_ref, z_hi), (minus_ref, 1 - z_hi)):
            for p in range(per):
                start = pl.multiple_of(((x * Z_HI + h) * per + p) * width, width)
                out[x, 0, p] = x_ref[:, pl.ds(start, width)]
                out[x, 1, p] = cot_ref[:, pl.ds(start, width)]


def join_kernel(xc_plus_ref, xc_minus_ref, agg_plus_ref, agg_minus_ref, out_ref):
    for side, (xc, agg) in enumerate(((xc_plus_ref, agg_plus_ref), (xc_minus_ref, agg_minus_ref))):
        for which in range(2):
            out_ref[:, which, side] = xc[:, which]
        out_ref[:, 2, side] = agg[...]


def join_back_kernel(plus_ref, minus_ref, out_ref):
    out_ref[:, 0] = plus_ref[...]
    out_ref[:, 1] = minus_ref[...]


def local_kernel(slots, chunk, x_ref, dst_ref, src_ref, cnt_ref, half_ref, acc_ref):
    step = pl.program_id(0)
    width = cnt_ref.shape[1]
    dim = x_ref.shape[0]
    half_ref[...] = cnt_ref[...].astype(F32).astype(BF16)

    @pl.when(step == 0)
    def _():
        acc_ref[...] = jnp.zeros_like(acc_ref)

    @pl.when(step * chunk >= slots)
    def _():
        ones = jnp.ones((16, width), BF16)
        for i in range(chunk):
            tile = step * chunk + i
            start = pl.multiple_of(src_ref[tile] * width, width)
            rows = jnp.concatenate([x_ref[:, pl.ds(start, width)], ones], axis=0)
            dst = dst_ref[tile]
            acc_ref[dst] += dot(rows, half_ref[i], LAST)[: dim + 8]


def aggregate_kernel(
    slots, a_ref, b_ref, dst_ref, src_ref, half_ref, acc_in, plus_ref, minus_ref, deg_ref, acc_ref
):
    place_a, place_b = places()
    z_hi = column()[1]
    cap, dim, width = a_ref.shape[1:]
    blocks = acc_in.shape[0]
    per = plus_ref.shape[1]
    ones = jnp.ones((16, width), BF16)
    acc_ref[...] = acc_in[...]
    for tile in range(slots):
        slot = src_ref[tile] - blocks
        kind = slot // cap
        m = lax.rem(slot, cap)
        row_a = place_a - offset_of(kind)
        row_b = place_b - offset_of(kind)
        got = jnp.where(inside(row_a), a_ref[bounded(row_a), m], b_ref[bounded(row_b), m])
        rows = jnp.concatenate([got, ones], axis=0)
        dst = dst_ref[tile]
        acc_ref[dst] += dot(rows, half_ref[tile], LAST)[: dim + 8]
    for block in range(blocks):
        deg_ref[block] = jnp.maximum(acc_ref[block, dim : dim + 8], 1.0)
    for x in range(X):
        for out, h in ((plus_ref, z_hi), (minus_ref, 1 - z_hi)):
            for p in range(per):
                block = (x * Z_HI + h) * per + p
                out[x, p] = (acc_ref[block, :dim] / deg_ref[block, :1]).astype(BF16)


def node_kernel(
    in_ref, wt_ref, neigh_ref, own_w_ref, bias_ref, plus_ref, minus_ref, dz_ref, xa_ref, cot_ref, home_ref
):
    _, _, sides, per_col, dim, width = in_ref.shape
    full = X * Z_HI * dim
    half = range_half()
    for x in range(X):
        for side, z in ((0, half), (1, 1 - half)):
            start = (x * Z_HI + z) * dim
            rows = pl.ds(pl.multiple_of(start, dim), dim)
            agg_rows = pl.ds(pl.multiple_of(full + start, dim), dim)
            for p in range(per_col):
                lanes = slice(p * width, (p + 1) * width)
                xa_ref[rows, lanes] = in_ref[x, 0, side, p]
                cot_ref[rows, lanes] = in_ref[x, 1, side, p]
                xa_ref[agg_rows, lanes] = in_ref[x, 2, side, p]
    for p in range(per_col):
        lanes = slice(p * width, (p + 1) * width)
        pre = dot(wt_ref[...], xa_ref[:, lanes]) + bias_ref[...]
        dz = (cot_ref[:, lanes].astype(F32) * gelu_slope(pre)).astype(BF16)
        dz_ref[:, lanes] = dz
        home_ref[0, :, lanes] = dot(neigh_ref[...], dz).astype(BF16)
        home_ref[1, :, lanes] = dot(own_w_ref[...], dz).astype(BF16)
    for x in range(X):
        for out, z in ((minus_ref, half), (plus_ref, 1 - half)):
            rows = pl.ds(pl.multiple_of((x * Z_HI + z) * dim, dim), dim)
            for which in range(2):
                for p in range(per_col):
                    out[x, which, p] = home_ref[which, rows, p * width : (p + 1) * width]


def weight_kernel(dim, xa_ref, dz_ref, part_ref):
    full = dz_ref.shape[0]
    grads = dot(xa_ref[...], dz_ref[...], LAST)
    total = dot(jnp.ones((16, dz_ref.shape[1]), BF16), dz_ref[...], LAST)
    tail = jnp.concatenate([total[:8, :128], total[8:, 128:]], axis=0).astype(BF16)
    for which in range(2):
        for quarter in range(4):
            for x in range(X):
                rows = [
                    grads[start : start + 8]
                    for z in range(Z_HI)
                    for start in [which * full + (x * Z_HI + z) * dim + quarter * 8]
                ]
                piece = (which * 4 + quarter) * X + x
                part_ref[piece, :, :full] = jnp.concatenate(rows, axis=0).astype(BF16)
                part_ref[piece, :, full:] = tail


def contribution_kernel(
    slots, home_ref, deg_ref, dst_ref, src_ref, half_ref, b_ref, scaled_ref, *rest
):
    near_refs, hold_ref = rest[:-1], rest[-1]
    place_a, place_b = places()
    z_hi = column()[1]
    blocks = scaled_ref.shape[0]
    cap = b_ref.shape[1]
    per = home_ref.shape[3]
    for x in range(X):
        for side, h in ((0, 1 - z_hi), (1, z_hi)):
            for p in range(per):
                block = (x * Z_HI + h) * per + p
                value = home_ref[x, side, 0, p].astype(F32) / deg_ref[block, :1]
                scaled_ref[block] = value.astype(BF16)
    for tile in range(slots):
        value = dot(scaled_ref[dst_ref[tile]], half_ref[tile])
        hold_ref[src_ref[tile] - blocks] = value.astype(BF16)
    for peer in range(GROUP):
        kind = kind_of(place_b - peer)
        for m in range(cap):
            b_ref[peer, m] = hold_ref[kind * cap + m]
    for flip, ref in enumerate(near_refs, start=1):
        kind = kind_of(place_a - jnp.bitwise_xor(place_a, flip))
        for m in range(cap):
            ref[m] = hold_ref[kind * cap + m]


def local_back_kernel(slots, scaled_ref, home_ref, dst_ref, src_ref, half_ref, acc_ref):
    z_hi = column()[1]
    per = home_ref.shape[3]
    for x in range(X):
        for side, h in ((0, 1 - z_hi), (1, z_hi)):
            for p in range(per):
                acc_ref[(x * Z_HI + h) * per + p] = home_ref[x, side, 1, p].astype(F32)
    for tile in range(slots, half_ref.shape[0]):
        acc_ref[src_ref[tile]] += dot(scaled_ref[dst_ref[tile]], half_ref[tile])


def finish_kernel(acc_in, b_ref, send_ref, *rest):
    near_refs, (out_ref, acc_ref) = rest[:-2], rest[-2:]
    place_a, place_b = places()
    kinds, cap = send_ref.shape
    width = acc_in.shape[2]
    acc_ref[...] = acc_in[...]
    for kind in range(kinds):
        offset = (kind // 2 + 1) * (1 - 2 * (kind % 2))
        away = jnp.logical_not(inside(place_a + offset))
        row_b = bounded(place_b + offset)
        for m in range(cap):
            got = jnp.where(away, b_ref[row_b, m].astype(F32), 0.0)
            acc_ref[send_ref[kind, m]] += got
    for flip, ref in enumerate(near_refs, start=1):
        offset = jnp.bitwise_xor(place_a, flip) - place_a
        used = jnp.abs(offset) <= kinds // 2
        kind = kind_of(offset)
        for m in range(cap):
            acc_ref[send_ref[kind, m]] += jnp.where(used, ref[m].astype(F32), 0.0)
    for block in range(acc_ref.shape[0]):
        out_ref[:, block * width : (block + 1) * width] = acc_ref[block].astype(BF16)


def rank(y, z_lo, core, x, z_hi):
    return ((y * Z_LO + z_lo) * CORE + core) * X * Z_HI + x * Z_HI + z_hi


def swap(rows, shift):
    devices = lax.axis_size("blk")
    groups = [
        [(first + shift + i) % devices for i in range(GROUP)] for first in range(0, devices, GROUP)
    ]
    return lax.all_to_all(rows, "blk", 0, 0, axis_index_groups=groups, tiled=False)


def flipped(rows, flip):
    route = [
        (e, e ^ flip)
        for e in range(lax.axis_size("blk"))
        if abs((e ^ flip) - e) <= GROUP // 2
    ]
    return lax.ppermute(rows, "blk", route)


def over_x(rows):
    groups = [[x * Z_HI + h for x in range(X)] for h in range(Z_HI)]
    return lax.all_to_all(rows, "col", 0, 0, axis_index_groups=groups, tiled=False)


def along_z(rows, step):
    chips = Z_LO * Z_HI
    route = []
    for y in range(Y):
        for core in range(CORE):
            for x in range(X):
                for z in range(chips):
                    to = (z + step) % chips
                    route.append(
                        (
                            rank(y, z % Z_LO, core, x, z // Z_LO),
                            rank(y, to % Z_LO, core, x, to // Z_LO),
                        )
                    )
    return lax.ppermute(rows, ("blk", "col"), sorted(route))


def per_device(
    node_feats, tile_dst, tile_src, tile_cnt, send_blk, self_weight, neigh_weight, bias, cotangent
):
    dim, nodes = node_feats.shape
    tiles, width = tile_cnt.shape[:2]
    blocks = nodes // width
    table = send_blk[0]
    kinds, cap = table.shape
    slots = kinds * cap
    cols = X * Z_HI
    per_col = blocks // cols
    full = cols * dim
    chunk = 8
    shape = lambda *dims: jax.ShapeDtypeStruct(dims + (dim, width), BF16)
    halo = shape(GROUP, cap)
    step = Z_LO // 2

    send_a, send_b = call(
        functools.partial(pack_kernel, width), (halo, halo), [VMEM, SMEM]
    )(node_feats, table)
    got_b = swap(send_b, GROUP // 2)
    xc_plus, xc_minus = call(
        functools.partial(split_kernel, width), (shape(X, 2, per_col),) * 2, [VMEM] * 2
    )(node_feats, cotangent)
    whole = lambda shape: pl.BlockSpec(shape, lambda i: (0,) * len(shape))
    half, acc = pl.pallas_call(
        functools.partial(local_kernel, slots, chunk),
        grid=(tiles // chunk,),
        out_shape=(
            jax.ShapeDtypeStruct(tile_cnt.shape, BF16),
            jax.ShapeDtypeStruct((blocks, dim + 8, width), F32),
        ),
        in_specs=[
            whole((dim, nodes)),
            SMEM,
            SMEM,
            pl.BlockSpec((chunk, width, width), lambda i: (i, 0, 0)),
        ],
        out_specs=(
            pl.BlockSpec((chunk, width, width), lambda i: (i, 0, 0)),
            whole((blocks, dim + 8, width)),
        ),
        compiler_params=pltpu.CompilerParams(vmem_limit_bytes=32 * 2**20),
        cost_estimate=pl.CostEstimate(
            flops=60000000, bytes_accessed=6000000, transcendentals=0
        ),
    )(node_feats, tile_dst, tile_src, tile_cnt)
    send_a, got_b, xc_plus, xc_minus, half, acc = lax.optimization_barrier(
        (send_a, got_b, xc_plus, xc_minus, half, acc)
    )
    xc_plus = along_z(xc_plus, step)
    xc_minus = along_z(xc_minus, -step)
    got_a = swap(send_a, 0)
    weight_t = jnp.concatenate([self_weight.T, neigh_weight.T], axis=1)
    bias_col = bias[:, None]
    agg_plus, agg_minus, degree = call(
        functools.partial(aggregate_kernel, slots),
        (shape(X, per_col), shape(X, per_col), jax.ShapeDtypeStruct((blocks, 8, width), F32)),
        [VMEM, VMEM, SMEM, SMEM, VMEM, VMEM],
        [pltpu.VMEM((blocks, dim + 8, width), F32)],
    )(got_a, got_b, tile_dst, tile_src, half, acc)
    agg_plus = along_z(agg_plus, step)
    agg_minus = along_z(agg_minus, -step)
    ranged = call(join_kernel, shape(X, 3, 2, per_col), [VMEM] * 4)(
        xc_plus, xc_minus, agg_plus, agg_minus
    )
    ranged = over_x(ranged)
    plus, minus, dz, xa = call(
        node_kernel,
        (
            shape(X, 2, per_col),
            shape(X, 2, per_col),
            jax.ShapeDtypeStruct((full, per_col * width), BF16),
            jax.ShapeDtypeStruct((2 * full, per_col * width), BF16),
        ),
        [VMEM] * 5,
        [
            pltpu.VMEM((full, per_col * width), BF16),
            pltpu.VMEM((2, full, per_col * width), BF16),
        ],
    )(ranged, weight_t, neigh_weight, self_weight, bias_col)
    plus = along_z(plus, step)
    minus = along_z(minus, -step)
    part = call(
        functools.partial(weight_kernel, dim),
        jax.ShapeDtypeStruct((Y * CORE * X, 16, full + 128), BF16),
        [VMEM] * 2,
    )(xa, dz)

    both = ("blk", "col")
    flat = [
        [rank(y, l, c, x, h) for y in range(Y) for c in range(CORE) for x in range(X)]
        for l in range(Z_LO)
        for h in range(Z_HI)
    ]
    line = [
        [rank(y, l, c, x, h) for h in range(Z_HI) for l in range(Z_LO)]
        for y in range(Y)
        for c in range(CORE)
        for x in range(X)
    ]
    plane = [[(y * Z_LO + l) * CORE + c for y in range(Y) for c in range(CORE)] for l in range(Z_LO)]
    part = lax.all_to_all(part, both, 0, 0, axis_index_groups=flat, tiled=False)
    home = call(join_back_kernel, shape(X, 2, 2, per_col), [VMEM] * 2)(plus, minus)
    home, part = lax.optimization_barrier((home, part))
    home = over_x(home)
    away_b, scaled, *near = call(
        functools.partial(contribution_kernel, slots),
        (halo, shape(blocks)) + (shape(cap),) * (GROUP - 1),
        [VMEM, VMEM, SMEM, SMEM, VMEM],
        [pltpu.VMEM((slots, dim, width), BF16)],
    )(home, degree, tile_dst, tile_src, half)
    back_b = swap(away_b, GROUP // 2)
    near = [flipped(rows, flip) for flip, rows in enumerate(near, start=1)]
    part = jnp.sum(part.astype(F32), axis=0)
    tail = jnp.concatenate([part[0:4, full:], part[8:12, full:]], axis=0)
    ends = [jnp.concatenate([part[8 * h : 8 * h + 8, :full], tail], axis=1) for h in range(Z_HI)]
    part = jnp.broadcast_to(jnp.stack(ends)[:, None], (Z_HI, Z_LO, 8, full + 128))
    part = part.reshape(Z_HI * Z_LO, 8, full + 128).astype(BF16)
    part, back_b = lax.optimization_barrier((part, back_b))
    part = lax.all_to_all(part, both, 0, 0, axis_index_groups=line, tiled=False)
    part = jnp.sum(part.astype(F32), axis=0)
    grad_bias = jnp.concatenate([part[0, full:], part[4, full:]])
    grad_bias = lax.dynamic_slice_in_dim(grad_bias, lax.axis_index("col") * dim, dim, 0)
    part = jnp.broadcast_to(part[None, :, :full].astype(BF16), (Y * CORE, 8, full))
    part = lax.all_to_all(part, "blk", 0, 0, axis_index_groups=plane, tiled=False)
    part = part.astype(F32).reshape(2, dim, full)
    grad_self, grad_neigh = part[0], part[1]
    acc = call(
        functools.partial(local_back_kernel, slots),
        jax.ShapeDtypeStruct((blocks, dim, width), F32),
        [VMEM, VMEM, SMEM, SMEM, VMEM],
    )(scaled, home, tile_dst, tile_src, half)
    grad_feats = call(
        finish_kernel,
        jax.ShapeDtypeStruct((dim, nodes), BF16),
        [VMEM, VMEM, SMEM] + [VMEM] * (GROUP - 1),
        [pltpu.VMEM((blocks, dim, width), F32)],
    )(acc, back_b, table, *near)
    return grad_feats, grad_self, grad_neigh, grad_bias


def solution(mesh):
    placed = (
        P("col", "blk"),
        P("blk"),
        P("blk"),
        P("blk", None, None),
        P("blk", None, None),
        P(),
        P(),
        P(),
        P("col", "blk"),
    )
    return jax.shard_map(
        per_device,
        mesh=mesh,
        in_specs=placed,
        out_specs=(P("col", "blk"), P("col", None), P("col", None), P("col")),
        check_vma=False,
    )
```

```python
import functools

import jax
import jax.numpy as jnp
from jax import lax
from jax.experimental import pallas as pl
from jax.experimental.pallas import tpu as pltpu
from jax.sharding import PartitionSpec as P

GROUP = 8
Y, Z_LO, CORE, X, Z_HI = 4, 8, 2, 4, 2
BF16 = jnp.bfloat16
F32 = jnp.float32
FIRST = (((0,), (0,)), ((), ()))
LAST = (((1,), (1,)), ((), ()))
VMEM = pl.BlockSpec(memory_space=pltpu.VMEM)
SMEM = pl.BlockSpec(memory_space=pltpu.SMEM)


def gelu_slope(pre_act):
    inner = 0.7978845608 * (pre_act + 0.044715 * pre_act * pre_act * pre_act)
    tanh_value = jnp.tanh(inner)
    return 0.5 * (1.0 + tanh_value) + 0.5 * pre_act * (
        1.0 - tanh_value * tanh_value
    ) * 0.7978845608 * (1.0 + 3.0 * 0.044715 * pre_act * pre_act)


def dot(left, right, dims=(((1,), (0,)), ((), ()))):
    return lax.dot_general(left, right, dims, preferred_element_type=F32)


def call(body, out_shape, in_specs, scratch=(), cost=(1e7, 1e6)):
    outs = jax.tree.map(lambda _: VMEM, out_shape)
    return pl.pallas_call(
        body,
        out_shape=out_shape,
        in_specs=in_specs,
        out_specs=outs,
        scratch_shapes=scratch,
        compiler_params=pltpu.CompilerParams(vmem_limit_bytes=32 * 2**20),
        cost_estimate=pl.CostEstimate(
            flops=int(cost[0]), bytes_accessed=int(cost[1]), transcendentals=0
        ),
    )


def places():
    blk = lax.axis_index("blk")
    return lax.rem(blk, GROUP), lax.rem(blk + GROUP // 2, GROUP)


def kind_of(distance):
    k = 2 * (jnp.abs(distance) - 1) + jnp.where(distance < 0, 1, 0)
    return jnp.clip(k, 0, 7)


def offset_of(kind):
    return (kind // 2 + 1) * (1 - 2 * lax.rem(kind, 2))


def inside(place):
    return jnp.logical_and(place >= 0, place < GROUP)


def bounded(place):
    return jnp.clip(place, 0, GROUP - 1)


def pack_kernel(width, x_ref, send_ref, a_ref, b_ref):
    place_a, place_b = places()
    cap = send_ref.shape[1]
    for ref, place in ((b_ref, place_b), (a_ref, place_a)):
        for peer in range(GROUP):
            kind = kind_of(peer - place)
            for m in range(cap):
                start = pl.multiple_of(send_ref[kind, m] * width, width)
                ref[peer, m] = x_ref[:, pl.ds(start, width)]


def column():
    col = lax.axis_index("col")
    return col // Z_HI, lax.rem(col, Z_HI)


def range_half():
    z = column()[1] * Z_LO + lax.rem(lax.axis_index("blk") // CORE, Z_LO)
    middle = jnp.logical_and(z >= Z_LO // 2, z < Z_LO // 2 * 3)
    return jnp.where(middle, 0, 1)


def split_kernel(width, x_ref, cot_ref, plus_ref, minus_ref):
    z_hi = column()[1]
    per = plus_ref.shape[2]
    for x in range(X):
        for out, h in ((plus_ref, z_hi), (minus_ref, 1 - z_hi)):
            for p in range(per):
                start = pl.multiple_of(((x * Z_HI + h) * per + p) * width, width)
                out[x, 0, p] = x_ref[:, pl.ds(start, width)]
                out[x, 1, p] = cot_ref[:, pl.ds(start, width)]


def join_kernel(xc_plus_ref, xc_minus_ref, agg_plus_ref, agg_minus_ref, out_ref):
    for side, (xc, agg) in enumerate(((xc_plus_ref, agg_plus_ref), (xc_minus_ref, agg_minus_ref))):
        for which in range(2):
            out_ref[:, which, side] = xc[:, which]
        out_ref[:, 2, side] = agg[...]


def turn_kernel(plus_ref, minus_ref, *outs):
    x = column()[0]
    for step, out in enumerate(outs):
        to = lax.rem(x + step, X)
        out[0] = plus_ref[to]
        out[1] = minus_ref[to]


def fold_kernel(part_ref, out_ref):
    full = part_ref.shape[2] - 128
    total = part_ref[0].astype(F32)
    for i in range(1, part_ref.shape[0]):
        total += part_ref[i].astype(F32)
    total = total.astype(BF16)
    tail = jnp.concatenate([total[0:4, full:], total[8:12, full:]], axis=0)
    for z in range(Z_HI * Z_LO):
        first = z // Z_LO * 8
        out_ref[z, :, :full] = total[first : first + 8, :full]
        out_ref[z, :, full:] = tail


def gather_kernel(part_ref, out_ref, tail_ref):
    full = part_ref.shape[2] - 128
    total = part_ref[0].astype(F32)
    for i in range(1, part_ref.shape[0]):
        total += part_ref[i].astype(F32)
    tail_ref[...] = total[:, full:]
    for i in range(out_ref.shape[0]):
        out_ref[i] = total[:, :full].astype(BF16)


def local_kernel(slots, chunk, x_ref, dst_ref, src_ref, cnt_ref, half_ref, acc_ref):
    step = pl.program_id(0)
    width = cnt_ref.shape[1]
    dim = x_ref.shape[0]
    half_ref[...] = cnt_ref[...].astype(F32).astype(BF16)

    @pl.when(step == 0)
    def _():
        acc_ref[...] = jnp.zeros_like(acc_ref)

    @pl.when(step * chunk >= slots)
    def _():
        ones = jnp.ones((16, width), BF16)
        for i in range(chunk):
            tile = step * chunk + i
            start = pl.multiple_of(src_ref[tile] * width, width)
            rows = jnp.concatenate([x_ref[:, pl.ds(start, width)], ones], axis=0)
            dst = dst_ref[tile]
            acc_ref[dst] += dot(rows, half_ref[i], LAST)[: dim + 8]


def aggregate_kernel(
    slots, a_ref, b_ref, dst_ref, src_ref, half_ref, acc_in, plus_ref, minus_ref, deg_ref, acc_ref
):
    place_a, place_b = places()
    z_hi = column()[1]
    cap, dim, width = a_ref.shape[1:]
    blocks = acc_in.shape[0]
    per = plus_ref.shape[1]
    ones = jnp.ones((16, width), BF16)
    acc_ref[...] = acc_in[...]
    for tile in range(slots):
        slot = src_ref[tile] - blocks
        kind = slot // cap
        m = lax.rem(slot, cap)
        row_a = place_a - offset_of(kind)
        row_b = place_b - offset_of(kind)
        got = jnp.where(inside(row_a), a_ref[bounded(row_a), m], b_ref[bounded(row_b), m])
        rows = jnp.concatenate([got, ones], axis=0)
        dst = dst_ref[tile]
        acc_ref[dst] += dot(rows, half_ref[tile], LAST)[: dim + 8]
    for block in range(blocks):
        deg_ref[block] = jnp.maximum(acc_ref[block, dim : dim + 8], 1.0)
    for x in range(X):
        for out, h in ((plus_ref, z_hi), (minus_ref, 1 - z_hi)):
            for p in range(per):
                block = (x * Z_HI + h) * per + p
                out[x, p] = (acc_ref[block, :dim] / deg_ref[block, :1]).astype(BF16)


def node_kernel(
    in_ref, wt_ref, neigh_ref, own_w_ref, bias_ref, plus_ref, minus_ref, dz_ref, xa_ref, cot_ref, home_ref
):
    _, _, sides, per_col, dim, width = in_ref.shape
    full = X * Z_HI * dim
    half = range_half()
    for x in range(X):
        for side, z in ((0, half), (1, 1 - half)):
            start = (x * Z_HI + z) * dim
            rows = pl.ds(pl.multiple_of(start, dim), dim)
            agg_rows = pl.ds(pl.multiple_of(full + start, dim), dim)
            for p in range(per_col):
                lanes = slice(p * width, (p + 1) * width)
                xa_ref[rows, lanes] = in_ref[x, 0, side, p]
                cot_ref[rows, lanes] = in_ref[x, 1, side, p]
                xa_ref[agg_rows, lanes] = in_ref[x, 2, side, p]
    for p in range(per_col):
        lanes = slice(p * width, (p + 1) * width)
        pre = dot(wt_ref[...], xa_ref[:, lanes]) + bias_ref[...]
        dz = (cot_ref[:, lanes].astype(F32) * gelu_slope(pre)).astype(BF16)
        dz_ref[:, lanes] = dz
        home_ref[0, :, lanes] = dot(neigh_ref[...], dz).astype(BF16)
        home_ref[1, :, lanes] = dot(own_w_ref[...], dz).astype(BF16)
    for x in range(X):
        for out, z in ((minus_ref, half), (plus_ref, 1 - half)):
            rows = pl.ds(pl.multiple_of((x * Z_HI + z) * dim, dim), dim)
            for which in range(2):
                for p in range(per_col):
                    out[x, which, p] = home_ref[which, rows, p * width : (p + 1) * width]


def weight_kernel(dim, xa_ref, dz_ref, part_ref):
    full = dz_ref.shape[0]
    grads = dot(xa_ref[...], dz_ref[...], LAST)
    total = dot(jnp.ones((16, dz_ref.shape[1]), BF16), dz_ref[...], LAST)
    tail = jnp.concatenate([total[:8, :128], total[8:, 128:]], axis=0).astype(BF16)
    for which in range(2):
        for quarter in range(4):
            for x in range(X):
                rows = [
                    grads[start : start + 8]
                    for z in range(Z_HI)
                    for start in [which * full + (x * Z_HI + z) * dim + quarter * 8]
                ]
                piece = (which * 4 + quarter) * X + x
                part_ref[piece, :, :full] = jnp.concatenate(rows, axis=0).astype(BF16)
                part_ref[piece, :, full:] = tail


def home_pieces(refs, which):
    x, z_hi = column()
    per = refs[0].shape[2]
    for step, ref in enumerate(refs):
        source = lax.rem(x + X - step, X)
        for side, h in ((0, 1 - z_hi), (1, z_hi)):
            for p in range(per):
                yield (source * Z_HI + h) * per + p, ref[side, which, p]


def contribution_kernel(
    slots, zero_ref, one_ref, two_ref, three_ref, deg_ref, dst_ref, src_ref, half_ref, *outs
):
    a_ref, b_ref, scaled_ref, hold_ref = outs
    place_a, place_b = places()
    blocks = scaled_ref.shape[0]
    cap = a_ref.shape[1]
    for block, piece in home_pieces((zero_ref, one_ref, two_ref, three_ref), 0):
        scaled_ref[block] = (piece.astype(F32) / deg_ref[block][:1]).astype(BF16)
    for tile in range(slots):
        value = dot(scaled_ref[dst_ref[tile]], half_ref[tile])
        hold_ref[src_ref[tile] - blocks] = value.astype(BF16)
    for ref, place in ((b_ref, place_b), (a_ref, place_a)):
        for peer in range(GROUP):
            kind = kind_of(place - peer)
            for m in range(cap):
                ref[peer, m] = hold_ref[kind * cap + m]


def local_back_kernel(
    slots, zero_ref, one_ref, two_ref, three_ref, scaled_ref, dst_ref, src_ref, half_ref, acc_ref
):
    for block, piece in home_pieces((zero_ref, one_ref, two_ref, three_ref), 1):
        acc_ref[block] = piece.astype(F32)
    for tile in range(slots, half_ref.shape[0]):
        acc_ref[src_ref[tile]] += dot(scaled_ref[dst_ref[tile]], half_ref[tile])


def finish_kernel(acc_in, a_ref, b_ref, send_ref, out_ref, acc_ref):
    place_a, place_b = places()
    kinds, cap = send_ref.shape
    width = acc_in.shape[2]
    acc_ref[...] = acc_in[...]
    for kind in range(kinds):
        offset = (kind // 2 + 1) * (1 - 2 * (kind % 2))
        row_a = place_a + offset
        row_b = place_b + offset
        for m in range(cap):
            got = jnp.where(inside(row_a), a_ref[bounded(row_a), m], b_ref[bounded(row_b), m])
            acc_ref[send_ref[kind, m]] += got.astype(F32)
    for block in range(acc_ref.shape[0]):
        out_ref[:, block * width : (block + 1) * width] = acc_ref[block].astype(BF16)


def rank(y, z_lo, core, x, z_hi):
    return ((y * Z_LO + z_lo) * CORE + core) * X * Z_HI + x * Z_HI + z_hi


def swap(rows, shift):
    devices = lax.axis_size("blk")
    groups = [
        [(first + shift + i) % devices for i in range(GROUP)] for first in range(0, devices, GROUP)
    ]
    return lax.all_to_all(rows, "blk", 0, 0, axis_index_groups=groups, tiled=False)


def over_x(rows):
    groups = [[x * Z_HI + h for x in range(X)] for h in range(Z_HI)]
    return lax.all_to_all(rows, "col", 0, 0, axis_index_groups=groups, tiled=False)


def along_z(rows, step):
    chips = Z_LO * Z_HI
    route = []
    for y in range(Y):
        for core in range(CORE):
            for x in range(X):
                for z in range(chips):
                    to = (z + step) % chips
                    route.append(
                        (
                            rank(y, z % Z_LO, core, x, z // Z_LO),
                            rank(y, to % Z_LO, core, x, to // Z_LO),
                        )
                    )
    return lax.ppermute(rows, ("blk", "col"), sorted(route))


def per_device(
    node_feats, tile_dst, tile_src, tile_cnt, send_blk, self_weight, neigh_weight, bias, cotangent
):
    dim, nodes = node_feats.shape
    tiles, width = tile_cnt.shape[:2]
    blocks = nodes // width
    table = send_blk[0]
    kinds, cap = table.shape
    slots = kinds * cap
    cols = X * Z_HI
    per_col = blocks // cols
    full = cols * dim
    chunk = 8
    shape = lambda *dims: jax.ShapeDtypeStruct(dims + (dim, width), BF16)
    halo = shape(GROUP, cap)
    step = Z_LO // 2

    send_a, send_b = call(
        functools.partial(pack_kernel, width), (halo, halo), [VMEM, SMEM]
    )(node_feats, table)
    got_b = swap(send_b, GROUP // 2)
    xc_plus, xc_minus = call(
        functools.partial(split_kernel, width), (shape(X, 2, per_col),) * 2, [VMEM] * 2
    )(node_feats, cotangent)
    whole = lambda shape: pl.BlockSpec(shape, lambda i: (0,) * len(shape))
    half, acc = pl.pallas_call(
        functools.partial(local_kernel, slots, chunk),
        grid=(tiles // chunk,),
        out_shape=(
            jax.ShapeDtypeStruct(tile_cnt.shape, BF16),
            jax.ShapeDtypeStruct((blocks, dim + 8, width), F32),
        ),
        in_specs=[
            whole((dim, nodes)),
            SMEM,
            SMEM,
            pl.BlockSpec((chunk, width, width), lambda i: (i, 0, 0)),
        ],
        out_specs=(
            pl.BlockSpec((chunk, width, width), lambda i: (i, 0, 0)),
            whole((blocks, dim + 8, width)),
        ),
        compiler_params=pltpu.CompilerParams(vmem_limit_bytes=32 * 2**20),
        cost_estimate=pl.CostEstimate(
            flops=60000000, bytes_accessed=6000000, transcendentals=0
        ),
    )(node_feats, tile_dst, tile_src, tile_cnt)
    send_a, got_b, xc_plus, xc_minus, half, acc = lax.optimization_barrier(
        (send_a, got_b, xc_plus, xc_minus, half, acc)
    )
    xc_plus = along_z(xc_plus, step)
    xc_minus = along_z(xc_minus, -step)
    got_a = swap(send_a, 0)
    weight_t = jnp.concatenate([self_weight.T, neigh_weight.T], axis=1)
    bias_col = bias[:, None]
    agg_plus, agg_minus, degree = call(
        functools.partial(aggregate_kernel, slots),
        (shape(X, per_col), shape(X, per_col), jax.ShapeDtypeStruct((blocks, 8, width), F32)),
        [VMEM, VMEM, SMEM, SMEM, VMEM, VMEM],
        [pltpu.VMEM((blocks, dim + 8, width), F32)],
    )(got_a, got_b, tile_dst, tile_src, half, acc)
    agg_plus = along_z(agg_plus, step)
    agg_minus = along_z(agg_minus, -step)
    ranged = call(join_kernel, shape(X, 3, 2, per_col), [VMEM] * 4)(
        xc_plus, xc_minus, agg_plus, agg_minus
    )
    ranged = over_x(ranged)
    plus, minus, dz, xa = call(
        node_kernel,
        (
            shape(X, 2, per_col),
            shape(X, 2, per_col),
            jax.ShapeDtypeStruct((full, per_col * width), BF16),
            jax.ShapeDtypeStruct((2 * full, per_col * width), BF16),
        ),
        [VMEM] * 5,
        [
            pltpu.VMEM((full, per_col * width), BF16),
            pltpu.VMEM((2, full, per_col * width), BF16),
        ],
    )(ranged, weight_t, neigh_weight, self_weight, bias_col)
    plus = along_z(plus, step)
    minus = along_z(minus, -step)
    part = call(
        functools.partial(weight_kernel, dim),
        jax.ShapeDtypeStruct((Y * CORE * X, 16, full + 128), BF16),
        [VMEM] * 2,
    )(xa, dz)

    both = ("blk", "col")
    flat = [
        [rank(y, l, c, x, h) for y in range(Y) for c in range(CORE) for x in range(X)]
        for l in range(Z_LO)
        for h in range(Z_HI)
    ]
    line = [
        [rank(y, l, c, x, h) for h in range(Z_HI) for l in range(Z_LO)]
        for y in range(Y)
        for c in range(CORE)
        for x in range(X)
    ]
    plane = [[(y * Z_LO + l) * CORE + c for y in range(Y) for c in range(CORE)] for l in range(Z_LO)]
    part = lax.all_to_all(part, both, 0, 0, axis_index_groups=flat, tiled=False)
    (part,) = call(
        fold_kernel, (jax.ShapeDtypeStruct((Z_HI * Z_LO, 8, full + 128), BF16),), [VMEM]
    )(part)
    part, plus, minus = lax.optimization_barrier((part, plus, minus))
    part = lax.all_to_all(part, both, 0, 0, axis_index_groups=line, tiled=False)
    home = call(turn_kernel, (shape(2, 2, per_col),) * X, [VMEM] * 2)(plus, minus)
    route = lambda turn: [(c, (c + Z_HI * turn) % cols) for c in range(cols)]
    home = [home[0]] + [lax.ppermute(home[turn], "col", route(turn)) for turn in range(1, X)]
    away_a, away_b, scaled = call(
        functools.partial(contribution_kernel, slots),
        (halo, halo, shape(blocks)),
        [VMEM] * 5 + [SMEM, SMEM, VMEM],
        [pltpu.VMEM((slots, dim, width), BF16)],
    )(*home, degree, tile_dst, tile_src, half)
    away_b, part = lax.optimization_barrier((away_b, part))
    back_b = swap(away_b, GROUP // 2)
    away_a, back_b = lax.optimization_barrier((away_a, back_b))
    back_a = swap(away_a, 0)
    part, tail = call(
        gather_kernel,
        (
            jax.ShapeDtypeStruct((Y * CORE, 8, full), BF16),
            jax.ShapeDtypeStruct((8, 128), F32),
        ),
        [VMEM],
    )(part)
    grad_bias = jnp.concatenate([tail[0], tail[4]])
    grad_bias = lax.dynamic_slice_in_dim(grad_bias, lax.axis_index("col") * dim, dim, 0)
    part, back_a = lax.optimization_barrier((part, back_a))
    part = lax.all_to_all(part, "blk", 0, 0, axis_index_groups=plane, tiled=False)
    part = part.astype(F32).reshape(2, dim, full)
    grad_self, grad_neigh = part[0], part[1]
    acc = call(
        functools.partial(local_back_kernel, slots),
        jax.ShapeDtypeStruct((blocks, dim, width), F32),
        [VMEM] * 5 + [SMEM, SMEM, VMEM],
    )(*home, scaled, tile_dst, tile_src, half)
    grad_feats = call(
        finish_kernel,
        jax.ShapeDtypeStruct((dim, nodes), BF16),
        [VMEM, VMEM, VMEM, SMEM],
        [pltpu.VMEM((blocks, dim, width), F32)],
    )(acc, back_a, back_b, table)
    return grad_feats, grad_self, grad_neigh, grad_bias


def solution(mesh):
    placed = (
        P("col", "blk"),
        P("blk"),
        P("blk"),
        P("blk", None, None),
        P("blk", None, None),
        P(),
        P(),
        P(),
        P("col", "blk"),
    )
    return jax.shard_map(
        per_device,
        mesh=mesh,
        in_specs=placed,
        out_specs=(P("col", "blk"), P("col", None), P("col", None), P("col")),
        check_vma=False,
    )
```

```python
import functools

import jax
import jax.numpy as jnp
from jax import lax
from jax.experimental import pallas as pl
from jax.experimental.pallas import tpu as pltpu
from jax.sharding import PartitionSpec as P

GROUP = 8
Y, Z_LO, CORE, X, Z_HI = 4, 8, 2, 4, 2
BF16 = jnp.bfloat16
F32 = jnp.float32
FIRST = (((0,), (0,)), ((), ()))
LAST = (((1,), (1,)), ((), ()))
VMEM = pl.BlockSpec(memory_space=pltpu.VMEM)
SMEM = pl.BlockSpec(memory_space=pltpu.SMEM)


def gelu_slope(pre_act):
    inner = 0.7978845608 * (pre_act + 0.044715 * pre_act * pre_act * pre_act)
    tanh_value = jnp.tanh(inner)
    return 0.5 * (1.0 + tanh_value) + 0.5 * pre_act * (
        1.0 - tanh_value * tanh_value
    ) * 0.7978845608 * (1.0 + 3.0 * 0.044715 * pre_act * pre_act)


def dot(left, right, dims=(((1,), (0,)), ((), ()))):
    return lax.dot_general(left, right, dims, preferred_element_type=F32)


def call(body, out_shape, in_specs, scratch=(), cost=(1e7, 1e6)):
    outs = jax.tree.map(lambda _: VMEM, out_shape)
    return pl.pallas_call(
        body,
        out_shape=out_shape,
        in_specs=in_specs,
        out_specs=outs,
        scratch_shapes=scratch,
        compiler_params=pltpu.CompilerParams(vmem_limit_bytes=32 * 2**20),
        cost_estimate=pl.CostEstimate(
            flops=int(cost[0]), bytes_accessed=int(cost[1]), transcendentals=0
        ),
    )


def places():
    blk = lax.axis_index("blk")
    return lax.rem(blk, GROUP), lax.rem(blk + GROUP // 2, GROUP)


def kind_of(distance):
    k = 2 * (jnp.abs(distance) - 1) + jnp.where(distance < 0, 1, 0)
    return jnp.clip(k, 0, 7)


def offset_of(kind):
    return (kind // 2 + 1) * (1 - 2 * lax.rem(kind, 2))


def inside(place):
    return jnp.logical_and(place >= 0, place < GROUP)


def bounded(place):
    return jnp.clip(place, 0, GROUP - 1)


def pack_kernel(width, x_ref, send_ref, a_ref, b_ref):
    place_a, place_b = places()
    cap = send_ref.shape[1]
    for ref, place in ((b_ref, place_b), (a_ref, place_a)):
        for peer in range(GROUP):
            kind = kind_of(peer - place)
            for m in range(cap):
                start = pl.multiple_of(send_ref[kind, m] * width, width)
                ref[peer, m] = x_ref[:, pl.ds(start, width)]


def column():
    col = lax.axis_index("col")
    return col // Z_HI, lax.rem(col, Z_HI)


def range_half():
    z = column()[1] * Z_LO + lax.rem(lax.axis_index("blk") // CORE, Z_LO)
    middle = jnp.logical_and(z >= Z_LO // 2, z < Z_LO // 2 * 3)
    return jnp.where(middle, 0, 1)


def split_kernel(width, x_ref, cot_ref, plus_ref, minus_ref):
    z_hi = column()[1]
    per = plus_ref.shape[2]
    for x in range(X):
        for out, h in ((plus_ref, z_hi), (minus_ref, 1 - z_hi)):
            for p in range(per):
                start = pl.multiple_of(((x * Z_HI + h) * per + p) * width, width)
                out[x, 0, p] = x_ref[:, pl.ds(start, width)]
                out[x, 1, p] = cot_ref[:, pl.ds(start, width)]


def join_kernel(xc_plus_ref, xc_minus_ref, agg_plus_ref, agg_minus_ref, out_ref):
    for side, (xc, agg) in enumerate(((xc_plus_ref, agg_plus_ref), (xc_minus_ref, agg_minus_ref))):
        for which in range(2):
            out_ref[:, which, side] = xc[:, which]
        out_ref[:, 2, side] = agg[...]


def turn_kernel(plus_ref, minus_ref, *outs):
    x = column()[0]
    for step, out in enumerate(outs):
        to = lax.rem(x + step, X)
        out[0] = plus_ref[to]
        out[1] = minus_ref[to]


def fold_kernel(part_ref, out_ref):
    full = part_ref.shape[2] - 128
    total = part_ref[0].astype(F32)
    for i in range(1, part_ref.shape[0]):
        total += part_ref[i].astype(F32)
    total = total.astype(BF16)
    tail = jnp.concatenate([total[0:4, full:], total[8:12, full:]], axis=0)
    for z in range(Z_HI * Z_LO):
        first = z // Z_LO * 8
        out_ref[z, :, :full] = total[first : first + 8, :full]
        out_ref[z, :, full:] = tail


def total_kernel(part_ref, out_ref, tail_ref):
    full = part_ref.shape[2] - 128
    total = part_ref[0].astype(F32)
    for i in range(1, part_ref.shape[0]):
        total += part_ref[i].astype(F32)
    out_ref[...] = total[:, :full]
    tail_ref[...] = total[:, full:]


def pair_kernel(one_ref, two_ref, out_ref):
    half = one_ref.shape[0]
    out_ref[:half] = one_ref[...]
    out_ref[half:] = two_ref[...]


def order_kernel(near_ref, far_ref, self_ref, neigh_ref):
    blk = lax.axis_index("blk")
    mine = blk // (Z_LO * CORE) * CORE + lax.rem(blk, CORE)
    for piece in range(Y * CORE):
        offset = jnp.bitwise_xor(mine, piece)
        rows = jnp.where(lax.rem(offset, 2) == 0, near_ref[offset // 2], far_ref[offset // 2])
        out = self_ref if piece < 4 else neigh_ref
        out[piece % 4 * 8 : piece % 4 * 8 + 8] = rows


def local_kernel(slots, chunk, x_ref, dst_ref, src_ref, cnt_ref, half_ref, acc_ref):
    step = pl.program_id(0)
    width = cnt_ref.shape[1]
    dim = x_ref.shape[0]
    half_ref[...] = cnt_ref[...].astype(F32).astype(BF16)

    @pl.when(step == 0)
    def _():
        acc_ref[...] = jnp.zeros_like(acc_ref)

    @pl.when(step * chunk >= slots)
    def _():
        ones = jnp.ones((16, width), BF16)
        for i in range(chunk):
            tile = step * chunk + i
            start = pl.multiple_of(src_ref[tile] * width, width)
            rows = jnp.concatenate([x_ref[:, pl.ds(start, width)], ones], axis=0)
            dst = dst_ref[tile]
            acc_ref[dst] += dot(rows, half_ref[i], LAST)[: dim + 8]


def aggregate_kernel(
    slots, a_ref, b_ref, dst_ref, src_ref, half_ref, acc_in, plus_ref, minus_ref, deg_ref, acc_ref
):
    place_a, place_b = places()
    z_hi = column()[1]
    cap, dim, width = a_ref.shape[1:]
    blocks = acc_in.shape[0]
    per = plus_ref.shape[1]
    ones = jnp.ones((16, width), BF16)
    acc_ref[...] = acc_in[...]
    for tile in range(slots):
        slot = src_ref[tile] - blocks
        kind = slot // cap
        m = lax.rem(slot, cap)
        row_a = place_a - offset_of(kind)
        row_b = place_b - offset_of(kind)
        got = jnp.where(inside(row_a), a_ref[bounded(row_a), m], b_ref[bounded(row_b), m])
        rows = jnp.concatenate([got, ones], axis=0)
        dst = dst_ref[tile]
        acc_ref[dst] += dot(rows, half_ref[tile], LAST)[: dim + 8]
    for block in range(blocks):
        deg_ref[block] = jnp.maximum(acc_ref[block, dim : dim + 8], 1.0)
    for x in range(X):
        for out, h in ((plus_ref, z_hi), (minus_ref, 1 - z_hi)):
            for p in range(per):
                block = (x * Z_HI + h) * per + p
                out[x, p] = (acc_ref[block, :dim] / deg_ref[block, :1]).astype(BF16)


def node_kernel(
    in_ref, wt_ref, neigh_ref, own_w_ref, bias_ref, plus_ref, minus_ref, dz_ref, xa_ref, cot_ref, home_ref
):
    _, _, sides, per_col, dim, width = in_ref.shape
    full = X * Z_HI * dim
    half = range_half()
    for x in range(X):
        for side, z in ((0, half), (1, 1 - half)):
            start = (x * Z_HI + z) * dim
            rows = pl.ds(pl.multiple_of(start, dim), dim)
            agg_rows = pl.ds(pl.multiple_of(full + start, dim), dim)
            for p in range(per_col):
                lanes = slice(p * width, (p + 1) * width)
                xa_ref[rows, lanes] = in_ref[x, 0, side, p]
                cot_ref[rows, lanes] = in_ref[x, 1, side, p]
                xa_ref[agg_rows, lanes] = in_ref[x, 2, side, p]
    for p in range(per_col):
        lanes = slice(p * width, (p + 1) * width)
        pre = dot(wt_ref[...], xa_ref[:, lanes]) + bias_ref[...]
        dz = (cot_ref[:, lanes].astype(F32) * gelu_slope(pre)).astype(BF16)
        dz_ref[:, lanes] = dz
        home_ref[0, :, lanes] = dot(neigh_ref[...], dz).astype(BF16)
        home_ref[1, :, lanes] = dot(own_w_ref[...], dz).astype(BF16)
    for x in range(X):
        for out, z in ((minus_ref, half), (plus_ref, 1 - half)):
            rows = pl.ds(pl.multiple_of((x * Z_HI + z) * dim, dim), dim)
            for which in range(2):
                for p in range(per_col):
                    out[x, which, p] = home_ref[which, rows, p * width : (p + 1) * width]


def weight_kernel(dim, xa_ref, dz_ref, part_ref):
    full = dz_ref.shape[0]
    grads = dot(xa_ref[...], dz_ref[...], LAST)
    total = dot(jnp.ones((16, dz_ref.shape[1]), BF16), dz_ref[...], LAST)
    tail = jnp.concatenate([total[:8, :128], total[8:, 128:]], axis=0).astype(BF16)
    for which in range(2):
        for quarter in range(4):
            for x in range(X):
                rows = [
                    grads[start : start + 8]
                    for z in range(Z_HI)
                    for start in [which * full + (x * Z_HI + z) * dim + quarter * 8]
                ]
                piece = (which * 4 + quarter) * X + x
                part_ref[piece, :, :full] = jnp.concatenate(rows, axis=0).astype(BF16)
                part_ref[piece, :, full:] = tail


def home_pieces(refs, which):
    x, z_hi = column()
    per = refs[0].shape[2]
    for step, ref in enumerate(refs):
        source = lax.rem(x + X - step, X)
        for side, h in ((0, 1 - z_hi), (1, z_hi)):
            for p in range(per):
                yield (source * Z_HI + h) * per + p, ref[side, which, p]


def contribution_kernel(
    slots, zero_ref, one_ref, two_ref, three_ref, deg_ref, dst_ref, src_ref, half_ref, *outs
):
    a_ref, b_ref, scaled_ref, hold_ref = outs
    place_a, place_b = places()
    blocks = scaled_ref.shape[0]
    cap = a_ref.shape[1]
    for block, piece in home_pieces((zero_ref, one_ref, two_ref, three_ref), 0):
        scaled_ref[block] = (piece.astype(F32) / deg_ref[block][:1]).astype(BF16)
    for tile in range(slots):
        value = dot(scaled_ref[dst_ref[tile]], half_ref[tile])
        hold_ref[src_ref[tile] - blocks] = value.astype(BF16)
    for ref, place in ((b_ref, place_b), (a_ref, place_a)):
        for peer in range(GROUP):
            kind = kind_of(place - peer)
            for m in range(cap):
                ref[peer, m] = hold_ref[kind * cap + m]


def local_back_kernel(
    slots, zero_ref, one_ref, two_ref, three_ref, scaled_ref, dst_ref, src_ref, half_ref, acc_ref
):
    for block, piece in home_pieces((zero_ref, one_ref, two_ref, three_ref), 1):
        acc_ref[block] = piece.astype(F32)
    for tile in range(slots, half_ref.shape[0]):
        acc_ref[src_ref[tile]] += dot(scaled_ref[dst_ref[tile]], half_ref[tile])


def finish_kernel(acc_in, a_ref, b_ref, send_ref, out_ref, acc_ref):
    place_a, place_b = places()
    kinds, cap = send_ref.shape
    width = acc_in.shape[2]
    acc_ref[...] = acc_in[...]
    for kind in range(kinds):
        offset = (kind // 2 + 1) * (1 - 2 * (kind % 2))
        row_a = place_a + offset
        row_b = place_b + offset
        for m in range(cap):
            got = jnp.where(inside(row_a), a_ref[bounded(row_a), m], b_ref[bounded(row_b), m])
            acc_ref[send_ref[kind, m]] += got.astype(F32)
    for block in range(acc_ref.shape[0]):
        out_ref[:, block * width : (block + 1) * width] = acc_ref[block].astype(BF16)


def rank(y, z_lo, core, x, z_hi):
    return ((y * Z_LO + z_lo) * CORE + core) * X * Z_HI + x * Z_HI + z_hi


def swap(rows, shift):
    devices = lax.axis_size("blk")
    groups = [
        [(first + shift + i) % devices for i in range(GROUP)] for first in range(0, devices, GROUP)
    ]
    return lax.all_to_all(rows, "blk", 0, 0, axis_index_groups=groups, tiled=False)


def across(rows, bit):
    return lax.ppermute(rows, "blk", [(e, e ^ bit) for e in range(lax.axis_size("blk"))])


def over_x(rows):
    groups = [[x * Z_HI + h for x in range(X)] for h in range(Z_HI)]
    return lax.all_to_all(rows, "col", 0, 0, axis_index_groups=groups, tiled=False)


def along_z(rows, step):
    chips = Z_LO * Z_HI
    route = []
    for y in range(Y):
        for core in range(CORE):
            for x in range(X):
                for z in range(chips):
                    to = (z + step) % chips
                    route.append(
                        (
                            rank(y, z % Z_LO, core, x, z // Z_LO),
                            rank(y, to % Z_LO, core, x, to // Z_LO),
                        )
                    )
    return lax.ppermute(rows, ("blk", "col"), sorted(route))


def per_device(
    node_feats, tile_dst, tile_src, tile_cnt, send_blk, self_weight, neigh_weight, bias, cotangent
):
    dim, nodes = node_feats.shape
    tiles, width = tile_cnt.shape[:2]
    blocks = nodes // width
    table = send_blk[0]
    kinds, cap = table.shape
    slots = kinds * cap
    cols = X * Z_HI
    per_col = blocks // cols
    full = cols * dim
    chunk = 8
    shape = lambda *dims: jax.ShapeDtypeStruct(dims + (dim, width), BF16)
    halo = shape(GROUP, cap)
    step = Z_LO // 2

    send_a, send_b = call(
        functools.partial(pack_kernel, width), (halo, halo), [VMEM, SMEM]
    )(node_feats, table)
    got_b = swap(send_b, GROUP // 2)
    xc_plus, xc_minus = call(
        functools.partial(split_kernel, width), (shape(X, 2, per_col),) * 2, [VMEM] * 2
    )(node_feats, cotangent)
    whole = lambda shape: pl.BlockSpec(shape, lambda i: (0,) * len(shape))
    half, acc = pl.pallas_call(
        functools.partial(local_kernel, slots, chunk),
        grid=(tiles // chunk,),
        out_shape=(
            jax.ShapeDtypeStruct(tile_cnt.shape, BF16),
            jax.ShapeDtypeStruct((blocks, dim + 8, width), F32),
        ),
        in_specs=[
            whole((dim, nodes)),
            SMEM,
            SMEM,
            pl.BlockSpec((chunk, width, width), lambda i: (i, 0, 0)),
        ],
        out_specs=(
            pl.BlockSpec((chunk, width, width), lambda i: (i, 0, 0)),
            whole((blocks, dim + 8, width)),
        ),
        compiler_params=pltpu.CompilerParams(vmem_limit_bytes=32 * 2**20),
        cost_estimate=pl.CostEstimate(
            flops=60000000, bytes_accessed=6000000, transcendentals=0
        ),
    )(node_feats, tile_dst, tile_src, tile_cnt)
    send_a, got_b, xc_plus, xc_minus, half, acc = lax.optimization_barrier(
        (send_a, got_b, xc_plus, xc_minus, half, acc)
    )
    xc_plus = along_z(xc_plus, step)
    xc_minus = along_z(xc_minus, -step)
    got_a = swap(send_a, 0)
    weight_t = jnp.concatenate([self_weight.T, neigh_weight.T], axis=1)
    bias_col = bias[:, None]
    agg_plus, agg_minus, degree = call(
        functools.partial(aggregate_kernel, slots),
        (shape(X, per_col), shape(X, per_col), jax.ShapeDtypeStruct((blocks, 8, width), F32)),
        [VMEM, VMEM, SMEM, SMEM, VMEM, VMEM],
        [pltpu.VMEM((blocks, dim + 8, width), F32)],
    )(got_a, got_b, tile_dst, tile_src, half, acc)
    agg_plus = along_z(agg_plus, step)
    agg_minus = along_z(agg_minus, -step)
    ranged = call(join_kernel, shape(X, 3, 2, per_col), [VMEM] * 4)(
        xc_plus, xc_minus, agg_plus, agg_minus
    )
    ranged = over_x(ranged)
    plus, minus, dz, xa = call(
        node_kernel,
        (
            shape(X, 2, per_col),
            shape(X, 2, per_col),
            jax.ShapeDtypeStruct((full, per_col * width), BF16),
            jax.ShapeDtypeStruct((2 * full, per_col * width), BF16),
        ),
        [VMEM] * 5,
        [
            pltpu.VMEM((full, per_col * width), BF16),
            pltpu.VMEM((2, full, per_col * width), BF16),
        ],
    )(ranged, weight_t, neigh_weight, self_weight, bias_col)
    plus = along_z(plus, step)
    minus = along_z(minus, -step)
    part = call(
        functools.partial(weight_kernel, dim),
        jax.ShapeDtypeStruct((Y * CORE * X, 16, full + 128), BF16),
        [VMEM] * 2,
    )(xa, dz)

    both = ("blk", "col")
    flat = [
        [rank(y, l, c, x, h) for y in range(Y) for c in range(CORE) for x in range(X)]
        for l in range(Z_LO)
        for h in range(Z_HI)
    ]
    line = [
        [rank(y, l, c, x, h) for h in range(Z_HI) for l in range(Z_LO)]
        for y in range(Y)
        for c in range(CORE)
        for x in range(X)
    ]
    part = lax.all_to_all(part, both, 0, 0, axis_index_groups=flat, tiled=False)
    (part,) = call(
        fold_kernel, (jax.ShapeDtypeStruct((Z_HI * Z_LO, 8, full + 128), BF16),), [VMEM]
    )(part)
    part, plus, minus = lax.optimization_barrier((part, plus, minus))
    part = lax.all_to_all(part, both, 0, 0, axis_index_groups=line, tiled=False)
    home = call(turn_kernel, (shape(2, 2, per_col),) * X, [VMEM] * 2)(plus, minus)
    route = lambda turn: [(c, (c + Z_HI * turn) % cols) for c in range(cols)]
    home = [home[0]] + [lax.ppermute(home[turn], "col", route(turn)) for turn in range(1, X)]
    away_a, away_b, scaled = call(
        functools.partial(contribution_kernel, slots),
        (halo, halo, shape(blocks)),
        [VMEM] * 5 + [SMEM, SMEM, VMEM],
        [pltpu.VMEM((slots, dim, width), BF16)],
    )(*home, degree, tile_dst, tile_src, half)
    row = jax.ShapeDtypeStruct((1, 8, full), F32)
    rows, tail = call(
        lambda part_ref, out_ref, tail_ref: total_kernel(part_ref, out_ref.at[0], tail_ref),
        (row, jax.ShapeDtypeStruct((8, 128), F32)),
        [VMEM],
    )(part)
    grad_bias = jnp.concatenate([tail[0], tail[4]])
    grad_bias = lax.dynamic_slice_in_dim(grad_bias, lax.axis_index("col") * dim, dim, 0)
    away_b, rows = lax.optimization_barrier((away_b, rows))
    back_b = swap(away_b, GROUP // 2)
    pair = call(pair_kernel, jax.ShapeDtypeStruct((2, 8, full), F32), [VMEM] * 2)(
        rows, across(rows, Z_LO * CORE)
    )
    away_a, back_b, pair = lax.optimization_barrier((away_a, back_b, pair))
    back_a = swap(away_a, 0)
    rows = call(pair_kernel, jax.ShapeDtypeStruct((4, 8, full), F32), [VMEM] * 2)(
        pair, across(pair, 2 * Z_LO * CORE)
    )
    grad = jax.ShapeDtypeStruct((dim, full), F32)
    grad_self, grad_neigh = call(order_kernel, (grad, grad), [VMEM] * 2)(rows, across(rows, 1))
    acc = call(
        functools.partial(local_back_kernel, slots),
        jax.ShapeDtypeStruct((blocks, dim, width), F32),
        [VMEM] * 5 + [SMEM, SMEM, VMEM],
    )(*home, scaled, tile_dst, tile_src, half)
    grad_feats = call(
        finish_kernel,
        jax.ShapeDtypeStruct((dim, nodes), BF16),
        [VMEM, VMEM, VMEM, SMEM],
        [pltpu.VMEM((blocks, dim, width), F32)],
    )(acc, back_a, back_b, table)
    return grad_feats, grad_self, grad_neigh, grad_bias


def solution(mesh):
    placed = (
        P("col", "blk"),
        P("blk"),
        P("blk"),
        P("blk", None, None),
        P("blk", None, None),
        P(),
        P(),
        P(),
        P("col", "blk"),
    )
    return jax.shard_map(
        per_device,
        mesh=mesh,
        in_specs=placed,
        out_specs=(P("col", "blk"), P("col", None), P("col", None), P("col")),
        check_vma=False,
    )
```

```python
import functools

import jax
import jax.numpy as jnp
from jax import lax
from jax.experimental import pallas as pl
from jax.experimental.pallas import tpu as pltpu
from jax.sharding import PartitionSpec as P

GROUP = 8
Y, Z_LO, CORE, X, Z_HI = 4, 8, 2, 4, 2
BF16 = jnp.bfloat16
F32 = jnp.float32
FIRST = (((0,), (0,)), ((), ()))
LAST = (((1,), (1,)), ((), ()))
VMEM = pl.BlockSpec(memory_space=pltpu.VMEM)
SMEM = pl.BlockSpec(memory_space=pltpu.SMEM)


def gelu_slope(pre_act):
    inner = 0.7978845608 * (pre_act + 0.044715 * pre_act * pre_act * pre_act)
    tanh_value = jnp.tanh(inner)
    return 0.5 * (1.0 + tanh_value) + 0.5 * pre_act * (
        1.0 - tanh_value * tanh_value
    ) * 0.7978845608 * (1.0 + 3.0 * 0.044715 * pre_act * pre_act)


def dot(left, right, dims=(((1,), (0,)), ((), ()))):
    return lax.dot_general(left, right, dims, preferred_element_type=F32)


def call(body, out_shape, in_specs, scratch=(), cost=(1e7, 1e6)):
    outs = jax.tree.map(lambda _: VMEM, out_shape)
    return pl.pallas_call(
        body,
        out_shape=out_shape,
        in_specs=in_specs,
        out_specs=outs,
        scratch_shapes=scratch,
        compiler_params=pltpu.CompilerParams(vmem_limit_bytes=32 * 2**20),
        cost_estimate=pl.CostEstimate(
            flops=int(cost[0]), bytes_accessed=int(cost[1]), transcendentals=0
        ),
    )


def places():
    blk = lax.axis_index("blk")
    return lax.rem(blk, GROUP), lax.rem(blk + GROUP // 2, GROUP)


def kind_of(distance):
    k = 2 * (jnp.abs(distance) - 1) + jnp.where(distance < 0, 1, 0)
    return jnp.clip(k, 0, 7)


def offset_of(kind):
    return (kind // 2 + 1) * (1 - 2 * lax.rem(kind, 2))


def inside(place):
    return jnp.logical_and(place >= 0, place < GROUP)


def bounded(place):
    return jnp.clip(place, 0, GROUP - 1)


def pack_kernel(width, x_ref, send_ref, a_ref, b_ref, block_ref):
    place_a, place_b = places()
    for block in range(block_ref.shape[0]):
        block_ref[block] = x_ref[:, block * width : (block + 1) * width]
    cap = send_ref.shape[1]
    for ref, place in ((b_ref, place_b), (a_ref, place_a)):
        for peer in range(GROUP):
            kind = kind_of(peer - place)
            for m in range(cap):
                start = pl.multiple_of(send_ref[kind, m] * width, width)
                ref[peer, m] = x_ref[:, pl.ds(start, width)]


def column():
    col = lax.axis_index("col")
    return col // Z_HI, lax.rem(col, Z_HI)


def range_half():
    z = column()[1] * Z_LO + lax.rem(lax.axis_index("blk") // CORE, Z_LO)
    middle = jnp.logical_and(z >= Z_LO // 2, z < Z_LO // 2 * 3)
    return jnp.where(middle, 0, 1)


def split_kernel(width, x_ref, cot_ref, plus_ref, minus_ref):
    z_hi = column()[1]
    per = plus_ref.shape[2]
    for x in range(X):
        for out, h in ((plus_ref, z_hi), (minus_ref, 1 - z_hi)):
            for p in range(per):
                block = (x * Z_HI + h) * per + p
                start = pl.multiple_of(block * width, width)
                out[x, 0, p] = x_ref[block]
                out[x, 1, p] = cot_ref[:, pl.ds(start, width)]


def join_kernel(xc_plus_ref, xc_minus_ref, agg_plus_ref, agg_minus_ref, out_ref):
    for side, (xc, agg) in enumerate(((xc_plus_ref, agg_plus_ref), (xc_minus_ref, agg_minus_ref))):
        for which in range(2):
            out_ref[:, which, side] = xc[:, which]
        out_ref[:, 2, side] = agg[...]


def turn_kernel(plus_ref, minus_ref, *outs):
    x = column()[0]
    for step, out in enumerate(outs):
        to = lax.rem(x + step, X)
        out[0] = plus_ref[to]
        out[1] = minus_ref[to]


def fold_kernel(part_ref, out_ref):
    full = part_ref.shape[2] - 128
    total = part_ref[0].astype(F32)
    for i in range(1, part_ref.shape[0]):
        total += part_ref[i].astype(F32)
    total = total.astype(BF16)
    tail = jnp.concatenate([total[0:4, full:], total[8:12, full:]], axis=0)
    for z in range(Z_HI * Z_LO):
        first = z // Z_LO * 8
        out_ref[z, :, :full] = total[first : first + 8, :full]
        out_ref[z, :, full:] = tail


def total_kernel(part_ref, out_ref, tail_ref):
    full = part_ref.shape[2] - 128
    total = part_ref[0].astype(F32)
    for i in range(1, part_ref.shape[0]):
        total += part_ref[i].astype(F32)
    out_ref[...] = total[:, :full]
    tail_ref[...] = total[:, full:]


def pair_kernel(one_ref, two_ref, out_ref):
    half = one_ref.shape[0]
    out_ref[:half] = one_ref[...]
    out_ref[half:] = two_ref[...]


def order_kernel(near_ref, far_ref, self_ref, neigh_ref):
    blk = lax.axis_index("blk")
    mine = blk // (Z_LO * CORE) * CORE + lax.rem(blk, CORE)
    for piece in range(Y * CORE):
        offset = jnp.bitwise_xor(mine, piece)
        rows = jnp.where(lax.rem(offset, 2) == 0, near_ref[offset // 2], far_ref[offset // 2])
        out = self_ref if piece < 4 else neigh_ref
        out[piece % 4 * 8 : piece % 4 * 8 + 8] = rows


def local_kernel(slots, chunk, x_ref, dst_ref, src_ref, cnt_ref, half_ref, acc_ref):
    step = pl.program_id(0)
    width = cnt_ref.shape[1]
    dim = x_ref.shape[1]
    half_ref[...] = cnt_ref[...].astype(F32).astype(BF16)

    @pl.when(step == 0)
    def _():
        acc_ref[...] = jnp.zeros_like(acc_ref)

    @pl.when(step * chunk >= slots)
    def _():
        ones = jnp.ones((16, width), BF16)
        for i in range(chunk):
            tile = step * chunk + i
            rows = jnp.concatenate([x_ref[src_ref[tile]], ones], axis=0)
            dst = dst_ref[tile]
            acc_ref[dst] += dot(rows, half_ref[i], LAST)[: dim + 8]


def aggregate_kernel(
    slots, a_ref, b_ref, dst_ref, src_ref, half_ref, acc_in, plus_ref, minus_ref, deg_ref, acc_ref
):
    place_a, place_b = places()
    z_hi = column()[1]
    cap, dim, width = a_ref.shape[1:]
    blocks = acc_in.shape[0]
    per = plus_ref.shape[1]
    ones = jnp.ones((16, width), BF16)
    acc_ref[...] = acc_in[...]
    for tile in range(slots):
        slot = src_ref[tile] - blocks
        kind = slot // cap
        m = lax.rem(slot, cap)
        row_a = place_a - offset_of(kind)
        row_b = place_b - offset_of(kind)
        got = jnp.where(inside(row_a), a_ref[bounded(row_a), m], b_ref[bounded(row_b), m])
        rows = jnp.concatenate([got, ones], axis=0)
        dst = dst_ref[tile]
        acc_ref[dst] += dot(rows, half_ref[tile], LAST)[: dim + 8]
    for block in range(blocks):
        deg_ref[block] = jnp.maximum(acc_ref[block, dim : dim + 8], 1.0)
    for x in range(X):
        for out, h in ((plus_ref, z_hi), (minus_ref, 1 - z_hi)):
            for p in range(per):
                block = (x * Z_HI + h) * per + p
                out[x, p] = (acc_ref[block, :dim] / deg_ref[block, :1]).astype(BF16)


def node_kernel(
    in_ref, wt_ref, neigh_ref, own_w_ref, bias_ref, plus_ref, minus_ref, dz_ref, xa_ref, cot_ref, home_ref
):
    _, _, sides, per_col, dim, width = in_ref.shape
    full = X * Z_HI * dim
    half = range_half()
    for x in range(X):
        for side, z in ((0, half), (1, 1 - half)):
            start = (x * Z_HI + z) * dim
            rows = pl.ds(pl.multiple_of(start, dim), dim)
            agg_rows = pl.ds(pl.multiple_of(full + start, dim), dim)
            for p in range(per_col):
                lanes = slice(p * width, (p + 1) * width)
                xa_ref[rows, lanes] = in_ref[x, 0, side, p]
                cot_ref[rows, lanes] = in_ref[x, 1, side, p]
                xa_ref[agg_rows, lanes] = in_ref[x, 2, side, p]
    for p in range(per_col):
        lanes = slice(p * width, (p + 1) * width)
        pre = dot(wt_ref[...], xa_ref[:, lanes]) + bias_ref[...]
        dz = (cot_ref[:, lanes].astype(F32) * gelu_slope(pre)).astype(BF16)
        dz_ref[:, lanes] = dz
        home_ref[0, :, lanes] = dot(neigh_ref[...], dz).astype(BF16)
        home_ref[1, :, lanes] = dot(own_w_ref[...], dz).astype(BF16)
    for x in range(X):
        for out, z in ((minus_ref, half), (plus_ref, 1 - half)):
            rows = pl.ds(pl.multiple_of((x * Z_HI + z) * dim, dim), dim)
            for which in range(2):
                for p in range(per_col):
                    out[x, which, p] = home_ref[which, rows, p * width : (p + 1) * width]


def weight_kernel(dim, xa_ref, dz_ref, part_ref):
    full = dz_ref.shape[0]
    grads = dot(xa_ref[...], dz_ref[...], LAST)
    total = dot(jnp.ones((16, dz_ref.shape[1]), BF16), dz_ref[...], LAST)
    tail = jnp.concatenate([total[:8, :128], total[8:, 128:]], axis=0).astype(BF16)
    for which in range(2):
        for quarter in range(4):
            for x in range(X):
                rows = [
                    grads[start : start + 8]
                    for z in range(Z_HI)
                    for start in [which * full + (x * Z_HI + z) * dim + quarter * 8]
                ]
                piece = (which * 4 + quarter) * X + x
                part_ref[piece, :, :full] = jnp.concatenate(rows, axis=0).astype(BF16)
                part_ref[piece, :, full:] = tail


def home_pieces(refs, which):
    x, z_hi = column()
    per = refs[0].shape[2]
    for step, ref in enumerate(refs):
        source = lax.rem(x + X - step, X)
        for side, h in ((0, 1 - z_hi), (1, z_hi)):
            for p in range(per):
                yield (source * Z_HI + h) * per + p, ref[side, which, p]


def contribution_kernel(
    slots, zero_ref, one_ref, two_ref, three_ref, deg_ref, dst_ref, src_ref, half_ref, *outs
):
    a_ref, b_ref, scaled_ref, hold_ref = outs
    place_a, place_b = places()
    blocks = scaled_ref.shape[0]
    cap = a_ref.shape[1]
    for block, piece in home_pieces((zero_ref, one_ref, two_ref, three_ref), 0):
        scaled_ref[block] = (piece.astype(F32) / deg_ref[block][:1]).astype(BF16)
    for tile in range(slots):
        value = dot(scaled_ref[dst_ref[tile]], half_ref[tile])
        hold_ref[src_ref[tile] - blocks] = value.astype(BF16)
    for ref, place in ((b_ref, place_b), (a_ref, place_a)):
        for peer in range(GROUP):
            kind = kind_of(place - peer)
            for m in range(cap):
                ref[peer, m] = hold_ref[kind * cap + m]


def local_back_kernel(
    slots, zero_ref, one_ref, two_ref, three_ref, scaled_ref, dst_ref, src_ref, half_ref, acc_ref
):
    for block, piece in home_pieces((zero_ref, one_ref, two_ref, three_ref), 1):
        acc_ref[block] = piece.astype(F32)
    for tile in range(slots, half_ref.shape[0]):
        acc_ref[src_ref[tile]] += dot(scaled_ref[dst_ref[tile]], half_ref[tile])


def finish_kernel(acc_in, a_ref, b_ref, send_ref, out_ref, acc_ref):
    place_a, place_b = places()
    kinds, cap = send_ref.shape
    width = acc_in.shape[2]
    acc_ref[...] = acc_in[...]
    for kind in range(kinds):
        offset = (kind // 2 + 1) * (1 - 2 * (kind % 2))
        row_a = place_a + offset
        row_b = place_b + offset
        for m in range(cap):
            got = jnp.where(inside(row_a), a_ref[bounded(row_a), m], b_ref[bounded(row_b), m])
            acc_ref[send_ref[kind, m]] += got.astype(F32)
    for block in range(acc_ref.shape[0]):
        out_ref[:, block * width : (block + 1) * width] = acc_ref[block].astype(BF16)


def rank(y, z_lo, core, x, z_hi):
    return ((y * Z_LO + z_lo) * CORE + core) * X * Z_HI + x * Z_HI + z_hi


def swap(rows, shift):
    devices = lax.axis_size("blk")
    groups = [
        [(first + shift + i) % devices for i in range(GROUP)] for first in range(0, devices, GROUP)
    ]
    return lax.all_to_all(rows, "blk", 0, 0, axis_index_groups=groups, tiled=False)


def across(rows, bit):
    return lax.ppermute(rows, "blk", [(e, e ^ bit) for e in range(lax.axis_size("blk"))])


def over_x(rows):
    groups = [[x * Z_HI + h for x in range(X)] for h in range(Z_HI)]
    return lax.all_to_all(rows, "col", 0, 0, axis_index_groups=groups, tiled=False)


def along_z(rows, step):
    chips = Z_LO * Z_HI
    route = []
    for y in range(Y):
        for core in range(CORE):
            for x in range(X):
                for z in range(chips):
                    to = (z + step) % chips
                    route.append(
                        (
                            rank(y, z % Z_LO, core, x, z // Z_LO),
                            rank(y, to % Z_LO, core, x, to // Z_LO),
                        )
                    )
    return lax.ppermute(rows, ("blk", "col"), sorted(route))


def per_device(
    node_feats, tile_dst, tile_src, tile_cnt, send_blk, self_weight, neigh_weight, bias, cotangent
):
    dim, nodes = node_feats.shape
    tiles, width = tile_cnt.shape[:2]
    blocks = nodes // width
    table = send_blk[0]
    kinds, cap = table.shape
    slots = kinds * cap
    cols = X * Z_HI
    per_col = blocks // cols
    full = cols * dim
    chunk = 8
    shape = lambda *dims: jax.ShapeDtypeStruct(dims + (dim, width), BF16)
    halo = shape(GROUP, cap)
    step = Z_LO // 2

    send_a, send_b, feats = call(
        functools.partial(pack_kernel, width), (halo, halo, shape(blocks)), [VMEM, SMEM]
    )(node_feats, table)
    got_b = swap(send_b, GROUP // 2)
    xc_plus, xc_minus = call(
        functools.partial(split_kernel, width), (shape(X, 2, per_col),) * 2, [VMEM] * 2
    )(feats, cotangent)
    whole = lambda shape: pl.BlockSpec(shape, lambda i: (0,) * len(shape))
    half, acc = pl.pallas_call(
        functools.partial(local_kernel, slots, chunk),
        grid=(tiles // chunk,),
        out_shape=(
            jax.ShapeDtypeStruct(tile_cnt.shape, BF16),
            jax.ShapeDtypeStruct((blocks, dim + 8, width), F32),
        ),
        in_specs=[
            whole((blocks, dim, width)),
            SMEM,
            SMEM,
            pl.BlockSpec((chunk, width, width), lambda i: (i, 0, 0)),
        ],
        out_specs=(
            pl.BlockSpec((chunk, width, width), lambda i: (i, 0, 0)),
            whole((blocks, dim + 8, width)),
        ),
        compiler_params=pltpu.CompilerParams(vmem_limit_bytes=32 * 2**20),
        cost_estimate=pl.CostEstimate(
            flops=60000000, bytes_accessed=6000000, transcendentals=0
        ),
    )(feats, tile_dst, tile_src, tile_cnt)
    send_a, got_b, xc_plus, xc_minus, half, acc = lax.optimization_barrier(
        (send_a, got_b, xc_plus, xc_minus, half, acc)
    )
    xc_plus = along_z(xc_plus, step)
    xc_minus = along_z(xc_minus, -step)
    got_a = swap(send_a, 0)
    weight_t = jnp.concatenate([self_weight.T, neigh_weight.T], axis=1)
    bias_col = bias[:, None]
    agg_plus, agg_minus, degree = call(
        functools.partial(aggregate_kernel, slots),
        (shape(X, per_col), shape(X, per_col), jax.ShapeDtypeStruct((blocks, 8, width), F32)),
        [VMEM, VMEM, SMEM, SMEM, VMEM, VMEM],
        [pltpu.VMEM((blocks, dim + 8, width), F32)],
    )(got_a, got_b, tile_dst, tile_src, half, acc)
    agg_plus = along_z(agg_plus, step)
    agg_minus = along_z(agg_minus, -step)
    ranged = call(join_kernel, shape(X, 3, 2, per_col), [VMEM] * 4)(
        xc_plus, xc_minus, agg_plus, agg_minus
    )
    ranged = over_x(ranged)
    plus, minus, dz, xa = call(
        node_kernel,
        (
            shape(X, 2, per_col),
            shape(X, 2, per_col),
            jax.ShapeDtypeStruct((full, per_col * width), BF16),
            jax.ShapeDtypeStruct((2 * full, per_col * width), BF16),
        ),
        [VMEM] * 5,
        [
            pltpu.VMEM((full, per_col * width), BF16),
            pltpu.VMEM((2, full, per_col * width), BF16),
        ],
    )(ranged, weight_t, neigh_weight, self_weight, bias_col)
    plus = along_z(plus, step)
    minus = along_z(minus, -step)
    part = call(
        functools.partial(weight_kernel, dim),
        jax.ShapeDtypeStruct((Y * CORE * X, 16, full + 128), BF16),
        [VMEM] * 2,
    )(xa, dz)

    both = ("blk", "col")
    flat = [
        [rank(y, l, c, x, h) for y in range(Y) for c in range(CORE) for x in range(X)]
        for l in range(Z_LO)
        for h in range(Z_HI)
    ]
    line = [
        [rank(y, l, c, x, h) for h in range(Z_HI) for l in range(Z_LO)]
        for y in range(Y)
        for c in range(CORE)
        for x in range(X)
    ]
    part = lax.all_to_all(part, both, 0, 0, axis_index_groups=flat, tiled=False)
    home = call(turn_kernel, (shape(2, 2, per_col),) * X, [VMEM] * 2, cost=(1e10, 1e6))(plus, minus)
    part, *home = lax.optimization_barrier((part, *home))
    (part,) = call(
        fold_kernel, (jax.ShapeDtypeStruct((Z_HI * Z_LO, 8, full + 128), BF16),), [VMEM]
    )(part)
    part = lax.all_to_all(part, both, 0, 0, axis_index_groups=line, tiled=False)
    route = lambda turn: [(c, (c + Z_HI * turn) % cols) for c in range(cols)]
    home = [home[0]] + [lax.ppermute(home[turn], "col", route(turn)) for turn in range(1, X)]
    away_a, away_b, scaled = call(
        functools.partial(contribution_kernel, slots),
        (halo, halo, shape(blocks)),
        [VMEM] * 5 + [SMEM, SMEM, VMEM],
        [pltpu.VMEM((slots, dim, width), BF16)],
    )(*home, degree, tile_dst, tile_src, half)
    row = jax.ShapeDtypeStruct((1, 8, full), F32)
    rows, tail = call(
        lambda part_ref, out_ref, tail_ref: total_kernel(part_ref, out_ref.at[0], tail_ref),
        (row, jax.ShapeDtypeStruct((8, 128), F32)),
        [VMEM],
    )(part)
    grad_bias = jnp.concatenate([tail[0], tail[4]])
    grad_bias = lax.dynamic_slice_in_dim(grad_bias, lax.axis_index("col") * dim, dim, 0)
    away_b, rows = lax.optimization_barrier((away_b, rows))
    back_b = swap(away_b, GROUP // 2)
    pair = call(pair_kernel, jax.ShapeDtypeStruct((2, 8, full), F32), [VMEM] * 2)(
        rows, across(rows, Z_LO * CORE)
    )
    away_a, back_b, pair = lax.optimization_barrier((away_a, back_b, pair))
    back_a = swap(away_a, 0)
    rows = call(pair_kernel, jax.ShapeDtypeStruct((4, 8, full), F32), [VMEM] * 2)(
        pair, across(pair, 2 * Z_LO * CORE)
    )
    grad = jax.ShapeDtypeStruct((dim, full), F32)
    grad_self, grad_neigh = call(order_kernel, (grad, grad), [VMEM] * 2)(rows, across(rows, 1))
    acc = call(
        functools.partial(local_back_kernel, slots),
        jax.ShapeDtypeStruct((blocks, dim, width), F32),
        [VMEM] * 5 + [SMEM, SMEM, VMEM],
    )(*home, scaled, tile_dst, tile_src, half)
    grad_feats = call(
        finish_kernel,
        jax.ShapeDtypeStruct((dim, nodes), BF16),
        [VMEM, VMEM, VMEM, SMEM],
        [pltpu.VMEM((blocks, dim, width), F32)],
    )(acc, back_a, back_b, table)
    return grad_feats, grad_self, grad_neigh, grad_bias


def solution(mesh):
    placed = (
        P("col", "blk"),
        P("blk"),
        P("blk"),
        P("blk", None, None),
        P("blk", None, None),
        P(),
        P(),
        P(),
        P("col", "blk"),
    )
    return jax.shard_map(
        per_device,
        mesh=mesh,
        in_specs=placed,
        out_specs=(P("col", "blk"), P("col", None), P("col", None), P("col")),
        check_vma=False,
    )
```

```python
import functools

import jax
import jax.numpy as jnp
from jax import lax
from jax.experimental import pallas as pl
from jax.experimental.pallas import tpu as pltpu
from jax.sharding import PartitionSpec as P

GROUP = 8
Y, Z_LO, CORE, X, Z_HI = 4, 8, 2, 4, 2
BF16 = jnp.bfloat16
F32 = jnp.float32
FIRST = (((0,), (0,)), ((), ()))
LAST = (((1,), (1,)), ((), ()))
VMEM = pl.BlockSpec(memory_space=pltpu.VMEM)
SMEM = pl.BlockSpec(memory_space=pltpu.SMEM)


def gelu_slope(pre_act):
    inner = 0.7978845608 * (pre_act + 0.044715 * pre_act * pre_act * pre_act)
    tanh_value = jnp.tanh(inner)
    return 0.5 * (1.0 + tanh_value) + 0.5 * pre_act * (
        1.0 - tanh_value * tanh_value
    ) * 0.7978845608 * (1.0 + 3.0 * 0.044715 * pre_act * pre_act)


def dot(left, right, dims=(((1,), (0,)), ((), ()))):
    return lax.dot_general(left, right, dims, preferred_element_type=F32)


def call(body, out_shape, in_specs, scratch=(), cost=(1e7, 1e6)):
    outs = jax.tree.map(lambda _: VMEM, out_shape)
    return pl.pallas_call(
        body,
        out_shape=out_shape,
        in_specs=in_specs,
        out_specs=outs,
        scratch_shapes=scratch,
        compiler_params=pltpu.CompilerParams(vmem_limit_bytes=32 * 2**20),
        cost_estimate=pl.CostEstimate(
            flops=int(cost[0]), bytes_accessed=int(cost[1]), transcendentals=0
        ),
    )


def places():
    blk = lax.axis_index("blk")
    return lax.rem(blk, GROUP), lax.rem(blk + GROUP // 2, GROUP)


def kind_of(distance):
    k = 2 * (jnp.abs(distance) - 1) + jnp.where(distance < 0, 1, 0)
    return jnp.clip(k, 0, 7)


def offset_of(kind):
    return (kind // 2 + 1) * (1 - 2 * lax.rem(kind, 2))


def inside(place):
    return jnp.logical_and(place >= 0, place < GROUP)


def bounded(place):
    return jnp.clip(place, 0, GROUP - 1)


def pack_kernel(width, x_ref, send_ref, a_ref, b_ref, block_ref):
    place_a, place_b = places()
    for block in range(block_ref.shape[0]):
        block_ref[block] = x_ref[:, block * width : (block + 1) * width]
    cap = send_ref.shape[1]
    for ref, place in ((b_ref, place_b), (a_ref, place_a)):
        for peer in range(GROUP):
            kind = kind_of(peer - place)
            for m in range(cap):
                start = pl.multiple_of(send_ref[kind, m] * width, width)
                ref[peer, m] = x_ref[:, pl.ds(start, width)]


def column():
    col = lax.axis_index("col")
    return col // Z_HI, lax.rem(col, Z_HI)


def range_half():
    z = column()[1] * Z_LO + lax.rem(lax.axis_index("blk") // CORE, Z_LO)
    middle = jnp.logical_and(z >= Z_LO // 2, z < Z_LO // 2 * 3)
    return jnp.where(middle, 0, 1)


def split_kernel(width, x_ref, cot_ref, plus_ref, minus_ref):
    z_hi = column()[1]
    per = plus_ref.shape[2]
    for x in range(X):
        for out, h in ((plus_ref, z_hi), (minus_ref, 1 - z_hi)):
            for p in range(per):
                block = (x * Z_HI + h) * per + p
                start = pl.multiple_of(block * width, width)
                out[x, 0, p] = x_ref[block]
                out[x, 1, p] = cot_ref[:, pl.ds(start, width)]


def join_kernel(xc_plus_ref, xc_minus_ref, agg_plus_ref, agg_minus_ref, out_ref):
    for side, (xc, agg) in enumerate(((xc_plus_ref, agg_plus_ref), (xc_minus_ref, agg_minus_ref))):
        for which in range(2):
            out_ref[:, which, side] = xc[:, which]
        out_ref[:, 2, side] = agg[...]


def turn_kernel(plus_ref, minus_ref, *outs):
    x = column()[0]
    for step, out in enumerate(outs):
        to = lax.rem(x + step, X)
        out[0] = plus_ref[to]
        out[1] = minus_ref[to]


def fold_kernel(part_ref, out_ref):
    full = part_ref.shape[2] - 128
    total = part_ref[0].astype(F32)
    for i in range(1, part_ref.shape[0]):
        total += part_ref[i].astype(F32)
    total = total.astype(BF16)
    tail = jnp.concatenate([total[0:4, full:], total[8:12, full:]], axis=0)
    for z in range(Z_HI * Z_LO):
        first = z // Z_LO * 8
        out_ref[z, :, :full] = total[first : first + 8, :full]
        out_ref[z, :, full:] = tail


def total_kernel(part_ref, out_ref, tail_ref):
    full = part_ref.shape[2] - 128
    total = part_ref[0].astype(F32)
    for i in range(1, part_ref.shape[0]):
        total += part_ref[i].astype(F32)
    out_ref[...] = total[:, :full]
    tail_ref[...] = total[:, full:]


def pair_kernel(one_ref, two_ref, out_ref):
    half = one_ref.shape[0]
    out_ref[:half] = one_ref[...]
    out_ref[half:] = two_ref[...]


def order_kernel(near_ref, far_ref, self_ref, neigh_ref):
    blk = lax.axis_index("blk")
    mine = blk // (Z_LO * CORE) * CORE + lax.rem(blk, CORE)
    for piece in range(Y * CORE):
        offset = jnp.bitwise_xor(mine, piece)
        place = lax.rem(offset, 4)
        rows = jnp.where(offset < 4, near_ref[place], far_ref[place])
        out = self_ref if piece < 4 else neigh_ref
        out[piece % 4 * 8 : piece % 4 * 8 + 8] = rows


def local_kernel(slots, chunk, x_ref, dst_ref, src_ref, cnt_ref, half_ref, acc_ref):
    step = pl.program_id(0)
    width = cnt_ref.shape[1]
    dim = x_ref.shape[1]
    half_ref[...] = cnt_ref[...].astype(F32).astype(BF16)

    @pl.when(step == 0)
    def _():
        acc_ref[...] = jnp.zeros_like(acc_ref)

    @pl.when(step * chunk >= slots)
    def _():
        ones = jnp.ones((16, width), BF16)
        for i in range(chunk):
            tile = step * chunk + i
            rows = jnp.concatenate([x_ref[src_ref[tile]], ones], axis=0)
            dst = dst_ref[tile]
            acc_ref[dst] += dot(rows, half_ref[i], LAST)[: dim + 8]


def aggregate_kernel(
    slots, a_ref, b_ref, dst_ref, src_ref, half_ref, acc_in, plus_ref, minus_ref, deg_ref, acc_ref
):
    place_a, place_b = places()
    z_hi = column()[1]
    cap, dim, width = a_ref.shape[1:]
    blocks = acc_in.shape[0]
    per = plus_ref.shape[1]
    ones = jnp.ones((16, width), BF16)
    acc_ref[...] = acc_in[...]
    for tile in range(slots):
        slot = src_ref[tile] - blocks
        kind = slot // cap
        m = lax.rem(slot, cap)
        row_a = place_a - offset_of(kind)
        row_b = place_b - offset_of(kind)
        got = jnp.where(inside(row_a), a_ref[bounded(row_a), m], b_ref[bounded(row_b), m])
        rows = jnp.concatenate([got, ones], axis=0)
        dst = dst_ref[tile]
        acc_ref[dst] += dot(rows, half_ref[tile], LAST)[: dim + 8]
    for block in range(blocks):
        deg_ref[block] = jnp.maximum(acc_ref[block, dim : dim + 8], 1.0)
    for x in range(X):
        for out, h in ((plus_ref, z_hi), (minus_ref, 1 - z_hi)):
            for p in range(per):
                block = (x * Z_HI + h) * per + p
                out[x, p] = (acc_ref[block, :dim] / deg_ref[block, :1]).astype(BF16)


def node_kernel(
    in_ref, wt_ref, neigh_ref, own_w_ref, bias_ref, plus_ref, minus_ref, dz_ref, xa_ref, cot_ref, home_ref
):
    _, _, sides, per_col, dim, width = in_ref.shape
    full = X * Z_HI * dim
    half = range_half()
    for x in range(X):
        for side, z in ((0, half), (1, 1 - half)):
            start = (x * Z_HI + z) * dim
            rows = pl.ds(pl.multiple_of(start, dim), dim)
            agg_rows = pl.ds(pl.multiple_of(full + start, dim), dim)
            for p in range(per_col):
                lanes = slice(p * width, (p + 1) * width)
                xa_ref[rows, lanes] = in_ref[x, 0, side, p]
                cot_ref[rows, lanes] = in_ref[x, 1, side, p]
                xa_ref[agg_rows, lanes] = in_ref[x, 2, side, p]
    for p in range(per_col):
        lanes = slice(p * width, (p + 1) * width)
        pre = dot(wt_ref[...], xa_ref[:, lanes]) + bias_ref[...]
        dz = (cot_ref[:, lanes].astype(F32) * gelu_slope(pre)).astype(BF16)
        dz_ref[:, lanes] = dz
        home_ref[0, :, lanes] = dot(neigh_ref[...], dz).astype(BF16)
        home_ref[1, :, lanes] = dot(own_w_ref[...], dz).astype(BF16)
    for x in range(X):
        for out, z in ((minus_ref, half), (plus_ref, 1 - half)):
            rows = pl.ds(pl.multiple_of((x * Z_HI + z) * dim, dim), dim)
            for which in range(2):
                for p in range(per_col):
                    out[x, which, p] = home_ref[which, rows, p * width : (p + 1) * width]


def weight_kernel(dim, xa_ref, dz_ref, part_ref):
    full = dz_ref.shape[0]
    grads = dot(xa_ref[...], dz_ref[...], LAST)
    total = dot(jnp.ones((16, dz_ref.shape[1]), BF16), dz_ref[...], LAST)
    tail = jnp.concatenate([total[:8, :128], total[8:, 128:]], axis=0).astype(BF16)
    for which in range(2):
        for quarter in range(4):
            for x in range(X):
                rows = [
                    grads[start : start + 8]
                    for z in range(Z_HI)
                    for start in [which * full + (x * Z_HI + z) * dim + quarter * 8]
                ]
                piece = (which * 4 + quarter) * X + x
                part_ref[piece, :, :full] = jnp.concatenate(rows, axis=0).astype(BF16)
                part_ref[piece, :, full:] = tail


def home_pieces(refs, which):
    x, z_hi = column()
    per = refs[0].shape[2]
    for step, ref in enumerate(refs):
        source = lax.rem(x + X - step, X)
        for side, h in ((0, 1 - z_hi), (1, z_hi)):
            for p in range(per):
                yield (source * Z_HI + h) * per + p, ref[side, which, p]


def contribution_kernel(
    slots, zero_ref, one_ref, two_ref, three_ref, deg_ref, dst_ref, src_ref, half_ref, *outs
):
    a_ref, b_ref, scaled_ref, hold_ref = outs
    place_a, place_b = places()
    blocks = scaled_ref.shape[0]
    cap = a_ref.shape[1]
    for block, piece in home_pieces((zero_ref, one_ref, two_ref, three_ref), 0):
        scaled_ref[block] = (piece.astype(F32) / deg_ref[block][:1]).astype(BF16)
    for tile in range(slots):
        value = dot(scaled_ref[dst_ref[tile]], half_ref[tile])
        hold_ref[src_ref[tile] - blocks] = value.astype(BF16)
    for ref, place in ((b_ref, place_b), (a_ref, place_a)):
        for peer in range(GROUP):
            kind = kind_of(place - peer)
            for m in range(cap):
                ref[peer, m] = hold_ref[kind * cap + m]


def local_back_kernel(
    slots, zero_ref, one_ref, two_ref, three_ref, scaled_ref, dst_ref, src_ref, half_ref, acc_ref
):
    for block, piece in home_pieces((zero_ref, one_ref, two_ref, three_ref), 1):
        acc_ref[block] = piece.astype(F32)
    for tile in range(slots, half_ref.shape[0]):
        acc_ref[src_ref[tile]] += dot(scaled_ref[dst_ref[tile]], half_ref[tile])


def finish_kernel(acc_in, a_ref, b_ref, send_ref, out_ref, acc_ref):
    place_a, place_b = places()
    kinds, cap = send_ref.shape
    width = acc_in.shape[2]
    acc_ref[...] = acc_in[...]
    for kind in range(kinds):
        offset = (kind // 2 + 1) * (1 - 2 * (kind % 2))
        row_a = place_a + offset
        row_b = place_b + offset
        for m in range(cap):
            got = jnp.where(inside(row_a), a_ref[bounded(row_a), m], b_ref[bounded(row_b), m])
            acc_ref[send_ref[kind, m]] += got.astype(F32)
    for block in range(acc_ref.shape[0]):
        out_ref[:, block * width : (block + 1) * width] = acc_ref[block].astype(BF16)


def rank(y, z_lo, core, x, z_hi):
    return ((y * Z_LO + z_lo) * CORE + core) * X * Z_HI + x * Z_HI + z_hi


def swap(rows, shift):
    devices = lax.axis_size("blk")
    groups = [
        [(first + shift + i) % devices for i in range(GROUP)] for first in range(0, devices, GROUP)
    ]
    return lax.all_to_all(rows, "blk", 0, 0, axis_index_groups=groups, tiled=False)


def across(rows, bit):
    return lax.ppermute(rows, "blk", [(e, e ^ bit) for e in range(lax.axis_size("blk"))])


def over_x(rows):
    groups = [[x * Z_HI + h for x in range(X)] for h in range(Z_HI)]
    return lax.all_to_all(rows, "col", 0, 0, axis_index_groups=groups, tiled=False)


def along_z(rows, step):
    chips = Z_LO * Z_HI
    route = []
    for y in range(Y):
        for core in range(CORE):
            for x in range(X):
                for z in range(chips):
                    to = (z + step) % chips
                    route.append(
                        (
                            rank(y, z % Z_LO, core, x, z // Z_LO),
                            rank(y, to % Z_LO, core, x, to // Z_LO),
                        )
                    )
    return lax.ppermute(rows, ("blk", "col"), sorted(route))


def per_device(
    node_feats, tile_dst, tile_src, tile_cnt, send_blk, self_weight, neigh_weight, bias, cotangent
):
    dim, nodes = node_feats.shape
    tiles, width = tile_cnt.shape[:2]
    blocks = nodes // width
    table = send_blk[0]
    kinds, cap = table.shape
    slots = kinds * cap
    cols = X * Z_HI
    per_col = blocks // cols
    full = cols * dim
    chunk = 8
    shape = lambda *dims: jax.ShapeDtypeStruct(dims + (dim, width), BF16)
    halo = shape(GROUP, cap)
    step = Z_LO // 2

    send_a, send_b, feats = call(
        functools.partial(pack_kernel, width), (halo, halo, shape(blocks)), [VMEM, SMEM]
    )(node_feats, table)
    got_b = swap(send_b, GROUP // 2)
    xc_plus, xc_minus = call(
        functools.partial(split_kernel, width), (shape(X, 2, per_col),) * 2, [VMEM] * 2
    )(feats, cotangent)
    whole = lambda shape: pl.BlockSpec(shape, lambda i: (0,) * len(shape))
    half, acc = pl.pallas_call(
        functools.partial(local_kernel, slots, chunk),
        grid=(tiles // chunk,),
        out_shape=(
            jax.ShapeDtypeStruct(tile_cnt.shape, BF16),
            jax.ShapeDtypeStruct((blocks, dim + 8, width), F32),
        ),
        in_specs=[
            whole((blocks, dim, width)),
            SMEM,
            SMEM,
            pl.BlockSpec((chunk, width, width), lambda i: (i, 0, 0)),
        ],
        out_specs=(
            pl.BlockSpec((chunk, width, width), lambda i: (i, 0, 0)),
            whole((blocks, dim + 8, width)),
        ),
        compiler_params=pltpu.CompilerParams(vmem_limit_bytes=32 * 2**20),
        cost_estimate=pl.CostEstimate(
            flops=60000000, bytes_accessed=6000000, transcendentals=0
        ),
    )(feats, tile_dst, tile_src, tile_cnt)
    send_a, got_b, xc_plus, xc_minus, half, acc = lax.optimization_barrier(
        (send_a, got_b, xc_plus, xc_minus, half, acc)
    )
    xc_plus = along_z(xc_plus, step)
    xc_minus = along_z(xc_minus, -step)
    got_a = swap(send_a, 0)
    weight_t = jnp.concatenate([self_weight.T, neigh_weight.T], axis=1)
    bias_col = bias[:, None]
    agg_plus, agg_minus, degree = call(
        functools.partial(aggregate_kernel, slots),
        (shape(X, per_col), shape(X, per_col), jax.ShapeDtypeStruct((blocks, 8, width), F32)),
        [VMEM, VMEM, SMEM, SMEM, VMEM, VMEM],
        [pltpu.VMEM((blocks, dim + 8, width), F32)],
    )(got_a, got_b, tile_dst, tile_src, half, acc)
    agg_plus = along_z(agg_plus, step)
    agg_minus = along_z(agg_minus, -step)
    ranged = call(join_kernel, shape(X, 3, 2, per_col), [VMEM] * 4)(
        xc_plus, xc_minus, agg_plus, agg_minus
    )
    ranged = over_x(ranged)
    plus, minus, dz, xa = call(
        node_kernel,
        (
            shape(X, 2, per_col),
            shape(X, 2, per_col),
            jax.ShapeDtypeStruct((full, per_col * width), BF16),
            jax.ShapeDtypeStruct((2 * full, per_col * width), BF16),
        ),
        [VMEM] * 5,
        [
            pltpu.VMEM((full, per_col * width), BF16),
            pltpu.VMEM((2, full, per_col * width), BF16),
        ],
    )(ranged, weight_t, neigh_weight, self_weight, bias_col)
    plus = along_z(plus, step)
    minus = along_z(minus, -step)
    part = call(
        functools.partial(weight_kernel, dim),
        jax.ShapeDtypeStruct((Y * CORE * X, 16, full + 128), BF16),
        [VMEM] * 2,
    )(xa, dz)

    both = ("blk", "col")
    flat = [
        [rank(y, l, c, x, h) for y in range(Y) for c in range(CORE) for x in range(X)]
        for l in range(Z_LO)
        for h in range(Z_HI)
    ]
    line = [
        [rank(y, l, c, x, h) for h in range(Z_HI) for l in range(Z_LO)]
        for y in range(Y)
        for c in range(CORE)
        for x in range(X)
    ]
    part = lax.all_to_all(part, both, 0, 0, axis_index_groups=flat, tiled=False)
    home = call(turn_kernel, (shape(2, 2, per_col),) * X, [VMEM] * 2, cost=(1e10, 1e6))(plus, minus)
    part, *home = lax.optimization_barrier((part, *home))
    (part,) = call(
        fold_kernel, (jax.ShapeDtypeStruct((Z_HI * Z_LO, 8, full + 128), BF16),), [VMEM]
    )(part)
    part = lax.all_to_all(part, both, 0, 0, axis_index_groups=line, tiled=False)
    route = lambda turn: [(c, (c + Z_HI * turn) % cols) for c in range(cols)]
    home = [home[0]] + [lax.ppermute(home[turn], "col", route(turn)) for turn in range(1, X)]
    away_a, away_b, scaled = call(
        functools.partial(contribution_kernel, slots),
        (halo, halo, shape(blocks)),
        [VMEM] * 5 + [SMEM, SMEM, VMEM],
        [pltpu.VMEM((slots, dim, width), BF16)],
    )(*home, degree, tile_dst, tile_src, half)
    row = jax.ShapeDtypeStruct((1, 8, full), F32)
    rows, tail = call(
        lambda part_ref, out_ref, tail_ref: total_kernel(part_ref, out_ref.at[0], tail_ref),
        (row, jax.ShapeDtypeStruct((8, 128), F32)),
        [VMEM],
    )(part)
    grad_bias = jnp.concatenate([tail[0], tail[4]])
    grad_bias = lax.dynamic_slice_in_dim(grad_bias, lax.axis_index("col") * dim, dim, 0)
    away_b, rows = lax.optimization_barrier((away_b, rows))
    back_b = swap(away_b, GROUP // 2)
    for bit in (1, Z_LO * CORE):
        double = jax.ShapeDtypeStruct((2 * rows.shape[0], 8, full), F32)
        rows = call(pair_kernel, double, [VMEM] * 2)(rows, across(rows, bit))
    acc = call(
        functools.partial(local_back_kernel, slots),
        jax.ShapeDtypeStruct((blocks, dim, width), F32),
        [VMEM] * 5 + [SMEM, SMEM, VMEM],
    )(*home, scaled, tile_dst, tile_src, half)
    away_a, back_b, rows, acc = lax.optimization_barrier((away_a, back_b, rows, acc))
    back_a = swap(away_a, 0)
    grad = jax.ShapeDtypeStruct((dim, full), F32)
    grad_self, grad_neigh = call(order_kernel, (grad, grad), [VMEM] * 2)(
        rows, across(rows, 2 * Z_LO * CORE)
    )
    grad_feats = call(
        finish_kernel,
        jax.ShapeDtypeStruct((dim, nodes), BF16),
        [VMEM, VMEM, VMEM, SMEM],
        [pltpu.VMEM((blocks, dim, width), F32)],
    )(acc, back_a, back_b, table)
    return grad_feats, grad_self, grad_neigh, grad_bias


def solution(mesh):
    placed = (
        P("col", "blk"),
        P("blk"),
        P("blk"),
        P("blk", None, None),
        P("blk", None, None),
        P(),
        P(),
        P(),
        P("col", "blk"),
    )
    return jax.shard_map(
        per_device,
        mesh=mesh,
        in_specs=placed,
        out_specs=(P("col", "blk"), P("col", None), P("col", None), P("col")),
        check_vma=False,
    )
```

```python
import functools

import jax
import jax.numpy as jnp
from jax import lax
from jax.experimental import pallas as pl
from jax.experimental.pallas import tpu as pltpu
from jax.sharding import PartitionSpec as P

GROUP = 8
Y, Z_LO, CORE, X, Z_HI = 4, 8, 2, 4, 2
BF16 = jnp.bfloat16
F32 = jnp.float32
FIRST = (((0,), (0,)), ((), ()))
LAST = (((1,), (1,)), ((), ()))
VMEM = pl.BlockSpec(memory_space=pltpu.VMEM)
SMEM = pl.BlockSpec(memory_space=pltpu.SMEM)


def gelu_slope(pre_act):
    inner = 0.7978845608 * (pre_act + 0.044715 * pre_act * pre_act * pre_act)
    tanh_value = jnp.tanh(inner)
    return 0.5 * (1.0 + tanh_value) + 0.5 * pre_act * (
        1.0 - tanh_value * tanh_value
    ) * 0.7978845608 * (1.0 + 3.0 * 0.044715 * pre_act * pre_act)


def dot(left, right, dims=(((1,), (0,)), ((), ()))):
    return lax.dot_general(left, right, dims, preferred_element_type=F32)


def call(body, out_shape, in_specs, scratch=(), cost=(1e7, 1e6)):
    outs = jax.tree.map(lambda _: VMEM, out_shape)
    return pl.pallas_call(
        body,
        out_shape=out_shape,
        in_specs=in_specs,
        out_specs=outs,
        scratch_shapes=scratch,
        compiler_params=pltpu.CompilerParams(vmem_limit_bytes=32 * 2**20),
        cost_estimate=pl.CostEstimate(
            flops=int(cost[0]), bytes_accessed=int(cost[1]), transcendentals=0
        ),
    )


def places():
    blk = lax.axis_index("blk")
    return lax.rem(blk, GROUP), lax.rem(blk + GROUP // 2, GROUP)


def kind_of(distance):
    k = 2 * (jnp.abs(distance) - 1) + jnp.where(distance < 0, 1, 0)
    return jnp.clip(k, 0, 7)


def offset_of(kind):
    return (kind // 2 + 1) * (1 - 2 * lax.rem(kind, 2))


def inside(place):
    return jnp.logical_and(place >= 0, place < GROUP)


def bounded(place):
    return jnp.clip(place, 0, GROUP - 1)


def pack_kernel(width, x_ref, send_ref, b_ref, block_ref):
    place = places()[1]
    for peer in range(GROUP):
        kind = kind_of(peer - place)
        for m in range(send_ref.shape[0]):
            start = pl.multiple_of(send_ref[m, kind] * width, width)
            b_ref[peer, m] = x_ref[:, pl.ds(start, width)]
    for block in range(block_ref.shape[0]):
        block_ref[block] = x_ref[:, block * width : (block + 1) * width]


def near_kernel(x_ref, send_ref, a_ref):
    place = places()[0]
    for peer in range(GROUP):
        kind = kind_of(peer - place)
        for m in range(send_ref.shape[0]):
            a_ref[peer, m] = x_ref[send_ref[m, kind]]


def column():
    col = lax.axis_index("col")
    return col // Z_HI, lax.rem(col, Z_HI)


def range_half():
    z = column()[1] * Z_LO + lax.rem(lax.axis_index("blk") // CORE, Z_LO)
    middle = jnp.logical_and(z >= Z_LO // 2, z < Z_LO // 2 * 3)
    return jnp.where(middle, 0, 1)


def split_kernel(width, x_ref, cot_ref, plus_ref, minus_ref):
    z_hi = column()[1]
    per = plus_ref.shape[2]
    for x in range(X):
        for out, h in ((plus_ref, z_hi), (minus_ref, 1 - z_hi)):
            for p in range(per):
                block = (x * Z_HI + h) * per + p
                start = pl.multiple_of(block * width, width)
                out[x, 0, p] = x_ref[block]
                out[x, 1, p] = cot_ref[:, pl.ds(start, width)]


def join_kernel(xc_plus_ref, xc_minus_ref, agg_plus_ref, agg_minus_ref, out_ref):
    for side, (xc, agg) in enumerate(((xc_plus_ref, agg_plus_ref), (xc_minus_ref, agg_minus_ref))):
        for which in range(2):
            out_ref[:, which, side] = xc[:, which]
        out_ref[:, 2, side] = agg[...]


def turn_kernel(plus_ref, minus_ref, *outs):
    x = column()[0]
    for step, out in enumerate(outs):
        to = lax.rem(x + step, X)
        out[0] = plus_ref[to]
        out[1] = minus_ref[to]


def summed(part_ref):
    total = part_ref[0].astype(F32)
    for i in range(1, part_ref.shape[0]):
        total += part_ref[i].astype(F32)
    return total


def fold_kernel(part_ref, out_ref):
    total = summed(part_ref).astype(BF16)
    halves = out_ref.shape[1] - 1
    for z in range(Z_HI * Z_LO):
        first = z // Z_LO * halves
        for half in range(halves):
            out_ref[z, half] = total[first + half]
        out_ref[z, halves] = total[Z_HI * halves]


def total_kernel(part_ref, out_ref, tail_ref):
    total = summed(part_ref)
    halves = part_ref.shape[1] - 1
    for half in range(halves):
        out_ref[0, :, half * 128 : (half + 1) * 128] = total[half]
    tail_ref[...] = total[halves]


def pair_kernel(one_ref, two_ref, out_ref):
    half = one_ref.shape[0]
    out_ref[:half] = one_ref[...]
    out_ref[half:] = two_ref[...]


def order_kernel(near_ref, far_ref, self_ref, neigh_ref):
    blk = lax.axis_index("blk")
    mine = blk // (Z_LO * CORE) * CORE + lax.rem(blk, CORE)
    for piece in range(Y * CORE):
        offset = jnp.bitwise_xor(mine, piece)
        place = lax.rem(offset, 4)
        rows = jnp.where(offset < 4, near_ref[place], far_ref[place])
        out = self_ref if piece < 4 else neigh_ref
        out[piece % 4 * 8 : piece % 4 * 8 + 8] = rows


def local_kernel(slots, chunk, x_ref, dst_ref, src_ref, cnt_ref, half_ref, acc_ref):
    step = pl.program_id(0)
    width = cnt_ref.shape[1]
    dim = x_ref.shape[1]
    half_ref[...] = cnt_ref[...].astype(F32).astype(BF16)

    @pl.when(step == 0)
    def _():
        acc_ref[...] = jnp.zeros_like(acc_ref)

    @pl.when(step * chunk >= slots)
    def _():
        ones = jnp.ones((16, width), BF16)
        for i in range(chunk):
            tile = step * chunk + i
            rows = jnp.concatenate([x_ref[src_ref[tile]], ones], axis=0)
            dst = dst_ref[tile]
            acc_ref[dst] += dot(rows, half_ref[i], LAST)[: dim + 8]


def aggregate_kernel(
    slots, a_ref, b_ref, dst_ref, src_ref, half_ref, acc_in, plus_ref, minus_ref, deg_ref, acc_ref
):
    place_a, place_b = places()
    z_hi = column()[1]
    cap, dim, width = a_ref.shape[1:]
    blocks = acc_in.shape[0]
    per = plus_ref.shape[1]
    ones = jnp.ones((16, width), BF16)
    acc_ref[...] = acc_in[...]
    for tile in range(slots):
        slot = src_ref[tile] - blocks
        kind = slot // cap
        m = lax.rem(slot, cap)
        row_a = place_a - offset_of(kind)
        row_b = place_b - offset_of(kind)
        got = jnp.where(inside(row_a), a_ref[bounded(row_a), m], b_ref[bounded(row_b), m])
        rows = jnp.concatenate([got, ones], axis=0)
        dst = dst_ref[tile]
        acc_ref[dst] += dot(rows, half_ref[tile], LAST)[: dim + 8]
    for block in range(blocks):
        deg_ref[block] = jnp.maximum(acc_ref[block, dim : dim + 8], 1.0)
    for x in range(X):
        for out, h in ((plus_ref, z_hi), (minus_ref, 1 - z_hi)):
            for p in range(per):
                block = (x * Z_HI + h) * per + p
                out[x, p] = (acc_ref[block, :dim] / deg_ref[block, :1]).astype(BF16)


def node_kernel(
    in_ref, wt_ref, neigh_ref, own_w_ref, bias_ref, plus_ref, minus_ref, dz_ref, xa_ref, cot_ref, home_ref
):
    _, _, sides, per_col, dim, width = in_ref.shape
    full = X * Z_HI * dim
    half = range_half()
    for x in range(X):
        for side, z in ((0, half), (1, 1 - half)):
            start = (x * Z_HI + z) * dim
            rows = pl.ds(pl.multiple_of(start, dim), dim)
            agg_rows = pl.ds(pl.multiple_of(full + start, dim), dim)
            for p in range(per_col):
                lanes = slice(p * width, (p + 1) * width)
                xa_ref[rows, lanes] = in_ref[x, 0, side, p]
                cot_ref[rows, lanes] = in_ref[x, 1, side, p]
                xa_ref[agg_rows, lanes] = in_ref[x, 2, side, p]
    for p in range(per_col):
        lanes = slice(p * width, (p + 1) * width)
        pre = dot(wt_ref[...], xa_ref[:, lanes]) + bias_ref[...]
        dz = (cot_ref[:, lanes].astype(F32) * gelu_slope(pre)).astype(BF16)
        dz_ref[:, lanes] = dz
        home_ref[0, :, lanes] = dot(neigh_ref[...], dz).astype(BF16)
        home_ref[1, :, lanes] = dot(own_w_ref[...], dz).astype(BF16)
    for x in range(X):
        for out, z in ((minus_ref, half), (plus_ref, 1 - half)):
            rows = pl.ds(pl.multiple_of((x * Z_HI + z) * dim, dim), dim)
            for which in range(2):
                for p in range(per_col):
                    out[x, which, p] = home_ref[which, rows, p * width : (p + 1) * width]


def weight_kernel(dim, xa_ref, dz_ref, part_ref):
    full = dz_ref.shape[0]
    grads = dot(xa_ref[...], dz_ref[...], LAST)
    total = dot(jnp.ones((16, dz_ref.shape[1]), BF16), dz_ref[...], LAST)
    tail = jnp.concatenate([total[:4, :128], total[4:8, 128:]], axis=0).astype(BF16)
    halves = full // 128
    for which in range(2):
        for quarter in range(4):
            for x in range(X):
                piece = (which * 4 + quarter) * X + x
                for z in range(Z_HI):
                    start = which * full + (x * Z_HI + z) * dim + quarter * 8
                    for half in range(halves):
                        tile = grads[start : start + 8, half * 128 : (half + 1) * 128]
                        part_ref[piece, z * halves + half] = tile.astype(BF16)
                part_ref[piece, Z_HI * halves] = tail


def home_pieces(refs, which):
    x, z_hi = column()
    per = refs[0].shape[2]
    for step, ref in enumerate(refs):
        source = lax.rem(x + X - step, X)
        for side, h in ((0, 1 - z_hi), (1, z_hi)):
            for p in range(per):
                yield (source * Z_HI + h) * per + p, ref[side, which, p]


def contribution_kernel(
    slots, zero_ref, one_ref, two_ref, three_ref, deg_ref, dst_ref, src_ref, half_ref, *outs
):
    a_ref, b_ref, scaled_ref, hold_ref = outs
    place_a, place_b = places()
    blocks = scaled_ref.shape[0]
    cap = a_ref.shape[1]
    for block, piece in home_pieces((zero_ref, one_ref, two_ref, three_ref), 0):
        scaled_ref[block] = (piece.astype(F32) / deg_ref[block][:1]).astype(BF16)
    for tile in range(slots):
        value = dot(scaled_ref[dst_ref[tile]], half_ref[tile])
        hold_ref[src_ref[tile] - blocks] = value.astype(BF16)
    for ref, place in ((b_ref, place_b), (a_ref, place_a)):
        for peer in range(GROUP):
            kind = kind_of(place - peer)
            for m in range(cap):
                ref[peer, m] = hold_ref[kind * cap + m]


def local_back_kernel(
    slots, zero_ref, one_ref, two_ref, three_ref, scaled_ref, dst_ref, src_ref, half_ref, acc_ref
):
    for block, piece in home_pieces((zero_ref, one_ref, two_ref, three_ref), 1):
        acc_ref[block] = piece.astype(F32)
    for tile in range(slots, half_ref.shape[0]):
        acc_ref[src_ref[tile]] += dot(scaled_ref[dst_ref[tile]], half_ref[tile])


def finish_kernel(acc_in, a_ref, b_ref, send_ref, out_ref, acc_ref):
    place_a, place_b = places()
    cap, kinds = send_ref.shape
    width = acc_in.shape[2]
    acc_ref[...] = acc_in[...]
    for kind in range(kinds):
        offset = (kind // 2 + 1) * (1 - 2 * (kind % 2))
        row_a = place_a + offset
        row_b = place_b + offset
        for m in range(cap):
            got = jnp.where(inside(row_a), a_ref[bounded(row_a), m], b_ref[bounded(row_b), m])
            acc_ref[send_ref[m, kind]] += got.astype(F32)
    for block in range(acc_ref.shape[0]):
        out_ref[:, block * width : (block + 1) * width] = acc_ref[block].astype(BF16)


def rank(y, z_lo, core, x, z_hi):
    return ((y * Z_LO + z_lo) * CORE + core) * X * Z_HI + x * Z_HI + z_hi


def swap(rows, shift):
    devices = lax.axis_size("blk")
    groups = [
        [(first + shift + i) % devices for i in range(GROUP)] for first in range(0, devices, GROUP)
    ]
    return lax.all_to_all(rows, "blk", 0, 0, axis_index_groups=groups, tiled=False)


def across(rows, bit):
    return lax.ppermute(rows, "blk", [(e, e ^ bit) for e in range(lax.axis_size("blk"))])


def over_x(rows):
    groups = [[x * Z_HI + h for x in range(X)] for h in range(Z_HI)]
    return lax.all_to_all(rows, "col", 0, 0, axis_index_groups=groups, tiled=False)


def along_z(rows, step):
    chips = Z_LO * Z_HI
    route = []
    for y in range(Y):
        for core in range(CORE):
            for x in range(X):
                for z in range(chips):
                    to = (z + step) % chips
                    route.append(
                        (
                            rank(y, z % Z_LO, core, x, z // Z_LO),
                            rank(y, to % Z_LO, core, x, to // Z_LO),
                        )
                    )
    return lax.ppermute(rows, ("blk", "col"), sorted(route))


def per_device(
    node_feats, tile_dst, tile_src, tile_cnt, send_blk, self_weight, neigh_weight, bias, cotangent
):
    dim, nodes = node_feats.shape
    tiles, width = tile_cnt.shape[:2]
    blocks = nodes // width
    table = send_blk[0].T
    cap, kinds = table.shape
    slots = kinds * cap
    cols = X * Z_HI
    per_col = blocks // cols
    full = cols * dim
    chunk = 8
    shape = lambda *dims: jax.ShapeDtypeStruct(dims + (dim, width), BF16)
    halo = shape(GROUP, cap)
    step = Z_LO // 2

    send_b, feats = call(
        functools.partial(pack_kernel, width), (halo, shape(blocks)), [VMEM, SMEM]
    )(node_feats, table)
    got_b = swap(send_b, GROUP // 2)
    send_a = call(near_kernel, halo, [VMEM, SMEM])(feats, table)
    xc_plus, xc_minus = call(
        functools.partial(split_kernel, width), (shape(X, 2, per_col),) * 2, [VMEM] * 2
    )(feats, cotangent)
    whole = lambda shape: pl.BlockSpec(shape, lambda i: (0,) * len(shape))
    half, acc = pl.pallas_call(
        functools.partial(local_kernel, slots, chunk),
        grid=(tiles // chunk,),
        out_shape=(
            jax.ShapeDtypeStruct(tile_cnt.shape, BF16),
            jax.ShapeDtypeStruct((blocks, dim + 8, width), F32),
        ),
        in_specs=[
            whole((blocks, dim, width)),
            SMEM,
            SMEM,
            pl.BlockSpec((chunk, width, width), lambda i: (i, 0, 0)),
        ],
        out_specs=(
            pl.BlockSpec((chunk, width, width), lambda i: (i, 0, 0)),
            whole((blocks, dim + 8, width)),
        ),
        compiler_params=pltpu.CompilerParams(vmem_limit_bytes=32 * 2**20),
        cost_estimate=pl.CostEstimate(
            flops=60000000, bytes_accessed=6000000, transcendentals=0
        ),
    )(feats, tile_dst, tile_src, tile_cnt)
    send_a, got_b, xc_plus, xc_minus, half, acc = lax.optimization_barrier(
        (send_a, got_b, xc_plus, xc_minus, half, acc)
    )
    xc_plus = along_z(xc_plus, step)
    xc_minus = along_z(xc_minus, -step)
    got_a = swap(send_a, 0)
    weight_t = jnp.concatenate([self_weight.T, neigh_weight.T], axis=1)
    bias_col = bias[:, None]
    agg_plus, agg_minus, degree = call(
        functools.partial(aggregate_kernel, slots),
        (shape(X, per_col), shape(X, per_col), jax.ShapeDtypeStruct((blocks, 8, width), F32)),
        [VMEM, VMEM, SMEM, SMEM, VMEM, VMEM],
        [pltpu.VMEM((blocks, dim + 8, width), F32)],
    )(got_a, got_b, tile_dst, tile_src, half, acc)
    agg_plus = along_z(agg_plus, step)
    agg_minus = along_z(agg_minus, -step)
    ranged = call(join_kernel, shape(X, 3, 2, per_col), [VMEM] * 4)(
        xc_plus, xc_minus, agg_plus, agg_minus
    )
    ranged = over_x(ranged)
    plus, minus, dz, xa = call(
        node_kernel,
        (
            shape(X, 2, per_col),
            shape(X, 2, per_col),
            jax.ShapeDtypeStruct((full, per_col * width), BF16),
            jax.ShapeDtypeStruct((2 * full, per_col * width), BF16),
        ),
        [VMEM] * 5,
        [
            pltpu.VMEM((full, per_col * width), BF16),
            pltpu.VMEM((2, full, per_col * width), BF16),
        ],
    )(ranged, weight_t, neigh_weight, self_weight, bias_col)
    plus = along_z(plus, step)
    minus = along_z(minus, -step)
    part = call(
        functools.partial(weight_kernel, dim),
        jax.ShapeDtypeStruct((Y * CORE * X, Z_HI * full // 128 + 1, 8, 128), BF16),
        [VMEM] * 2,
    )(xa, dz)

    both = ("blk", "col")
    flat = [
        [rank(y, l, c, x, h) for y in range(Y) for c in range(CORE) for x in range(X)]
        for l in range(Z_LO)
        for h in range(Z_HI)
    ]
    line = [
        [rank(y, l, c, x, h) for h in range(Z_HI) for l in range(Z_LO)]
        for y in range(Y)
        for c in range(CORE)
        for x in range(X)
    ]
    part = lax.all_to_all(part, both, 0, 0, axis_index_groups=flat, tiled=False)
    home = call(turn_kernel, (shape(2, 2, per_col),) * X, [VMEM] * 2, cost=(1e10, 1e6))(plus, minus)
    part, *home = lax.optimization_barrier((part, *home))
    (part,) = call(
        fold_kernel, (jax.ShapeDtypeStruct((Z_HI * Z_LO, full // 128 + 1, 8, 128), BF16),), [VMEM]
    )(part)
    part = lax.all_to_all(part, both, 0, 0, axis_index_groups=line, tiled=False)
    route = lambda turn: [(c, (c + Z_HI * turn) % cols) for c in range(cols)]
    home = [home[0]] + [lax.ppermute(home[turn], "col", route(turn)) for turn in range(1, X)]
    away_a, away_b, scaled = call(
        functools.partial(contribution_kernel, slots),
        (halo, halo, shape(blocks)),
        [VMEM] * 5 + [SMEM, SMEM, VMEM],
        [pltpu.VMEM((slots, dim, width), BF16)],
    )(*home, degree, tile_dst, tile_src, half)
    row = jax.ShapeDtypeStruct((1, 8, full), F32)
    rows, tail = call(
        total_kernel,
        (row, jax.ShapeDtypeStruct((8, 128), F32)),
        [VMEM],
    )(part)
    grad_bias = jnp.concatenate([tail[0], tail[4]])
    grad_bias = lax.dynamic_slice_in_dim(grad_bias, lax.axis_index("col") * dim, dim, 0)
    away_b, rows = lax.optimization_barrier((away_b, rows))
    back_b = swap(away_b, GROUP // 2)
    for bit in (1, Z_LO * CORE):
        double = jax.ShapeDtypeStruct((2 * rows.shape[0], 8, full), F32)
        rows = call(pair_kernel, double, [VMEM] * 2)(rows, across(rows, bit))
    acc = call(
        functools.partial(local_back_kernel, slots),
        jax.ShapeDtypeStruct((blocks, dim, width), F32),
        [VMEM] * 5 + [SMEM, SMEM, VMEM],
    )(*home, scaled, tile_dst, tile_src, half)
    away_a, back_b, rows = lax.optimization_barrier((away_a, back_b, rows))
    back_a = swap(away_a, 0)
    grad = jax.ShapeDtypeStruct((dim, full), F32)
    grad_self, grad_neigh = call(order_kernel, (grad, grad), [VMEM] * 2)(
        rows, across(rows, 2 * Z_LO * CORE)
    )
    grad_feats = call(
        finish_kernel,
        jax.ShapeDtypeStruct((dim, nodes), BF16),
        [VMEM, VMEM, VMEM, SMEM],
        [pltpu.VMEM((blocks, dim, width), F32)],
    )(acc, back_a, back_b, table)
    return grad_feats, grad_self, grad_neigh, grad_bias


def solution(mesh):
    placed = (
        P("col", "blk"),
        P("blk"),
        P("blk"),
        P("blk", None, None),
        P("blk", None, None),
        P(),
        P(),
        P(),
        P("col", "blk"),
    )
    return jax.shard_map(
        per_device,
        mesh=mesh,
        in_specs=placed,
        out_specs=(P("col", "blk"), P("col", None), P("col", None), P("col")),
        check_vma=False,
    )
```

```python
import functools

import jax
import jax.numpy as jnp
from jax import lax
from jax.experimental import pallas as pl
from jax.experimental.pallas import tpu as pltpu
from jax.sharding import PartitionSpec as P

GROUP = 8
Y, Z_LO, CORE, X, Z_HI = 4, 8, 2, 4, 2
BF16 = jnp.bfloat16
F32 = jnp.float32
FIRST = (((0,), (0,)), ((), ()))
LAST = (((1,), (1,)), ((), ()))
VMEM = pl.BlockSpec(memory_space=pltpu.VMEM)
SMEM = pl.BlockSpec(memory_space=pltpu.SMEM)


def gelu_slope(pre_act):
    inner = 0.7978845608 * (pre_act + 0.044715 * pre_act * pre_act * pre_act)
    tanh_value = jnp.tanh(inner)
    return 0.5 * (1.0 + tanh_value) + 0.5 * pre_act * (
        1.0 - tanh_value * tanh_value
    ) * 0.7978845608 * (1.0 + 3.0 * 0.044715 * pre_act * pre_act)


def dot(left, right, dims=(((1,), (0,)), ((), ()))):
    return lax.dot_general(left, right, dims, preferred_element_type=F32)


def call(body, out_shape, in_specs, scratch=(), cost=(1e7, 1e6)):
    outs = jax.tree.map(lambda _: VMEM, out_shape)
    return pl.pallas_call(
        body,
        out_shape=out_shape,
        in_specs=in_specs,
        out_specs=outs,
        scratch_shapes=scratch,
        compiler_params=pltpu.CompilerParams(vmem_limit_bytes=32 * 2**20),
        cost_estimate=pl.CostEstimate(
            flops=int(cost[0]), bytes_accessed=int(cost[1]), transcendentals=0
        ),
    )


def places():
    blk = lax.axis_index("blk")
    return lax.rem(blk, GROUP), lax.rem(blk + GROUP // 2, GROUP)


def kind_of(distance):
    k = 2 * (jnp.abs(distance) - 1) + jnp.where(distance < 0, 1, 0)
    return jnp.clip(k, 0, 7)


def offset_of(kind):
    return (kind // 2 + 1) * (1 - 2 * lax.rem(kind, 2))


def inside(place):
    return jnp.logical_and(place >= 0, place < GROUP)


def bounded(place):
    return jnp.clip(place, 0, GROUP - 1)


def pack_kernel(width, x_hbm, send_hbm, a_ref, b_ref, block_ref, x_ref, send_ref, sems):
    copies = (
        pltpu.make_async_copy(x_hbm, x_ref, sems.at[0]),
        pltpu.make_async_copy(send_hbm, send_ref, sems.at[1]),
    )
    for copy in copies:
        copy.start()
    for copy in copies:
        copy.wait()
    for block in range(block_ref.shape[0]):
        block_ref[block] = x_ref[:, block * width : (block + 1) * width]
    place_a, place_b = places()
    for ref, place in ((b_ref, place_b), (a_ref, place_a)):
        for peer in range(GROUP):
            kind = kind_of(peer - place)
            for m in range(send_ref.shape[0]):
                start = pl.multiple_of(send_ref[m, kind] * width, width)
                ref[peer, m] = x_ref[:, pl.ds(start, width)]


def column():
    col = lax.axis_index("col")
    return col // Z_HI, lax.rem(col, Z_HI)


def range_half():
    z = column()[1] * Z_LO + lax.rem(lax.axis_index("blk") // CORE, Z_LO)
    middle = jnp.logical_and(z >= Z_LO // 2, z < Z_LO // 2 * 3)
    return jnp.where(middle, 0, 1)


def split_kernel(width, x_ref, cot_ref, plus_ref, minus_ref):
    z_hi = column()[1]
    per = plus_ref.shape[2]
    for x in range(X):
        for out, h in ((plus_ref, z_hi), (minus_ref, 1 - z_hi)):
            for p in range(per):
                block = (x * Z_HI + h) * per + p
                start = pl.multiple_of(block * width, width)
                out[x, 0, p] = x_ref[block]
                out[x, 1, p] = cot_ref[:, pl.ds(start, width)]


def join_kernel(xc_plus_ref, xc_minus_ref, agg_plus_ref, agg_minus_ref, out_ref):
    for side, (xc, agg) in enumerate(((xc_plus_ref, agg_plus_ref), (xc_minus_ref, agg_minus_ref))):
        for which in range(2):
            out_ref[:, which, side] = xc[:, which]
        out_ref[:, 2, side] = agg[...]


def turn_kernel(plus_ref, minus_ref, *outs):
    x = column()[0]
    for step, out in enumerate(outs):
        to = lax.rem(x + step, X)
        out[0] = plus_ref[to]
        out[1] = minus_ref[to]


def summed(part_ref):
    total = part_ref[0].astype(F32)
    for i in range(1, part_ref.shape[0]):
        total += part_ref[i].astype(F32)
    return total


def fold_kernel(part_ref, out_ref):
    total = summed(part_ref).astype(BF16)
    halves = out_ref.shape[1] - 1
    for z in range(Z_HI * Z_LO):
        first = z // Z_LO * halves
        for half in range(halves):
            out_ref[z, half] = total[first + half]
        out_ref[z, halves] = total[Z_HI * halves]


def total_kernel(part_ref, out_ref, tail_ref):
    total = summed(part_ref)
    halves = part_ref.shape[1] - 1
    for half in range(halves):
        out_ref[0, :, half * 128 : (half + 1) * 128] = total[half]
    tail_ref[...] = total[halves]


def pair_kernel(one_ref, two_ref, out_ref):
    half = one_ref.shape[0]
    out_ref[:half] = one_ref[...]
    out_ref[half:] = two_ref[...]


def order_kernel(near_ref, far_ref, self_ref, neigh_ref):
    blk = lax.axis_index("blk")
    mine = blk // (Z_LO * CORE) * CORE + lax.rem(blk, CORE)
    for piece in range(Y * CORE):
        offset = jnp.bitwise_xor(mine, piece)
        place = lax.rem(offset, 4)
        rows = jnp.where(offset < 4, near_ref[place], far_ref[place])
        out = self_ref if piece < 4 else neigh_ref
        out[piece % 4 * 8 : piece % 4 * 8 + 8] = rows


def local_kernel(slots, chunk, x_ref, ends_ref, cnt_ref, half_ref, acc_ref):
    dst_ref, src_ref = ends_ref.at[0], ends_ref.at[1]
    step = pl.program_id(0)
    width = cnt_ref.shape[1]
    dim = x_ref.shape[1]
    half_ref[...] = cnt_ref[...].astype(F32).astype(BF16)

    @pl.when(step == 0)
    def _():
        acc_ref[...] = jnp.zeros_like(acc_ref)

    @pl.when(step * chunk >= slots)
    def _():
        ones = jnp.ones((16, width), BF16)
        for i in range(chunk):
            tile = step * chunk + i
            rows = jnp.concatenate([x_ref[src_ref[tile]], ones], axis=0)
            dst = dst_ref[tile]
            acc_ref[dst] += dot(rows, half_ref[i], LAST)[: dim + 8]


def aggregate_kernel(
    slots, a_ref, b_ref, ends_ref, half_ref, acc_in, plus_ref, minus_ref, deg_ref, acc_ref
):
    dst_ref, src_ref = ends_ref.at[0], ends_ref.at[1]
    place_a, place_b = places()
    z_hi = column()[1]
    cap, dim, width = a_ref.shape[1:]
    blocks = acc_in.shape[0]
    per = plus_ref.shape[1]
    ones = jnp.ones((16, width), BF16)
    acc_ref[...] = acc_in[...]
    for tile in range(slots):
        slot = src_ref[tile] - blocks
        kind = slot // cap
        m = lax.rem(slot, cap)
        row_a = place_a - offset_of(kind)
        row_b = place_b - offset_of(kind)
        got = jnp.where(inside(row_a), a_ref[bounded(row_a), m], b_ref[bounded(row_b), m])
        rows = jnp.concatenate([got, ones], axis=0)
        dst = dst_ref[tile]
        acc_ref[dst] += dot(rows, half_ref[tile], LAST)[: dim + 8]
    for block in range(blocks):
        deg_ref[block] = jnp.maximum(acc_ref[block, dim : dim + 8], 1.0)
    for x in range(X):
        for out, h in ((plus_ref, z_hi), (minus_ref, 1 - z_hi)):
            for p in range(per):
                block = (x * Z_HI + h) * per + p
                out[x, p] = (acc_ref[block, :dim] / deg_ref[block, :1]).astype(BF16)


def node_kernel(
    in_ref, wt_ref, neigh_ref, own_w_ref, bias_ref, plus_ref, minus_ref, dz_ref, xa_ref, cot_ref, home_ref
):
    _, _, sides, per_col, dim, width = in_ref.shape
    full = X * Z_HI * dim
    half = range_half()
    for x in range(X):
        for side, z in ((0, half), (1, 1 - half)):
            start = (x * Z_HI + z) * dim
            rows = pl.ds(pl.multiple_of(start, dim), dim)
            agg_rows = pl.ds(pl.multiple_of(full + start, dim), dim)
            for p in range(per_col):
                lanes = slice(p * width, (p + 1) * width)
                xa_ref[rows, lanes] = in_ref[x, 0, side, p]
                cot_ref[rows, lanes] = in_ref[x, 1, side, p]
                xa_ref[agg_rows, lanes] = in_ref[x, 2, side, p]
    for p in range(per_col):
        lanes = slice(p * width, (p + 1) * width)
        pre = dot(wt_ref[...], xa_ref[:, lanes]) + bias_ref[...]
        dz = (cot_ref[:, lanes].astype(F32) * gelu_slope(pre)).astype(BF16)
        dz_ref[:, lanes] = dz
        home_ref[0, :, lanes] = dot(neigh_ref[...], dz).astype(BF16)
        home_ref[1, :, lanes] = dot(own_w_ref[...], dz).astype(BF16)
    for x in range(X):
        for out, z in ((minus_ref, half), (plus_ref, 1 - half)):
            rows = pl.ds(pl.multiple_of((x * Z_HI + z) * dim, dim), dim)
            for which in range(2):
                for p in range(per_col):
                    out[x, which, p] = home_ref[which, rows, p * width : (p + 1) * width]


def weight_kernel(dim, xa_ref, dz_ref, part_ref):
    full = dz_ref.shape[0]
    grads = dot(xa_ref[...], dz_ref[...], LAST)
    total = dot(jnp.ones((16, dz_ref.shape[1]), BF16), dz_ref[...], LAST)
    tail = jnp.concatenate([total[:4, :128], total[4:8, 128:]], axis=0).astype(BF16)
    halves = full // 128
    for which in range(2):
        for quarter in range(4):
            for x in range(X):
                piece = (which * 4 + quarter) * X + x
                for z in range(Z_HI):
                    start = which * full + (x * Z_HI + z) * dim + quarter * 8
                    for half in range(halves):
                        tile = grads[start : start + 8, half * 128 : (half + 1) * 128]
                        part_ref[piece, z * halves + half] = tile.astype(BF16)
                part_ref[piece, Z_HI * halves] = tail


def home_pieces(refs, which):
    x, z_hi = column()
    per = refs[0].shape[2]
    for step, ref in enumerate(refs):
        source = lax.rem(x + X - step, X)
        for side, h in ((0, 1 - z_hi), (1, z_hi)):
            for p in range(per):
                yield (source * Z_HI + h) * per + p, ref[side, which, p]


def contribution_kernel(
    slots, zero_ref, one_ref, two_ref, three_ref, deg_ref, ends_ref, half_ref, *outs
):
    dst_ref, src_ref = ends_ref.at[0], ends_ref.at[1]
    a_ref, b_ref, scaled_ref, hold_ref = outs
    place_a, place_b = places()
    blocks = scaled_ref.shape[0]
    cap = a_ref.shape[1]
    for block, piece in home_pieces((zero_ref, one_ref, two_ref, three_ref), 0):
        scaled_ref[block] = (piece.astype(F32) / deg_ref[block][:1]).astype(BF16)
    for tile in range(slots):
        value = dot(scaled_ref[dst_ref[tile]], half_ref[tile])
        hold_ref[src_ref[tile] - blocks] = value.astype(BF16)
    for ref, place in ((b_ref, place_b), (a_ref, place_a)):
        for peer in range(GROUP):
            kind = kind_of(place - peer)
            for m in range(cap):
                ref[peer, m] = hold_ref[kind * cap + m]


def local_back_kernel(
    slots, zero_ref, one_ref, two_ref, three_ref, scaled_ref, ends_ref, half_ref, acc_ref
):
    dst_ref, src_ref = ends_ref.at[0], ends_ref.at[1]
    for block, piece in home_pieces((zero_ref, one_ref, two_ref, three_ref), 1):
        acc_ref[block] = piece.astype(F32)
    for tile in range(slots, half_ref.shape[0]):
        acc_ref[src_ref[tile]] += dot(scaled_ref[dst_ref[tile]], half_ref[tile])


def finish_kernel(acc_in, a_ref, b_ref, send_ref, out_ref, acc_ref):
    place_a, place_b = places()
    cap, kinds = send_ref.shape
    width = acc_in.shape[2]
    acc_ref[...] = acc_in[...]
    for kind in range(kinds):
        offset = (kind // 2 + 1) * (1 - 2 * (kind % 2))
        row_a = place_a + offset
        row_b = place_b + offset
        for m in range(cap):
            got = jnp.where(inside(row_a), a_ref[bounded(row_a), m], b_ref[bounded(row_b), m])
            acc_ref[send_ref[m, kind]] += got.astype(F32)
    for block in range(acc_ref.shape[0]):
        out_ref[:, block * width : (block + 1) * width] = acc_ref[block].astype(BF16)


def rank(y, z_lo, core, x, z_hi):
    return ((y * Z_LO + z_lo) * CORE + core) * X * Z_HI + x * Z_HI + z_hi


def swap(rows, shift):
    devices = lax.axis_size("blk")
    groups = [
        [(first + shift + i) % devices for i in range(GROUP)] for first in range(0, devices, GROUP)
    ]
    return lax.all_to_all(rows, "blk", 0, 0, axis_index_groups=groups, tiled=False)


def across(rows, bit):
    return lax.ppermute(rows, "blk", [(e, e ^ bit) for e in range(lax.axis_size("blk"))])


def over_x(rows):
    groups = [[x * Z_HI + h for x in range(X)] for h in range(Z_HI)]
    return lax.all_to_all(rows, "col", 0, 0, axis_index_groups=groups, tiled=False)


def along_z(rows, step):
    chips = Z_LO * Z_HI
    route = []
    for y in range(Y):
        for core in range(CORE):
            for x in range(X):
                for z in range(chips):
                    to = (z + step) % chips
                    route.append(
                        (
                            rank(y, z % Z_LO, core, x, z // Z_LO),
                            rank(y, to % Z_LO, core, x, to // Z_LO),
                        )
                    )
    return lax.ppermute(rows, ("blk", "col"), sorted(route))


def per_device(
    node_feats, tile_dst, tile_src, tile_cnt, send_blk, self_weight, neigh_weight, bias, cotangent
):
    dim, nodes = node_feats.shape
    tiles, width = tile_cnt.shape[:2]
    blocks = nodes // width
    table = send_blk[0].T
    ends = jnp.stack([tile_dst, tile_src])
    cap, kinds = table.shape
    slots = kinds * cap
    cols = X * Z_HI
    per_col = blocks // cols
    full = cols * dim
    chunk = 8
    shape = lambda *dims: jax.ShapeDtypeStruct(dims + (dim, width), BF16)
    halo = shape(GROUP, cap)
    step = Z_LO // 2

    hbm = pl.BlockSpec(memory_space=pltpu.HBM)
    send_a, send_b, feats = call(
        functools.partial(pack_kernel, width),
        (halo, halo, shape(blocks)),
        [hbm, hbm],
        [
            pltpu.VMEM((dim, nodes), BF16),
            pltpu.SMEM((cap, kinds), jnp.int32),
            pltpu.SemaphoreType.DMA((2,)),
        ],
    )(node_feats, table)
    got_b = swap(send_b, GROUP // 2)
    xc_plus, xc_minus = call(
        functools.partial(split_kernel, width), (shape(X, 2, per_col),) * 2, [VMEM] * 2
    )(feats, cotangent)
    whole = lambda shape: pl.BlockSpec(shape, lambda i: (0,) * len(shape))
    half, acc = pl.pallas_call(
        functools.partial(local_kernel, slots, chunk),
        grid=(tiles // chunk,),
        out_shape=(
            jax.ShapeDtypeStruct(tile_cnt.shape, BF16),
            jax.ShapeDtypeStruct((blocks, dim + 8, width), F32),
        ),
        in_specs=[
            whole((blocks, dim, width)),
            SMEM,
            pl.BlockSpec((chunk, width, width), lambda i: (i, 0, 0)),
        ],
        out_specs=(
            pl.BlockSpec((chunk, width, width), lambda i: (i, 0, 0)),
            whole((blocks, dim + 8, width)),
        ),
        compiler_params=pltpu.CompilerParams(vmem_limit_bytes=32 * 2**20),
        cost_estimate=pl.CostEstimate(
            flops=60000000, bytes_accessed=6000000, transcendentals=0
        ),
    )(feats, ends, tile_cnt)
    send_a, got_b, xc_plus, xc_minus, half, acc = lax.optimization_barrier(
        (send_a, got_b, xc_plus, xc_minus, half, acc)
    )
    xc_plus = along_z(xc_plus, step)
    xc_minus = along_z(xc_minus, -step)
    got_a = swap(send_a, 0)
    weight_t = jnp.concatenate([self_weight.T, neigh_weight.T], axis=1)
    bias_col = bias[:, None]
    agg_plus, agg_minus, degree = call(
        functools.partial(aggregate_kernel, slots),
        (shape(X, per_col), shape(X, per_col), jax.ShapeDtypeStruct((blocks, 8, width), F32)),
        [VMEM, VMEM, SMEM, VMEM, VMEM],
        [pltpu.VMEM((blocks, dim + 8, width), F32)],
    )(got_a, got_b, ends, half, acc)
    agg_plus = along_z(agg_plus, step)
    agg_minus = along_z(agg_minus, -step)
    ranged = call(join_kernel, shape(X, 3, 2, per_col), [VMEM] * 4)(
        xc_plus, xc_minus, agg_plus, agg_minus
    )
    ranged = over_x(ranged)
    plus, minus, dz, xa = call(
        node_kernel,
        (
            shape(X, 2, per_col),
            shape(X, 2, per_col),
            jax.ShapeDtypeStruct((full, per_col * width), BF16),
            jax.ShapeDtypeStruct((2 * full, per_col * width), BF16),
        ),
        [VMEM] * 5,
        [
            pltpu.VMEM((full, per_col * width), BF16),
            pltpu.VMEM((2, full, per_col * width), BF16),
        ],
    )(ranged, weight_t, neigh_weight, self_weight, bias_col)
    plus = along_z(plus, step)
    minus = along_z(minus, -step)
    part = call(
        functools.partial(weight_kernel, dim),
        jax.ShapeDtypeStruct((Y * CORE * X, Z_HI * full // 128 + 1, 8, 128), BF16),
        [VMEM] * 2,
    )(xa, dz)

    both = ("blk", "col")
    flat = [
        [rank(y, l, c, x, h) for y in range(Y) for c in range(CORE) for x in range(X)]
        for l in range(Z_LO)
        for h in range(Z_HI)
    ]
    line = [
        [rank(y, l, c, x, h) for h in range(Z_HI) for l in range(Z_LO)]
        for y in range(Y)
        for c in range(CORE)
        for x in range(X)
    ]
    part = lax.all_to_all(part, both, 0, 0, axis_index_groups=flat, tiled=False)
    home = call(turn_kernel, (shape(2, 2, per_col),) * X, [VMEM] * 2, cost=(1e10, 1e6))(plus, minus)
    part, *home = lax.optimization_barrier((part, *home))
    (part,) = call(
        fold_kernel, (jax.ShapeDtypeStruct((Z_HI * Z_LO, full // 128 + 1, 8, 128), BF16),), [VMEM]
    )(part)
    part = lax.all_to_all(part, both, 0, 0, axis_index_groups=line, tiled=False)
    route = lambda turn: [(c, (c + Z_HI * turn) % cols) for c in range(cols)]
    home = [home[0]] + [lax.ppermute(home[turn], "col", route(turn)) for turn in range(1, X)]
    away_a, away_b, scaled = call(
        functools.partial(contribution_kernel, slots),
        (halo, halo, shape(blocks)),
        [VMEM] * 5 + [SMEM, VMEM],
        [pltpu.VMEM((slots, dim, width), BF16)],
    )(*home, degree, ends, half)
    row = jax.ShapeDtypeStruct((1, 8, full), F32)
    rows, tail = call(
        total_kernel,
        (row, jax.ShapeDtypeStruct((8, 128), F32)),
        [VMEM],
    )(part)
    grad_bias = jnp.concatenate([tail[0], tail[4]])
    grad_bias = lax.dynamic_slice_in_dim(grad_bias, lax.axis_index("col") * dim, dim, 0)
    away_b, rows = lax.optimization_barrier((away_b, rows))
    back_b = swap(away_b, GROUP // 2)
    for bit in (1, Z_LO * CORE):
        double = jax.ShapeDtypeStruct((2 * rows.shape[0], 8, full), F32)
        rows = call(pair_kernel, double, [VMEM] * 2)(rows, across(rows, bit))
    acc = call(
        functools.partial(local_back_kernel, slots),
        jax.ShapeDtypeStruct((blocks, dim, width), F32),
        [VMEM] * 5 + [SMEM, VMEM],
    )(*home, scaled, ends, half)
    away_a, back_b, rows = lax.optimization_barrier((away_a, back_b, rows))
    back_a = swap(away_a, 0)
    grad = jax.ShapeDtypeStruct((dim, full), F32)
    grad_self, grad_neigh = call(order_kernel, (grad, grad), [VMEM] * 2)(
        rows, across(rows, 2 * Z_LO * CORE)
    )
    grad_feats = call(
        finish_kernel,
        jax.ShapeDtypeStruct((dim, nodes), BF16),
        [VMEM, VMEM, VMEM, SMEM],
        [pltpu.VMEM((blocks, dim, width), F32)],
    )(acc, back_a, back_b, table)
    return grad_feats, grad_self, grad_neigh, grad_bias


def solution(mesh):
    placed = (
        P("col", "blk"),
        P("blk"),
        P("blk"),
        P("blk", None, None),
        P("blk", None, None),
        P(),
        P(),
        P(),
        P("col", "blk"),
    )
    return jax.shard_map(
        per_device,
        mesh=mesh,
        in_specs=placed,
        out_specs=(P("col", "blk"), P("col", None), P("col", None), P("col")),
        check_vma=False,
    )
```

```python
import functools

import jax
import jax.numpy as jnp
from jax import lax
from jax.experimental import pallas as pl
from jax.experimental.pallas import tpu as pltpu
from jax.sharding import PartitionSpec as P

GROUP = 8
Y, Z_LO, CORE, X, Z_HI = 4, 8, 2, 4, 2
BF16 = jnp.bfloat16
F32 = jnp.float32
FIRST = (((0,), (0,)), ((), ()))
LAST = (((1,), (1,)), ((), ()))
VMEM = pl.BlockSpec(memory_space=pltpu.VMEM)
SMEM = pl.BlockSpec(memory_space=pltpu.SMEM)


def gelu_slope(pre_act):
    inner = 0.7978845608 * (pre_act + 0.044715 * pre_act * pre_act * pre_act)
    tanh_value = jnp.tanh(inner)
    return 0.5 * (1.0 + tanh_value) + 0.5 * pre_act * (
        1.0 - tanh_value * tanh_value
    ) * 0.7978845608 * (1.0 + 3.0 * 0.044715 * pre_act * pre_act)


def dot(left, right, dims=(((1,), (0,)), ((), ()))):
    return lax.dot_general(left, right, dims, preferred_element_type=F32)


def call(body, out_shape, in_specs, scratch=(), cost=(1e7, 1e6)):
    outs = jax.tree.map(lambda _: VMEM, out_shape)
    return pl.pallas_call(
        body,
        out_shape=out_shape,
        in_specs=in_specs,
        out_specs=outs,
        scratch_shapes=scratch,
        compiler_params=pltpu.CompilerParams(vmem_limit_bytes=32 * 2**20),
        cost_estimate=pl.CostEstimate(
            flops=int(cost[0]), bytes_accessed=int(cost[1]), transcendentals=0
        ),
    )


def places():
    blk = lax.axis_index("blk")
    return lax.rem(blk, GROUP), lax.rem(blk + GROUP // 2, GROUP)


def kind_of(distance):
    k = 2 * (jnp.abs(distance) - 1) + jnp.where(distance < 0, 1, 0)
    return jnp.clip(k, 0, 7)


def offset_of(kind):
    return (kind // 2 + 1) * (1 - 2 * lax.rem(kind, 2))


def inside(place):
    return jnp.logical_and(place >= 0, place < GROUP)


def bounded(place):
    return jnp.clip(place, 0, GROUP - 1)


def pack_kernel(width, x_hbm, send_hbm, a_ref, b_ref, block_ref, x_ref, send_ref, sems):
    copies = (
        pltpu.make_async_copy(x_hbm, x_ref, sems.at[0]),
        pltpu.make_async_copy(send_hbm, send_ref, sems.at[1]),
    )
    for copy in copies:
        copy.start()
    for copy in copies:
        copy.wait()
    for block in range(block_ref.shape[0]):
        block_ref[block] = x_ref[:, block * width : (block + 1) * width]
    place_a, place_b = places()
    for ref, place in ((b_ref, place_b), (a_ref, place_a)):
        for peer in range(GROUP):
            kind = kind_of(peer - place)
            for m in range(send_ref.shape[0]):
                start = pl.multiple_of(send_ref[m, kind] * width, width)
                ref[peer, m] = x_ref[:, pl.ds(start, width)]


def column():
    col = lax.axis_index("col")
    return col // Z_HI, lax.rem(col, Z_HI)


def range_half():
    z = column()[1] * Z_LO + lax.rem(lax.axis_index("blk") // CORE, Z_LO)
    middle = jnp.logical_and(z >= Z_LO // 2, z < Z_LO // 2 * 3)
    return jnp.where(middle, 0, 1)


def split_kernel(width, x_ref, cot_ref, plus_ref, minus_ref):
    z_hi = column()[1]
    per = plus_ref.shape[2]
    for x in range(X):
        for out, h in ((plus_ref, z_hi), (minus_ref, 1 - z_hi)):
            for p in range(per):
                block = (x * Z_HI + h) * per + p
                start = pl.multiple_of(block * width, width)
                out[x, 0, p] = x_ref[block]
                out[x, 1, p] = cot_ref[:, pl.ds(start, width)]


def join_kernel(xc_plus_ref, xc_minus_ref, agg_plus_ref, agg_minus_ref, out_ref):
    for side, (xc, agg) in enumerate(((xc_plus_ref, agg_plus_ref), (xc_minus_ref, agg_minus_ref))):
        for which in range(2):
            out_ref[:, which, side] = xc[:, which]
        out_ref[:, 2, side] = agg[...]


def turn_kernel(plus_ref, minus_ref, *outs):
    x = column()[0]
    for step, out in enumerate(outs):
        to = lax.rem(x + step, X)
        out[0] = plus_ref[to]
        out[1] = minus_ref[to]


def summed(part_ref):
    total = part_ref[0].astype(F32)
    for i in range(1, part_ref.shape[0]):
        total += part_ref[i].astype(F32)
    return total


def fold_kernel(part_ref, out_ref):
    total = summed(part_ref).astype(BF16)
    halves = out_ref.shape[1] - 1
    for z in range(Z_HI * Z_LO):
        first = z // Z_LO * halves
        for half in range(halves):
            out_ref[z, half] = total[first + half]
        out_ref[z, halves] = total[Z_HI * halves]


def total_kernel(part_ref, out_ref, tail_ref):
    total = summed(part_ref)
    halves = part_ref.shape[1] - 1
    for half in range(halves):
        out_ref[0, :, half * 128 : (half + 1) * 128] = total[half]
    tail_ref[...] = total[halves]


def pair_kernel(one_ref, two_ref, out_ref):
    half = one_ref.shape[0]
    out_ref[:half] = one_ref[...]
    out_ref[half:] = two_ref[...]


def order_kernel(near_ref, far_ref, self_ref, neigh_ref):
    blk = lax.axis_index("blk")
    mine = blk // (Z_LO * CORE) * CORE + lax.rem(blk, CORE)
    for piece in range(Y * CORE):
        offset = jnp.bitwise_xor(mine, piece)
        place = lax.rem(offset, 4)
        rows = jnp.where(offset < 4, near_ref[place], far_ref[place])
        out = self_ref if piece < 4 else neigh_ref
        out[piece % 4 * 8 : piece % 4 * 8 + 8] = rows


def local_kernel(slots, chunk, x_ref, ends_ref, cnt_ref, half_ref, acc_ref):
    dst_ref, src_ref = ends_ref.at[0], ends_ref.at[1]
    step = pl.program_id(0)
    width = cnt_ref.shape[1]
    dim = x_ref.shape[1]
    half_ref[...] = cnt_ref[...].astype(F32).astype(BF16)

    @pl.when(step == 0)
    def _():
        acc_ref[...] = jnp.zeros_like(acc_ref)

    @pl.when(step * chunk >= slots)
    def _():
        ones = jnp.ones((16, width), BF16)
        for i in range(chunk):
            tile = step * chunk + i
            rows = jnp.concatenate([x_ref[src_ref[tile]], ones], axis=0)
            dst = dst_ref[tile]
            acc_ref[dst] += dot(rows, half_ref[i], LAST)[: dim + 8]


def aggregate_kernel(
    slots, a_ref, b_ref, ends_ref, half_ref, acc_in, plus_ref, minus_ref, deg_ref, acc_ref
):
    dst_ref, src_ref = ends_ref.at[0], ends_ref.at[1]
    place_a, place_b = places()
    z_hi = column()[1]
    cap, dim, width = a_ref.shape[1:]
    blocks = acc_in.shape[0]
    per = plus_ref.shape[1]
    ones = jnp.ones((16, width), BF16)
    acc_ref[...] = acc_in[...]
    for tile in range(slots):
        slot = src_ref[tile] - blocks
        kind = slot // cap
        m = lax.rem(slot, cap)
        row_a = place_a - offset_of(kind)
        row_b = place_b - offset_of(kind)
        got = jnp.where(inside(row_a), a_ref[bounded(row_a), m], b_ref[bounded(row_b), m])
        rows = jnp.concatenate([got, ones], axis=0)
        dst = dst_ref[tile]
        acc_ref[dst] += dot(rows, half_ref[tile], LAST)[: dim + 8]
    for block in range(blocks):
        deg_ref[block] = jnp.maximum(acc_ref[block, dim : dim + 8], 1.0)
    for x in range(X):
        for out, h in ((plus_ref, z_hi), (minus_ref, 1 - z_hi)):
            for p in range(per):
                block = (x * Z_HI + h) * per + p
                out[x, p] = (acc_ref[block, :dim] / deg_ref[block, :1]).astype(BF16)


def node_kernel(
    in_ref, wt_ref, neigh_ref, own_w_ref, bias_ref, plus_ref, minus_ref, dz_ref, xa_ref, cot_ref, home_ref
):
    _, _, sides, per_col, dim, width = in_ref.shape
    full = X * Z_HI * dim
    half = range_half()
    for x in range(X):
        for side, z in ((0, half), (1, 1 - half)):
            start = (x * Z_HI + z) * dim
            rows = pl.ds(pl.multiple_of(start, dim), dim)
            agg_rows = pl.ds(pl.multiple_of(full + start, dim), dim)
            for p in range(per_col):
                lanes = slice(p * width, (p + 1) * width)
                xa_ref[rows, lanes] = in_ref[x, 0, side, p]
                cot_ref[rows, lanes] = in_ref[x, 1, side, p]
                xa_ref[agg_rows, lanes] = in_ref[x, 2, side, p]
    for p in range(per_col):
        lanes = slice(p * width, (p + 1) * width)
        pre = dot(wt_ref[...], xa_ref[:, lanes]) + bias_ref[...]
        dz = (cot_ref[:, lanes].astype(F32) * gelu_slope(pre)).astype(BF16)
        dz_ref[:, lanes] = dz
        home_ref[0, :, lanes] = dot(neigh_ref[...], dz).astype(BF16)
        home_ref[1, :, lanes] = dot(own_w_ref[...], dz).astype(BF16)
    for x in range(X):
        for out, z in ((minus_ref, half), (plus_ref, 1 - half)):
            rows = pl.ds(pl.multiple_of((x * Z_HI + z) * dim, dim), dim)
            for which in range(2):
                for p in range(per_col):
                    out[x, which, p] = home_ref[which, rows, p * width : (p + 1) * width]


def weight_kernel(dim, xa_ref, dz_ref, part_ref):
    full = dz_ref.shape[0]
    grads = dot(xa_ref[...], dz_ref[...], LAST)
    total = dot(jnp.ones((16, dz_ref.shape[1]), BF16), dz_ref[...], LAST)
    tail = jnp.concatenate([total[:4, :128], total[4:8, 128:]], axis=0).astype(BF16)
    halves = full // 128
    for which in range(2):
        for quarter in range(4):
            for x in range(X):
                piece = (which * 4 + quarter) * X + x
                for z in range(Z_HI):
                    start = which * full + (x * Z_HI + z) * dim + quarter * 8
                    for half in range(halves):
                        tile = grads[start : start + 8, half * 128 : (half + 1) * 128]
                        part_ref[piece, z * halves + half] = tile.astype(BF16)
                part_ref[piece, Z_HI * halves] = tail


def home_pieces(refs, which):
    x, z_hi = column()
    per = refs[0].shape[2]
    for step, ref in enumerate(refs):
        source = lax.rem(x + X - step, X)
        for side, h in ((0, 1 - z_hi), (1, z_hi)):
            for p in range(per):
                yield (source * Z_HI + h) * per + p, ref[side, which, p]


def contribution_kernel(
    slots, zero_ref, one_ref, two_ref, three_ref, deg_ref, ends_ref, half_ref, *outs
):
    dst_ref, src_ref = ends_ref.at[0], ends_ref.at[1]
    a_ref, b_ref, scaled_ref, hold_ref = outs
    place_a, place_b = places()
    blocks = scaled_ref.shape[0]
    cap = a_ref.shape[1]
    for block, piece in home_pieces((zero_ref, one_ref, two_ref, three_ref), 0):
        scaled_ref[block] = (piece.astype(F32) / deg_ref[block][:1]).astype(BF16)
    for tile in range(slots):
        value = dot(scaled_ref[dst_ref[tile]], half_ref[tile])
        hold_ref[src_ref[tile] - blocks] = value.astype(BF16)
    for ref, place in ((b_ref, place_b), (a_ref, place_a)):
        for peer in range(GROUP):
            kind = kind_of(place - peer)
            for m in range(cap):
                ref[peer, m] = hold_ref[kind * cap + m]


def local_back_kernel(
    slots, zero_ref, one_ref, two_ref, three_ref, scaled_ref, ends_ref, half_ref, acc_ref
):
    dst_ref, src_ref = ends_ref.at[0], ends_ref.at[1]
    for block, piece in home_pieces((zero_ref, one_ref, two_ref, three_ref), 1):
        acc_ref[block] = piece.astype(F32)
    for tile in range(slots, half_ref.shape[0]):
        acc_ref[src_ref[tile]] += dot(scaled_ref[dst_ref[tile]], half_ref[tile])


def finish_kernel(acc_in, a_ref, b_ref, send_ref, out_ref, acc_ref):
    place_a, place_b = places()
    cap, kinds = send_ref.shape
    width = acc_in.shape[2]
    acc_ref[...] = acc_in[...]
    for kind in range(kinds):
        offset = (kind // 2 + 1) * (1 - 2 * (kind % 2))
        row_a = place_a + offset
        row_b = place_b + offset
        for m in range(cap):
            got = jnp.where(inside(row_a), a_ref[bounded(row_a), m], b_ref[bounded(row_b), m])
            acc_ref[send_ref[m, kind]] += got.astype(F32)
    for block in range(acc_ref.shape[0]):
        out_ref[:, block * width : (block + 1) * width] = acc_ref[block].astype(BF16)


def rank(y, z_lo, core, x, z_hi):
    return ((y * Z_LO + z_lo) * CORE + core) * X * Z_HI + x * Z_HI + z_hi


def swap(rows, shift):
    devices = lax.axis_size("blk")
    groups = [
        [(first + shift + i) % devices for i in range(GROUP)] for first in range(0, devices, GROUP)
    ]
    return lax.all_to_all(rows, "blk", 0, 0, axis_index_groups=groups, tiled=False)


def across(rows, bit):
    return lax.ppermute(rows, "blk", [(e, e ^ bit) for e in range(lax.axis_size("blk"))])


def over_x(rows):
    groups = [[x * Z_HI + h for x in range(X)] for h in range(Z_HI)]
    return lax.all_to_all(rows, "col", 0, 0, axis_index_groups=groups, tiled=False)


def along_z(rows, step):
    chips = Z_LO * Z_HI
    route = []
    for y in range(Y):
        for core in range(CORE):
            for x in range(X):
                for z in range(chips):
                    to = (z + step) % chips
                    route.append(
                        (
                            rank(y, z % Z_LO, core, x, z // Z_LO),
                            rank(y, to % Z_LO, core, x, to // Z_LO),
                        )
                    )
    return lax.ppermute(rows, ("blk", "col"), sorted(route))


def per_device(
    node_feats, tile_dst, tile_src, tile_cnt, send_blk, self_weight, neigh_weight, bias, cotangent
):
    dim, nodes = node_feats.shape
    tiles, width = tile_cnt.shape[:2]
    blocks = nodes // width
    table = send_blk[0].T
    ends = jnp.stack([tile_dst, tile_src])
    cap, kinds = table.shape
    slots = kinds * cap
    cols = X * Z_HI
    per_col = blocks // cols
    full = cols * dim
    chunk = 8
    shape = lambda *dims: jax.ShapeDtypeStruct(dims + (dim, width), BF16)
    halo = shape(GROUP, cap)
    step = Z_LO // 2

    hbm = pl.BlockSpec(memory_space=pltpu.HBM)
    send_a, send_b, feats = call(
        functools.partial(pack_kernel, width),
        (halo, halo, shape(blocks)),
        [hbm, hbm],
        [
            pltpu.VMEM((dim, nodes), BF16),
            pltpu.SMEM((cap, kinds), jnp.int32),
            pltpu.SemaphoreType.DMA((2,)),
        ],
    )(node_feats, table)
    got_a = swap(send_a, 0)
    xc_plus, xc_minus = call(
        functools.partial(split_kernel, width), (shape(X, 2, per_col),) * 2, [VMEM] * 2
    )(feats, cotangent)
    whole = lambda shape: pl.BlockSpec(shape, lambda i: (0,) * len(shape))
    half, acc = pl.pallas_call(
        functools.partial(local_kernel, slots, chunk),
        grid=(tiles // chunk,),
        out_shape=(
            jax.ShapeDtypeStruct(tile_cnt.shape, BF16),
            jax.ShapeDtypeStruct((blocks, dim + 8, width), F32),
        ),
        in_specs=[
            whole((blocks, dim, width)),
            SMEM,
            pl.BlockSpec((chunk, width, width), lambda i: (i, 0, 0)),
        ],
        out_specs=(
            pl.BlockSpec((chunk, width, width), lambda i: (i, 0, 0)),
            whole((blocks, dim + 8, width)),
        ),
        compiler_params=pltpu.CompilerParams(vmem_limit_bytes=32 * 2**20),
        cost_estimate=pl.CostEstimate(
            flops=60000000, bytes_accessed=6000000, transcendentals=0
        ),
    )(feats, ends, tile_cnt)
    send_b, got_a, xc_plus, xc_minus, half, acc = lax.optimization_barrier(
        (send_b, got_a, xc_plus, xc_minus, half, acc)
    )
    xc_plus = along_z(xc_plus, step)
    xc_minus = along_z(xc_minus, -step)
    got_b = swap(send_b, GROUP // 2)
    weight_t = jnp.concatenate([self_weight.T, neigh_weight.T], axis=1)
    bias_col = bias[:, None]
    agg_plus, agg_minus, degree = call(
        functools.partial(aggregate_kernel, slots),
        (shape(X, per_col), shape(X, per_col), jax.ShapeDtypeStruct((blocks, 8, width), F32)),
        [VMEM, VMEM, SMEM, VMEM, VMEM],
        [pltpu.VMEM((blocks, dim + 8, width), F32)],
    )(got_a, got_b, ends, half, acc)
    agg_plus = along_z(agg_plus, step)
    agg_minus = along_z(agg_minus, -step)
    ranged = call(join_kernel, shape(X, 3, 2, per_col), [VMEM] * 4)(
        xc_plus, xc_minus, agg_plus, agg_minus
    )
    ranged = over_x(ranged)
    plus, minus, dz, xa = call(
        node_kernel,
        (
            shape(X, 2, per_col),
            shape(X, 2, per_col),
            jax.ShapeDtypeStruct((full, per_col * width), BF16),
            jax.ShapeDtypeStruct((2 * full, per_col * width), BF16),
        ),
        [VMEM] * 5,
        [
            pltpu.VMEM((full, per_col * width), BF16),
            pltpu.VMEM((2, full, per_col * width), BF16),
        ],
    )(ranged, weight_t, neigh_weight, self_weight, bias_col)
    plus = along_z(plus, step)
    minus = along_z(minus, -step)
    part = call(
        functools.partial(weight_kernel, dim),
        jax.ShapeDtypeStruct((Y * CORE * X, Z_HI * full // 128 + 1, 8, 128), BF16),
        [VMEM] * 2,
    )(xa, dz)

    both = ("blk", "col")
    flat = [
        [rank(y, l, c, x, h) for y in range(Y) for c in range(CORE) for x in range(X)]
        for l in range(Z_LO)
        for h in range(Z_HI)
    ]
    line = [
        [rank(y, l, c, x, h) for h in range(Z_HI) for l in range(Z_LO)]
        for y in range(Y)
        for c in range(CORE)
        for x in range(X)
    ]
    part = lax.all_to_all(part, both, 0, 0, axis_index_groups=flat, tiled=False)
    home = call(turn_kernel, (shape(2, 2, per_col),) * X, [VMEM] * 2, cost=(1e10, 1e6))(plus, minus)
    part, *home = lax.optimization_barrier((part, *home))
    (part,) = call(
        fold_kernel, (jax.ShapeDtypeStruct((Z_HI * Z_LO, full // 128 + 1, 8, 128), BF16),), [VMEM]
    )(part)
    part = lax.all_to_all(part, both, 0, 0, axis_index_groups=line, tiled=False)
    route = lambda turn: [(c, (c + Z_HI * turn) % cols) for c in range(cols)]
    home = [home[0]] + [lax.ppermute(home[turn], "col", route(turn)) for turn in range(1, X)]
    away_a, away_b, scaled = call(
        functools.partial(contribution_kernel, slots),
        (halo, halo, shape(blocks)),
        [VMEM] * 5 + [SMEM, VMEM],
        [pltpu.VMEM((slots, dim, width), BF16)],
    )(*home, degree, ends, half)
    row = jax.ShapeDtypeStruct((1, 8, full), F32)
    rows, tail = call(
        total_kernel,
        (row, jax.ShapeDtypeStruct((8, 128), F32)),
        [VMEM],
    )(part)
    grad_bias = jnp.concatenate([tail[0], tail[4]])
    grad_bias = lax.dynamic_slice_in_dim(grad_bias, lax.axis_index("col") * dim, dim, 0)
    away_a, rows = lax.optimization_barrier((away_a, rows))
    back_a = swap(away_a, 0)
    for bit in (1, Z_LO * CORE):
        double = jax.ShapeDtypeStruct((2 * rows.shape[0], 8, full), F32)
        rows = call(pair_kernel, double, [VMEM] * 2)(rows, across(rows, bit))
    acc = call(
        functools.partial(local_back_kernel, slots),
        jax.ShapeDtypeStruct((blocks, dim, width), F32),
        [VMEM] * 5 + [SMEM, VMEM],
    )(*home, scaled, ends, half)
    away_b, back_a, rows = lax.optimization_barrier((away_b, back_a, rows))
    back_b = swap(away_b, GROUP // 2)
    grad = jax.ShapeDtypeStruct((dim, full), F32)
    grad_self, grad_neigh = call(order_kernel, (grad, grad), [VMEM] * 2)(
        rows, across(rows, 2 * Z_LO * CORE)
    )
    grad_feats = call(
        finish_kernel,
        jax.ShapeDtypeStruct((dim, nodes), BF16),
        [VMEM, VMEM, VMEM, SMEM],
        [pltpu.VMEM((blocks, dim, width), F32)],
    )(acc, back_a, back_b, table)
    return grad_feats, grad_self, grad_neigh, grad_bias


def solution(mesh):
    placed = (
        P("col", "blk"),
        P("blk"),
        P("blk"),
        P("blk", None, None),
        P("blk", None, None),
        P(),
        P(),
        P(),
        P("col", "blk"),
    )
    return jax.shard_map(
        per_device,
        mesh=mesh,
        in_specs=placed,
        out_specs=(P("col", "blk"), P("col", None), P("col", None), P("col")),
        check_vma=False,
    )
```

```python
import functools

import jax
import jax.numpy as jnp
from jax import lax
from jax.experimental import pallas as pl
from jax.experimental.pallas import tpu as pltpu
from jax.sharding import PartitionSpec as P

GROUP = 8
Y, Z_LO, CORE, X, Z_HI = 4, 8, 2, 4, 2
BF16 = jnp.bfloat16
F32 = jnp.float32
FIRST = (((0,), (0,)), ((), ()))
LAST = (((1,), (1,)), ((), ()))
VMEM = pl.BlockSpec(memory_space=pltpu.VMEM)
SMEM = pl.BlockSpec(memory_space=pltpu.SMEM)


def gelu_slope(pre_act):
    inner = 0.7978845608 * (pre_act + 0.044715 * pre_act * pre_act * pre_act)
    tanh_value = jnp.tanh(inner)
    return 0.5 * (1.0 + tanh_value) + 0.5 * pre_act * (
        1.0 - tanh_value * tanh_value
    ) * 0.7978845608 * (1.0 + 3.0 * 0.044715 * pre_act * pre_act)


def dot(left, right, dims=(((1,), (0,)), ((), ()))):
    return lax.dot_general(left, right, dims, preferred_element_type=F32)


def call(body, out_shape, in_specs, scratch=(), cost=(1e7, 1e6), room=32):
    outs = jax.tree.map(lambda _: VMEM, out_shape)
    return pl.pallas_call(
        body,
        out_shape=out_shape,
        in_specs=in_specs,
        out_specs=outs,
        scratch_shapes=scratch,
        compiler_params=pltpu.CompilerParams(vmem_limit_bytes=room * 2**20),
        cost_estimate=pl.CostEstimate(
            flops=int(cost[0]), bytes_accessed=int(cost[1]), transcendentals=0
        ),
    )


def places():
    blk = lax.axis_index("blk")
    return lax.rem(blk, GROUP), lax.rem(blk + GROUP // 2, GROUP)


def kind_of(distance):
    k = 2 * (jnp.abs(distance) - 1) + jnp.where(distance < 0, 1, 0)
    return jnp.clip(k, 0, 7)


def offset_of(kind):
    return (kind // 2 + 1) * (1 - 2 * lax.rem(kind, 2))


def inside(place):
    return jnp.logical_and(place >= 0, place < GROUP)


def bounded(place):
    return jnp.clip(place, 0, GROUP - 1)


def pack_kernel(width, x_hbm, send_hbm, a_ref, b_ref, block_ref, x_ref, send_ref, sems):
    copies = (
        pltpu.make_async_copy(x_hbm, x_ref, sems.at[0]),
        pltpu.make_async_copy(send_hbm, send_ref, sems.at[1]),
    )
    for copy in copies:
        copy.start()
    for copy in copies:
        copy.wait()
    for block in range(block_ref.shape[0]):
        block_ref[block] = x_ref[:, block * width : (block + 1) * width]
    place_a, place_b = places()
    for ref, place in ((b_ref, place_b), (a_ref, place_a)):
        for peer in range(GROUP):
            kind = kind_of(peer - place)
            for m in range(send_ref.shape[0]):
                start = pl.multiple_of(send_ref[m, kind] * width, width)
                ref[peer, m] = x_ref[:, pl.ds(start, width)]


def column():
    col = lax.axis_index("col")
    return col // Z_HI, lax.rem(col, Z_HI)


def range_half():
    z = column()[1] * Z_LO + lax.rem(lax.axis_index("blk") // CORE, Z_LO)
    middle = jnp.logical_and(z >= Z_LO // 2, z < Z_LO // 2 * 3)
    return jnp.where(middle, 0, 1)


def split_kernel(width, x_ref, cot_ref, plus_ref, minus_ref):
    z_hi = column()[1]
    per = plus_ref.shape[2]
    for x in range(X):
        for out, h in ((plus_ref, z_hi), (minus_ref, 1 - z_hi)):
            for p in range(per):
                block = (x * Z_HI + h) * per + p
                start = pl.multiple_of(block * width, width)
                out[x, 0, p] = x_ref[block]
                out[x, 1, p] = cot_ref[:, pl.ds(start, width)]


def join_kernel(xc_plus_ref, xc_minus_ref, agg_plus_ref, agg_minus_ref, out_ref):
    for side, (xc, agg) in enumerate(((xc_plus_ref, agg_plus_ref), (xc_minus_ref, agg_minus_ref))):
        for which in range(2):
            out_ref[:, which, side] = xc[:, which]
        out_ref[:, 2, side] = agg[...]


def turn_kernel(plus_ref, minus_ref, *outs):
    x = column()[0]
    for step, out in enumerate(outs):
        to = lax.rem(x + step, X)
        out[0] = plus_ref[to]
        out[1] = minus_ref[to]


def summed(part_ref):
    total = part_ref[0].astype(F32)
    for i in range(1, part_ref.shape[0]):
        total += part_ref[i].astype(F32)
    return total


def fold_kernel(part_ref, out_ref):
    total = summed(part_ref).astype(BF16)
    halves = out_ref.shape[1] - 1
    for z in range(Z_HI * Z_LO):
        first = z // Z_LO * halves
        for half in range(halves):
            out_ref[z, half] = total[first + half]
        out_ref[z, halves] = total[Z_HI * halves]


def total_kernel(part_ref, out_ref, tail_ref):
    total = summed(part_ref)
    halves = part_ref.shape[1] - 1
    for half in range(halves):
        out_ref[0, :, half * 128 : (half + 1) * 128] = total[half]
    tail_ref[...] = total[halves]


def pair_kernel(one_ref, two_ref, out_ref):
    half = one_ref.shape[0]
    out_ref[:half] = one_ref[...]
    out_ref[half:] = two_ref[...]


def order_kernel(near_ref, far_ref, self_ref, neigh_ref):
    blk = lax.axis_index("blk")
    mine = blk // (Z_LO * CORE) * CORE + lax.rem(blk, CORE)
    for piece in range(Y * CORE):
        offset = jnp.bitwise_xor(mine, piece)
        place = lax.rem(offset, 4)
        rows = jnp.where(offset < 4, near_ref[place], far_ref[place])
        out = self_ref if piece < 4 else neigh_ref
        out[piece % 4 * 8 : piece % 4 * 8 + 8] = rows


def local_kernel(slots, chunk, x_ref, ends_ref, cnt_ref, half_ref, acc_ref):
    dst_ref, src_ref = ends_ref.at[0], ends_ref.at[1]
    step = pl.program_id(0)
    width = cnt_ref.shape[1]
    dim = x_ref.shape[1]
    half_ref[...] = cnt_ref[...].astype(F32).astype(BF16)

    @pl.when(step == 0)
    def _():
        acc_ref[...] = jnp.zeros_like(acc_ref)

    @pl.when(step * chunk >= slots)
    def _():
        ones = jnp.ones((16, width), BF16)
        for i in range(chunk):
            tile = step * chunk + i
            rows = jnp.concatenate([x_ref[src_ref[tile]], ones], axis=0)
            dst = dst_ref[tile]
            acc_ref[dst] += dot(rows, half_ref[i], LAST)[: dim + 8]


def aggregate_kernel(
    slots, a_ref, b_ref, ends_ref, half_ref, acc_in, plus_ref, minus_ref, deg_ref, acc_ref
):
    dst_ref, src_ref = ends_ref.at[0], ends_ref.at[1]
    place_a, place_b = places()
    z_hi = column()[1]
    cap, dim, width = a_ref.shape[1:]
    blocks = acc_in.shape[0]
    per = plus_ref.shape[1]
    ones = jnp.ones((16, width), BF16)
    acc_ref[...] = acc_in[...]
    for tile in range(slots):
        slot = src_ref[tile] - blocks
        kind = slot // cap
        m = lax.rem(slot, cap)
        row_a = place_a - offset_of(kind)
        row_b = place_b - offset_of(kind)
        got = jnp.where(inside(row_a), a_ref[bounded(row_a), m], b_ref[bounded(row_b), m])
        rows = jnp.concatenate([got, ones], axis=0)
        dst = dst_ref[tile]
        acc_ref[dst] += dot(rows, half_ref[tile], LAST)[: dim + 8]
    for block in range(blocks):
        deg_ref[block] = jnp.maximum(acc_ref[block, dim : dim + 8], 1.0)
    for x in range(X):
        for out, h in ((plus_ref, z_hi), (minus_ref, 1 - z_hi)):
            for p in range(per):
                block = (x * Z_HI + h) * per + p
                out[x, p] = (acc_ref[block, :dim] / deg_ref[block, :1]).astype(BF16)


def node_kernel(
    in_ref, wt_ref, neigh_ref, own_w_ref, bias_ref, plus_ref, minus_ref, dz_ref, xa_ref, cot_ref, home_ref
):
    _, _, sides, per_col, dim, width = in_ref.shape
    full = X * Z_HI * dim
    half = range_half()
    for x in range(X):
        for side, z in ((0, half), (1, 1 - half)):
            start = (x * Z_HI + z) * dim
            rows = pl.ds(pl.multiple_of(start, dim), dim)
            agg_rows = pl.ds(pl.multiple_of(full + start, dim), dim)
            for p in range(per_col):
                lanes = slice(p * width, (p + 1) * width)
                xa_ref[rows, lanes] = in_ref[x, 0, side, p]
                cot_ref[rows, lanes] = in_ref[x, 1, side, p]
                xa_ref[agg_rows, lanes] = in_ref[x, 2, side, p]
    for p in range(per_col):
        lanes = slice(p * width, (p + 1) * width)
        pre = dot(wt_ref[...], xa_ref[:, lanes]) + bias_ref[...]
        dz = (cot_ref[:, lanes].astype(F32) * gelu_slope(pre)).astype(BF16)
        dz_ref[:, lanes] = dz
        home_ref[0, :, lanes] = dot(neigh_ref[...], dz).astype(BF16)
        home_ref[1, :, lanes] = dot(own_w_ref[...], dz).astype(BF16)
    for x in range(X):
        for out, z in ((minus_ref, half), (plus_ref, 1 - half)):
            rows = pl.ds(pl.multiple_of((x * Z_HI + z) * dim, dim), dim)
            for which in range(2):
                for p in range(per_col):
                    out[x, which, p] = home_ref[which, rows, p * width : (p + 1) * width]


def weight_kernel(dim, xa_ref, dz_ref, part_ref):
    full = dz_ref.shape[0]
    grads = dot(xa_ref[...], dz_ref[...], LAST)
    total = dot(jnp.ones((16, dz_ref.shape[1]), BF16), dz_ref[...], LAST)
    tail = jnp.concatenate([total[:4, :128], total[4:8, 128:]], axis=0).astype(BF16)
    halves = full // 128
    for which in range(2):
        for quarter in range(4):
            for x in range(X):
                piece = (which * 4 + quarter) * X + x
                for z in range(Z_HI):
                    start = which * full + (x * Z_HI + z) * dim + quarter * 8
                    for half in range(halves):
                        tile = grads[start : start + 8, half * 128 : (half + 1) * 128]
                        part_ref[piece, z * halves + half] = tile.astype(BF16)
                part_ref[piece, Z_HI * halves] = tail


def home_pieces(refs, which):
    x, z_hi = column()
    per = refs[0].shape[2]
    for step, ref in enumerate(refs):
        source = lax.rem(x + X - step, X)
        for side, h in ((0, 1 - z_hi), (1, z_hi)):
            for p in range(per):
                yield (source * Z_HI + h) * per + p, ref[side, which, p]


def contribution_kernel(
    slots, zero_ref, one_ref, two_ref, three_ref, deg_ref, ends_ref, half_ref, *outs
):
    dst_ref, src_ref = ends_ref.at[0], ends_ref.at[1]
    a_ref, b_ref, scaled_ref, hold_ref = outs
    place_a, place_b = places()
    blocks = scaled_ref.shape[0]
    cap = a_ref.shape[1]
    for block, piece in home_pieces((zero_ref, one_ref, two_ref, three_ref), 0):
        scaled_ref[block] = (piece.astype(F32) / deg_ref[block][:1]).astype(BF16)
    for tile in range(slots):
        value = dot(scaled_ref[dst_ref[tile]], half_ref[tile])
        hold_ref[src_ref[tile] - blocks] = value.astype(BF16)
    for ref, place in ((b_ref, place_b), (a_ref, place_a)):
        for peer in range(GROUP):
            kind = kind_of(place - peer)
            for m in range(cap):
                ref[peer, m] = hold_ref[kind * cap + m]


def local_back_kernel(
    slots, zero_ref, one_ref, two_ref, three_ref, scaled_ref, ends_ref, half_ref, acc_ref
):
    dst_ref, src_ref = ends_ref.at[0], ends_ref.at[1]
    for block, piece in home_pieces((zero_ref, one_ref, two_ref, three_ref), 1):
        acc_ref[block] = piece.astype(F32)
    for tile in range(slots, half_ref.shape[0]):
        acc_ref[src_ref[tile]] += dot(scaled_ref[dst_ref[tile]], half_ref[tile])


def finish_kernel(acc_in, a_ref, b_ref, send_ref, out_ref, acc_ref):
    place_a, place_b = places()
    cap, kinds = send_ref.shape
    width = acc_in.shape[2]
    acc_ref[...] = acc_in[...]
    for kind in range(kinds):
        offset = (kind // 2 + 1) * (1 - 2 * (kind % 2))
        row_a = place_a + offset
        row_b = place_b + offset
        for m in range(cap):
            got = jnp.where(inside(row_a), a_ref[bounded(row_a), m], b_ref[bounded(row_b), m])
            acc_ref[send_ref[m, kind]] += got.astype(F32)
    for block in range(acc_ref.shape[0]):
        out_ref[:, block * width : (block + 1) * width] = acc_ref[block].astype(BF16)


def rank(y, z_lo, core, x, z_hi):
    return ((y * Z_LO + z_lo) * CORE + core) * X * Z_HI + x * Z_HI + z_hi


def swap(rows, shift):
    devices = lax.axis_size("blk")
    groups = [
        [(first + shift + i) % devices for i in range(GROUP)] for first in range(0, devices, GROUP)
    ]
    return lax.all_to_all(rows, "blk", 0, 0, axis_index_groups=groups, tiled=False)


def across(rows, bit):
    return lax.ppermute(rows, "blk", [(e, e ^ bit) for e in range(lax.axis_size("blk"))])


def over_x(rows):
    groups = [[x * Z_HI + h for x in range(X)] for h in range(Z_HI)]
    return lax.all_to_all(rows, "col", 0, 0, axis_index_groups=groups, tiled=False)


def along_z(rows, step):
    chips = Z_LO * Z_HI
    route = []
    for y in range(Y):
        for core in range(CORE):
            for x in range(X):
                for z in range(chips):
                    to = (z + step) % chips
                    route.append(
                        (
                            rank(y, z % Z_LO, core, x, z // Z_LO),
                            rank(y, to % Z_LO, core, x, to // Z_LO),
                        )
                    )
    return lax.ppermute(rows, ("blk", "col"), sorted(route))


def per_device(
    node_feats, tile_dst, tile_src, tile_cnt, send_blk, self_weight, neigh_weight, bias, cotangent
):
    dim, nodes = node_feats.shape
    tiles, width = tile_cnt.shape[:2]
    blocks = nodes // width
    table = send_blk[0].T
    ends = jnp.stack([tile_dst, tile_src])
    cap, kinds = table.shape
    slots = kinds * cap
    cols = X * Z_HI
    per_col = blocks // cols
    full = cols * dim
    chunk = 8
    shape = lambda *dims: jax.ShapeDtypeStruct(dims + (dim, width), BF16)
    halo = shape(GROUP, cap)
    step = Z_LO // 2

    hbm = pl.BlockSpec(memory_space=pltpu.HBM)
    send_a, send_b, feats = call(
        functools.partial(pack_kernel, width),
        (halo, halo, shape(blocks)),
        [hbm, hbm],
        [
            pltpu.VMEM((dim, nodes), BF16),
            pltpu.SMEM((cap, kinds), jnp.int32),
            pltpu.SemaphoreType.DMA((2,)),
        ],
        room=60,
    )(node_feats, table)
    got_b = swap(send_b, GROUP // 2)
    xc_plus, xc_minus = call(
        functools.partial(split_kernel, width), (shape(X, 2, per_col),) * 2, [VMEM] * 2
    )(feats, cotangent)
    whole = lambda shape: pl.BlockSpec(shape, lambda i: (0,) * len(shape))
    half, acc = pl.pallas_call(
        functools.partial(local_kernel, slots, chunk),
        grid=(tiles // chunk,),
        out_shape=(
            jax.ShapeDtypeStruct(tile_cnt.shape, BF16),
            jax.ShapeDtypeStruct((blocks, dim + 8, width), F32),
        ),
        in_specs=[
            whole((blocks, dim, width)),
            SMEM,
            pl.BlockSpec((chunk, width, width), lambda i: (i, 0, 0)),
        ],
        out_specs=(
            pl.BlockSpec((chunk, width, width), lambda i: (i, 0, 0)),
            whole((blocks, dim + 8, width)),
        ),
        compiler_params=pltpu.CompilerParams(vmem_limit_bytes=32 * 2**20),
        cost_estimate=pl.CostEstimate(
            flops=60000000, bytes_accessed=6000000, transcendentals=0
        ),
    )(feats, ends, tile_cnt)
    send_a, got_b, xc_plus, xc_minus, half, acc = lax.optimization_barrier(
        (send_a, got_b, xc_plus, xc_minus, half, acc)
    )
    xc_plus = along_z(xc_plus, step)
    xc_minus = along_z(xc_minus, -step)
    got_a = swap(send_a, 0)
    weight_t = jnp.concatenate([self_weight.T, neigh_weight.T], axis=1)
    bias_col = bias[:, None]
    agg_plus, agg_minus, degree = call(
        functools.partial(aggregate_kernel, slots),
        (shape(X, per_col), shape(X, per_col), jax.ShapeDtypeStruct((blocks, 8, width), F32)),
        [VMEM, VMEM, SMEM, VMEM, VMEM],
        [pltpu.VMEM((blocks, dim + 8, width), F32)],
    )(got_a, got_b, ends, half, acc)
    agg_plus = along_z(agg_plus, step)
    agg_minus = along_z(agg_minus, -step)
    ranged = call(join_kernel, shape(X, 3, 2, per_col), [VMEM] * 4)(
        xc_plus, xc_minus, agg_plus, agg_minus
    )
    ranged = over_x(ranged)
    plus, minus, dz, xa = call(
        node_kernel,
        (
            shape(X, 2, per_col),
            shape(X, 2, per_col),
            jax.ShapeDtypeStruct((full, per_col * width), BF16),
            jax.ShapeDtypeStruct((2 * full, per_col * width), BF16),
        ),
        [VMEM] * 5,
        [
            pltpu.VMEM((full, per_col * width), BF16),
            pltpu.VMEM((2, full, per_col * width), BF16),
        ],
    )(ranged, weight_t, neigh_weight, self_weight, bias_col)
    plus = along_z(plus, step)
    minus = along_z(minus, -step)
    part = call(
        functools.partial(weight_kernel, dim),
        jax.ShapeDtypeStruct((Y * CORE * X, Z_HI * full // 128 + 1, 8, 128), BF16),
        [VMEM] * 2,
    )(xa, dz)

    both = ("blk", "col")
    flat = [
        [rank(y, l, c, x, h) for y in range(Y) for c in range(CORE) for x in range(X)]
        for l in range(Z_LO)
        for h in range(Z_HI)
    ]
    line = [
        [rank(y, l, c, x, h) for h in range(Z_HI) for l in range(Z_LO)]
        for y in range(Y)
        for c in range(CORE)
        for x in range(X)
    ]
    part = lax.all_to_all(part, both, 0, 0, axis_index_groups=flat, tiled=False)
    home = call(turn_kernel, (shape(2, 2, per_col),) * X, [VMEM] * 2, cost=(1e10, 1e6))(plus, minus)
    part, *home = lax.optimization_barrier((part, *home))
    (part,) = call(
        fold_kernel, (jax.ShapeDtypeStruct((Z_HI * Z_LO, full // 128 + 1, 8, 128), BF16),), [VMEM]
    )(part)
    part = lax.all_to_all(part, both, 0, 0, axis_index_groups=line, tiled=False)
    route = lambda turn: [(c, (c + Z_HI * turn) % cols) for c in range(cols)]
    home = [home[0]] + [lax.ppermute(home[turn], "col", route(turn)) for turn in range(1, X)]
    away_a, away_b, scaled = call(
        functools.partial(contribution_kernel, slots),
        (halo, halo, shape(blocks)),
        [VMEM] * 5 + [SMEM, VMEM],
        [pltpu.VMEM((slots, dim, width), BF16)],
    )(*home, degree, ends, half)
    row = jax.ShapeDtypeStruct((1, 8, full), F32)
    rows, tail = call(
        total_kernel,
        (row, jax.ShapeDtypeStruct((8, 128), F32)),
        [VMEM],
    )(part)
    grad_bias = jnp.concatenate([tail[0], tail[4]])
    grad_bias = lax.dynamic_slice_in_dim(grad_bias, lax.axis_index("col") * dim, dim, 0)
    away_b, rows = lax.optimization_barrier((away_b, rows))
    back_b = swap(away_b, GROUP // 2)
    for bit in (1, Z_LO * CORE):
        double = jax.ShapeDtypeStruct((2 * rows.shape[0], 8, full), F32)
        rows = call(pair_kernel, double, [VMEM] * 2)(rows, across(rows, bit))
    acc = call(
        functools.partial(local_back_kernel, slots),
        jax.ShapeDtypeStruct((blocks, dim, width), F32),
        [VMEM] * 5 + [SMEM, VMEM],
    )(*home, scaled, ends, half)
    away_a, back_b, rows = lax.optimization_barrier((away_a, back_b, rows))
    back_a = swap(away_a, 0)
    grad = jax.ShapeDtypeStruct((dim, full), F32)
    grad_self, grad_neigh = call(order_kernel, (grad, grad), [VMEM] * 2)(
        rows, across(rows, 2 * Z_LO * CORE)
    )
    grad_feats = call(
        finish_kernel,
        jax.ShapeDtypeStruct((dim, nodes), BF16),
        [VMEM, VMEM, VMEM, SMEM],
        [pltpu.VMEM((blocks, dim, width), F32)],
    )(acc, back_a, back_b, table)
    return grad_feats, grad_self, grad_neigh, grad_bias


def solution(mesh):
    placed = (
        P("col", "blk"),
        P("blk"),
        P("blk"),
        P("blk", None, None),
        P("blk", None, None),
        P(),
        P(),
        P(),
        P("col", "blk"),
    )
    return jax.shard_map(
        per_device,
        mesh=mesh,
        in_specs=placed,
        out_specs=(P("col", "blk"), P("col", None), P("col", None), P("col")),
        check_vma=False,
    )
```
